128 devices in a mesh: seq: 32 (over y, z, core), head: 4 (over x).
Axes of the slice: x: 4, y: 4, z: 4, core: 2. Of those that a mesh axis runs over, the one named last changes fastest.
Arguments:
- x_in: bfloat16 [16384, 8192], P('seq', 'head'), may hold values from -6 to 6
- bc_in: bfloat16 [16384, 4, 256], P('seq', 'head'), may hold values from -6 to 6
- z_in: bfloat16 [16384, 8192], P('seq', 'head'), may hold values from -6 to 6
- dt_raw: bfloat16 [128, 16384], P('head', 'seq'), may hold values from -20 to 4
- a_log: float32 [128], P('head'), may hold values from -6 to 0.7
- conv_x: float32 [4, 8192], P(None, 'head'), may hold values from -3 to 3
- conv_bc: float32 [4, 4, 256], P(None, 'head'), may hold values from -3 to 3
- d_skip: float32 [128], P('head'), may hold values from 0.5 to 2
- norm_gain: float32 [8192], P('head'), may hold values from 0.25 to 1.75
- out_weight: bfloat16 [8192, 4096], P('head'), may hold values from -0.09375 to 0.09375
Outputs:
- out: bfloat16 [4096, 16384], P('head', 'seq')
The draws below stay inside these ranges and needn't reach their ends.
All inputs are finite; a program needn't handle non-finite values.
Results may differ from the reference program's by a relative error of at most 0.02.
Values may be sent and summed in bfloat16 or wider, within the bound.
No kernel may reach another device: no remote copies, remote signals or barrier semaphores. Data moves between devices by JAX's collectives and lax.ppermute only.
A program may use at most 192 MiB of HBM per device.

```python
import math
import jax
import jax.numpy as jnp
from jax import lax

HEAD_TOTAL = 128
HEAD_DIM = 64
STATE = 128
GROUPS = 4
D_OUT = 4096
CONV = 4
SPAN = 128
INNER = 8192
TOKEN_TOTAL = 16384
N_HEAD = 4


def decay_tables(key):
    base_key = jax.random.fold_in(key, 4242)
    random_keys = jax.random.split(base_key, 9)
    fast_heads = jax.random.randint(random_keys[0], (HEAD_TOTAL,), 0, 2) == 0
    fast_scale = jnp.exp(jax.random.uniform(random_keys[1], (HEAD_TOTAL,), jnp.float32, -0.7, 0.7))
    fast_rate = jnp.exp(jax.random.uniform(random_keys[2], (HEAD_TOTAL,), jnp.float32, math.log(1.0 / 50.0), math.log(1.0 / 30.0)))
    slow_total = jnp.exp(jax.random.uniform(random_keys[3], (HEAD_TOTAL,), jnp.float32, math.log(0.6), math.log(1.2)))
    slow_level = 2.5 / math.sqrt(STATE * TOKEN_TOTAL) * jnp.exp(jax.random.uniform(random_keys[8], (HEAD_TOTAL,), jnp.float32, -0.3, 0.3))
    slow_scale = slow_total / (TOKEN_TOTAL * slow_level * 1.151)
    decay_absolute = jnp.where(fast_heads, fast_scale, slow_scale)
    level_step = jnp.where(fast_heads, fast_rate / fast_scale, slow_level)
    rough_factor = jnp.exp(0.35 * jax.random.truncated_normal(random_keys[4], -2.5, 2.5, (HEAD_TOTAL, TOKEN_TOTAL), jnp.float32))
    block_len = max(TOKEN_TOTAL // 32, 1)
    block_count = TOKEN_TOTAL // block_len
    block_factor = jnp.exp(jax.random.uniform(random_keys[5], (HEAD_TOTAL, block_count), jnp.float32, -0.7, 0.7))
    block_factor = jnp.repeat(block_factor, block_len, axis=1)
    update_rounds = level_step[:, None] * rough_factor * block_factor
    segment_width = min(16, max(TOKEN_TOTAL // 8, 1))
    segment_offsets = jax.random.randint(random_keys[6], (HEAD_TOTAL, 2), 0, TOKEN_TOTAL - segment_width + 1)
    segment_error = -jnp.log(1.0 - jax.random.uniform(random_keys[7], (HEAD_TOTAL, 2), jnp.float32, 0.2, 0.3))
    segment_stride = segment_error / (decay_absolute[:, None] * segment_width)
    token_places = jnp.arange(TOKEN_TOTAL)[None, :]
    for segment_index in range(2):
        leading_token = segment_offsets[:, segment_index:segment_index + 1]
        within_segment = (token_places >= leading_token) & (token_places < leading_token + segment_width)
        update_rounds = jnp.where(within_segment, segment_stride[:, segment_index:segment_index + 1], update_rounds)
    return (decay_absolute, update_rounds)


def draw_dt_raw(key, part):
    decay_absolute, update_rounds = decay_tables(key)
    logits = update_rounds + jnp.log(-jnp.expm1(-update_rounds))
    return logits.astype(jnp.bfloat16)


def draw_a_log(key, part):
    decay_absolute, update_rounds = decay_tables(key)
    return jnp.log(decay_absolute).astype(jnp.float32)


def strengthened(array, stream_key, source, target, shards_of, factor):
    owner, partner = [(jnp.arange(array.shape[position]) // (array.shape[position] // shards_of)).reshape([-1 if axis == position else 1 for axis in range(array.ndim)]) for position in (source, target)]
    chosen = jax.random.permutation(stream_key, shards_of)[partner]
    strong = (owner == chosen) | (owner == (partner + shards_of // 2) % shards_of)
    return jnp.where(strong, factor * array, array)


def shard_levels(key, extent, cuts, smallest, top_value):
    level = 1.0
    for position, shards_of in cuts:
        heights = jax.random.uniform(jax.random.fold_in(jax.random.fold_in(key, 6), position), (shards_of,), jnp.float32, smallest / len(cuts), top_value / len(cuts))
        level = level * jnp.repeat(jnp.exp(heights), extent[position] // shards_of).reshape((-1,) + (1,) * (len(extent) - 1 - position))
    return level


def gaussian(rng, shape, width, bound, cuts=(), held_as=jnp.bfloat16):
    level = shard_levels(rng, shape, cuts, -0.22, 0.18) if cuts else 1.0
    values = jax.random.normal(rng, shape, jnp.float32) * width * level
    return jnp.minimum(jnp.maximum(values, -bound), bound).astype(held_as)


def noise_with(own_key, shape, deviation, reach, pieces, heavy, kind=jnp.bfloat16):
    values = deviation * jax.random.normal(own_key, shape, jnp.float32)
    if pieces:
        values = values * shard_levels(own_key, shape, pieces, -0.22, 0.18)
    return jnp.clip(strengthened(values, jax.random.fold_in(own_key, 3), *heavy), -reach, reach).astype(kind)


def setup_inputs(seed: int = 0) -> dict:
    key_list = jax.random.split(jax.random.key(seed), 11)
    x_in = gaussian(key_list[0], (TOKEN_TOTAL, INNER), 1.0, 6.0, ((0, 32), (1, 4)))
    bc_in = gaussian(key_list[1], (TOKEN_TOTAL, GROUPS, 2 * STATE), 1.0, 6.0, ((0, 32), (1, 4)))
    z_in = gaussian(key_list[2], (TOKEN_TOTAL, INNER), 1.0, 6.0, ((0, 32), (1, 4)))
    dt_raw = draw_dt_raw(jax.random.fold_in(key_list[10], 71), 0)
    a_log = draw_a_log(jax.random.fold_in(key_list[10], 71), 0)
    conv_x = gaussian(key_list[5], (CONV, INNER), CONV ** -0.5, 3.0, ((1, 4),), jnp.float32)
    conv_bc = gaussian(key_list[6], (CONV, GROUPS, 2 * STATE), CONV ** -0.5, 3.0, ((1, 4),), jnp.float32)
    d_skip = jnp.clip(0.5 + 1.5 * jax.random.uniform(key_list[7], (HEAD_TOTAL,), jnp.float32) ** shard_levels(key_list[7], (HEAD_TOTAL,), ((0, 4),), -0.2, 0.2), 0.5, 2.0)
    norm_gain = jnp.clip(1.0 + 0.15 * jax.random.normal(key_list[8], (INNER,), jnp.float32), 0.25, 1.75)
    out_weight = noise_with(key_list[9], (INNER, D_OUT), INNER ** -0.5, 0.09375, ((0, 4),), (0, 1, 4, 2.0))
    return {"x_in": x_in, "bc_in": bc_in, "z_in": z_in, "dt_raw": dt_raw, "a_log": a_log, "conv_x": conv_x, "conv_bc": conv_bc, "d_skip": d_skip, "norm_gain": norm_gain, "out_weight": out_weight}


def conv_silu(extended, weight, rows):
    running = weight[0] * extended[0:rows].astype(jnp.float32)
    for offset in range(1, weight.shape[0]):
        running = running + weight[offset] * extended[offset:offset + rows].astype(jnp.float32)
    return (running * jax.nn.sigmoid(running)).astype(jnp.bfloat16)

def reference(x_in, bc_in, z_in, dt_raw, a_log, conv_x, conv_bc, d_skip, norm_gain, out_weight):
    heads_group = HEAD_TOTAL // GROUPS
    blocks = TOKEN_TOTAL // SPAN
    x_conv = conv_silu(jnp.concatenate([jnp.zeros((CONV - 1, INNER), jnp.bfloat16), x_in], 0), conv_x, TOKEN_TOTAL)
    bc_conv = conv_silu(jnp.concatenate([jnp.zeros((CONV - 1, GROUPS, 2 * STATE), jnp.bfloat16), bc_in], 0), conv_bc, TOKEN_TOTAL)
    b_blocks = bc_conv[:, :, :STATE].reshape(blocks, SPAN, GROUPS, STATE)
    c_blocks = bc_conv[:, :, STATE:].reshape(blocks, SPAN, GROUPS, STATE)
    x_blocks = x_conv.reshape(blocks, SPAN, GROUPS, heads_group, HEAD_DIM)
    z_blocks = z_in.reshape(blocks, SPAN, INNER)
    step_size = jax.nn.softplus(dt_raw.astype(jnp.float32))
    rate = -jnp.exp(a_log)[:, None] * step_size
    step_blocks = jnp.transpose(step_size.reshape(GROUPS, heads_group, blocks, SPAN), (2, 0, 1, 3))
    rate_blocks = jnp.transpose(rate.reshape(GROUPS, heads_group, blocks, SPAN), (2, 0, 1, 3))
    weight_full = out_weight.astype(jnp.float32).reshape(N_HEAD, INNER // N_HEAD, D_OUT)
    row_ids = lax.broadcasted_iota(jnp.int32, (SPAN, SPAN), 0)
    col_ids = lax.broadcasted_iota(jnp.int32, (SPAN, SPAN), 1)
    causal = row_ids >= col_ids
    skip_table = d_skip.reshape(GROUPS, heads_group, 1)

    def one_block(state, inputs):
        x_blk, b_blk, c_blk, step_blk, rate_blk, z_blk = inputs
        log_decay = jnp.cumsum(rate_blk, axis=2)
        scores = jnp.einsum('tgn,sgn->gts', c_blk.astype(jnp.float32), b_blk.astype(jnp.float32))
        decay_gap = log_decay[..., :, None] - log_decay[..., None, :]
        mask_decay = jnp.where(causal, jnp.exp(jnp.where(causal, decay_gap, 0.0)), 0.0)
        mixing = (scores[:, None] * mask_decay * step_blk[..., None, :]).astype(jnp.bfloat16)
        y_intra = jnp.einsum('ghts,sghp->tghp', mixing.astype(jnp.float32), x_blk.astype(jnp.float32))
        tail_weight = jnp.exp(log_decay[..., -1:] - log_decay) * step_blk
        weighted_b = (tail_weight[..., None] * jnp.transpose(b_blk, (1, 0, 2))[:, None].astype(jnp.float32)).astype(jnp.bfloat16)
        block_state = jnp.einsum('sghp,ghsn->ghpn', x_blk.astype(jnp.float32), weighted_b.astype(jnp.float32))
        readout = jnp.einsum('tgn,ghpn->ghtp', c_blk.astype(jnp.float32), state, precision=lax.Precision.HIGHEST)
        y_state = jnp.exp(log_decay)[..., None] * readout
        summed = y_intra + jnp.transpose(y_state, (2, 0, 1, 3)) + skip_table * x_blk.astype(jnp.float32)
        gated_rows = summed.reshape(SPAN, INNER) * jax.nn.silu(z_blk.astype(jnp.float32))
        grouped = gated_rows.reshape(SPAN, GROUPS, INNER // GROUPS)
        inverse_rms = lax.rsqrt(lax.optimization_barrier(jnp.mean(grouped * grouped, axis=2, keepdims=True)) + 1e-05)
        normed = ((grouped * inverse_rms).reshape(SPAN, INNER) * norm_gain).astype(jnp.bfloat16)
        partial_terms = jnp.einsum('tkc,kcd->ktd', normed.astype(jnp.float32).reshape(SPAN, N_HEAD, INNER // N_HEAD), weight_full)
        rounded = lax.optimization_barrier(partial_terms.astype(jnp.bfloat16))
        result = lax.optimization_barrier(jnp.sum(rounded.astype(jnp.float32), axis=0)).astype(jnp.bfloat16)
        new_state = jnp.exp(log_decay[..., -1])[..., None, None] * state + block_state
        return (new_state, result)
    start_state = jnp.zeros((GROUPS, heads_group, HEAD_DIM, STATE), jnp.float32)
    final_state, outputs = lax.scan(one_block, start_state, (x_blocks, b_blocks, c_blocks, step_blocks, rate_blocks, z_blocks))
    return outputs.reshape(TOKEN_TOTAL, D_OUT).T
```

```python
import functools

import jax
import jax.numpy as jnp
from jax import lax
from jax.experimental import pallas as pl
from jax.experimental.pallas import tpu as pltpu
from jax.sharding import PartitionSpec as P

SPAN = 128
HEADS = 32
HD = 64
STATE = 128
TOK = 512
NB = 4
INNER = 2048
CHUNK = 256
NCH = INNER // CHUNK
HPC = CHUNK // HD
DOUT = 4096
QOUT = 1024
WROWS = 144
LOG2E = 1.4426950408889634
BF = jnp.bfloat16
F32 = jnp.float32
VMEM_LIMIT = 48 << 20


def silu(u):
    half = 0.5 * u
    return half + half * jnp.tanh(half)


def dot(a, b):
    return jnp.dot(a, b, preferred_element_type=F32)


def iota(shape, axis):
    return lax.broadcasted_iota(jnp.int32, shape, axis)


def onehot(first_head, width, lanes):
    k = iota((128, width), 0) & 31
    h = first_head + (iota((128, width), 1) // lanes)
    return jnp.where(k == h, 1.0, 0.0).astype(BF)


def split2(v):
    hi = v.astype(BF).astype(F32)
    return hi, (v - hi).astype(BF).astype(F32)


def column(row, n):
    eye = iota((n, n), 0) == iota((n, n), 1)
    return jnp.sum(jnp.where(eye, jnp.broadcast_to(row, (n, n)), 0.0), axis=1, keepdims=True)


def conv_rows(buf, taps, start, rows):
    u = taps[0:1] * buf[pl.ds(start + 5, rows), :]
    for k in range(1, 4):
        u = u + taps[k : k + 1] * buf[pl.ds(start + 5 + k, rows), :]
    return silu(u)


def first_body(x_ref, bc_ref, cwx_ref, cwb_ref, step_ref, lstep_ref, alog_ref, dskip_ref,
               xc_o, bc_o, st_o, dec_o, m2_o, tl_o, te_o, tw_o, buf, bt, dtab):
    i = pl.program_id(0)

    @pl.when(i == 0)
    def _():
        a = column(alog_ref[...], HEADS)
        step = step_ref[...]
        L = (-LOG2E * jnp.exp(a)) * step
        lane = iota((HEADS, TOK), 1) & (SPAN - 1)
        for k in (1, 2, 4, 8, 16, 32, 64):
            L = L + jnp.where(lane >= k, pltpu.roll(L, k, 1), 0.0)
        M = lstep_ref[...] - L
        end = jnp.concatenate(
            [jnp.broadcast_to(L[:, c * SPAN + SPAN - 1 : (c + 1) * SPAN], (HEADS, SPAN)) for c in range(NB)], axis=1
        )
        w_hi, w_lo = split2(jnp.exp2(end + M))
        e_hi, e_lo = split2(jnp.exp2(L))
        l_hi, rest = L.astype(BF).astype(F32), None
        rest = L - l_hi
        l_mid = rest.astype(BF).astype(F32)
        l_lo = rest - l_mid
        zero = jnp.zeros((HEADS, TOK), F32)
        tw_o[...] = jnp.transpose(jnp.concatenate([w_hi, w_lo, zero, zero], axis=0)).astype(BF)
        te = jnp.transpose(jnp.concatenate([e_hi, e_lo, zero, zero], axis=0))
        te_o[...] = te.astype(BF)
        tl_o[...] = jnp.transpose(jnp.concatenate([l_hi, l_mid, l_lo, zero], axis=0)).astype(BF)
        for j in range(NCH):
            m2_o[j, 0:HPC, :] = M[j * HPC : (j + 1) * HPC, :]
        d_hi, d_lo = split2(column(dskip_ref[...], HEADS))
        zcol = jnp.zeros((2 * HEADS, SPAN), F32)
        td = jnp.transpose(
            jnp.concatenate(
                [jnp.broadcast_to(d_hi, (HEADS, SPAN)), jnp.broadcast_to(d_lo, (HEADS, SPAN)), zcol], axis=0
            )
        )
        rows = [te[(c + 1) * SPAN - 1 : (c + 1) * SPAN, :] for c in range(NB)]
        dtab[...] = jnp.concatenate(rows + [td[0:1, :], jnp.zeros((11, SPAN), F32)], axis=0).astype(BF)
        buf[pl.ds(120, 400), :] = bc_ref[pl.ds(112, 400), :].astype(F32)
        for c in range(1, NB):
            v = conv_rows(buf, cwb_ref[...], c * SPAN, SPAN)
            bc_o[pl.ds((c - 1) * SPAN, SPAN), :] = v.astype(BF)
            bt[c - 1] = jnp.transpose(v[:, :STATE]).astype(BF)

    sel = onehot(i * HPC, CHUNK, HD)
    dec_o[...] = dot(dtab[...], sel)
    buf[pl.ds(120, 400), :] = x_ref[pl.ds(112, 400), :].astype(F32)
    taps = cwx_ref[...]
    for c in range(1, NB):
        v = conv_rows(buf, taps, c * SPAN, SPAN).astype(BF)
        xc_o[pl.ds((c - 1) * SPAN, SPAN), :] = v
        w = dot(tw_o[pl.ds(c * SPAN, SPAN), :], sel)
        st_o[c - 1] = dot(bt[c - 1], (v.astype(F32) * w).astype(BF))


def first_call(x, bc, cwx, cwb, step, lstep, alog, dskip):
    full = lambda *s: pl.BlockSpec(s, lambda i: (0,) * len(s))
    return pl.pallas_call(
        first_body,
        grid=(NCH,),
        in_specs=[
            pl.BlockSpec((TOK, CHUNK), lambda i: (0, i)),
            full(TOK, 256),
            pl.BlockSpec((4, CHUNK), lambda i: (0, i)),
            full(4, 256),
            full(HEADS, TOK),
            full(HEADS, TOK),
            full(1, HEADS),
            full(1, HEADS),
        ],
        out_specs=[
            pl.BlockSpec((TOK - SPAN, CHUNK), lambda i: (0, i)),
            full(TOK - SPAN, 256),
            pl.BlockSpec((NB - 1, STATE, CHUNK), lambda i: (0, 0, i)),
            pl.BlockSpec((16, CHUNK), lambda i: (0, i)),
            full(NCH, 8, TOK),
            full(TOK, 128),
            full(TOK, 128),
            full(TOK, 128),
        ],
        out_shape=[
            jax.ShapeDtypeStruct((TOK - SPAN, INNER), BF),
            jax.ShapeDtypeStruct((TOK - SPAN, 256), BF),
            jax.ShapeDtypeStruct((NB - 1, STATE, INNER), F32),
            jax.ShapeDtypeStruct((16, INNER), F32),
            jax.ShapeDtypeStruct((NCH, 8, TOK), F32),
            jax.ShapeDtypeStruct((TOK, 128), BF),
            jax.ShapeDtypeStruct((TOK, 128), BF),
            jax.ShapeDtypeStruct((TOK, 128), BF),
        ],
        scratch_shapes=[
            pltpu.VMEM((520, CHUNK), F32),
            pltpu.VMEM((NB - 1, STATE, SPAN), BF),
            pltpu.VMEM((16, 128), BF),
        ],
        compiler_params=pltpu.CompilerParams(vmem_limit_bytes=VMEM_LIMIT),
        cost_estimate=pl.CostEstimate(flops=10**9, bytes_accessed=8 << 20, transcendentals=10**6),
        name="first",
    )(x, bc, cwx, cwb, step, lstep, alog, dskip)


def chunk_of(i, scal):
    return (i + 4 * (1 - scal[0])) % NCH


def wire_rows(decay):
    hi, lo = split2(decay)
    return jnp.concatenate([hi, lo, jnp.zeros((14, decay.shape[1]), F32)], axis=0)


def second_body(scal, x_ref, hx_ref, bc_ref, hbc_ref, cwx_ref, cwb_ref, tw_ref, st_ref, dec_ref,
                xc_o, bc_o, pst_o, send_o, keep_o, buf, bt):
    i = pl.program_id(0)

    @pl.when(i == 0)
    def _():
        buf[pl.ds(0, 8), :] = hbc_ref[...].astype(F32)
        buf[pl.ds(8, SPAN), :] = bc_ref[...].astype(F32)
        v = conv_rows(buf, cwb_ref[...], 0, SPAN)
        bc_o[...] = v.astype(BF)
        bt[...] = jnp.transpose(v[:, :STATE]).astype(BF)

    sel = onehot(chunk_of(i, scal) * HPC, CHUNK, HD)
    buf[pl.ds(0, 8), :] = hx_ref[...].astype(F32)
    buf[pl.ds(8, SPAN), :] = x_ref[...].astype(F32)
    v = conv_rows(buf, cwx_ref[...], 0, SPAN).astype(BF)
    xc_o[...] = v
    w = dot(tw_ref[...], sel)
    state = dot(bt[...], (v.astype(F32) * w).astype(BF))
    dec = dec_ref[...]
    decay = dec[0:1]
    for c in range(1, NB):
        pst_o[c - 1] = state
        state = dec[c : c + 1] * state + st_ref[c - 1]
        decay = decay * dec[c : c + 1]

    @pl.when(i < 4)
    def _():
        send_o[0, 0:STATE, :] = state.astype(BF)
        send_o[0, STATE:WROWS, :] = wire_rows(decay).astype(BF)

    @pl.when(i >= 4)
    def _():
        keep_o[0, 0:STATE, :] = state
        keep_o[0, STATE:WROWS, :] = jnp.concatenate([decay, jnp.zeros((15, CHUNK), F32)], axis=0)


def second_call(scal, x, halo, bc, cwx, cwb, tw, st, dec):
    full = lambda *s: pl.BlockSpec(s, lambda i, sc: (0,) * len(s))
    lanes = lambda rows: pl.BlockSpec((rows, CHUNK), lambda i, sc: (0, chunk_of(i, sc)))
    deep = pl.BlockSpec((NB - 1, STATE, CHUNK), lambda i, sc: (0, 0, chunk_of(i, sc)))
    return pl.pallas_call(
        second_body,
        grid_spec=pltpu.PrefetchScalarGridSpec(
            num_scalar_prefetch=1,
            grid=(NCH,),
            in_specs=[
                lanes(SPAN),
                lanes(8),
                full(SPAN, 256),
                pl.BlockSpec((8, 256), lambda i, sc: (0, NCH)),
                lanes(4),
                full(4, 256),
                full(SPAN, 128),
                deep,
                lanes(16),
            ],
            out_specs=[
                lanes(SPAN),
                full(SPAN, 256),
                deep,
                pl.BlockSpec((1, WROWS, CHUNK), lambda i, sc: (jnp.minimum(i, 3), 0, 0)),
                pl.BlockSpec((1, WROWS, CHUNK), lambda i, sc: (jnp.maximum(i - 4, 0), 0, 0)),
            ],
            scratch_shapes=[pltpu.VMEM((136, CHUNK), F32), pltpu.VMEM((STATE, SPAN), BF)],
        ),
        out_shape=[
            jax.ShapeDtypeStruct((SPAN, INNER), BF),
            jax.ShapeDtypeStruct((SPAN, 256), BF),
            jax.ShapeDtypeStruct((NB - 1, STATE, INNER), F32),
            jax.ShapeDtypeStruct((4, WROWS, CHUNK), BF),
            jax.ShapeDtypeStruct((4, WROWS, CHUNK), F32),
        ],
        compiler_params=pltpu.CompilerParams(vmem_limit_bytes=VMEM_LIMIT),
        cost_estimate=pl.CostEstimate(flops=3 * 10**8, bytes_accessed=6 << 20, transcendentals=3 * 10**5),
        name="second",
    )(scal, x, halo, bc, halo, cwx, cwb, tw, st, dec)


def decay_of(v):
    return v[STATE : STATE + 1] + v[STATE + 1 : STATE + 2]


def small_call(body, name, scal, args, outs, scratch=()):
    return pl.pallas_call(
        body,
        grid_spec=pltpu.PrefetchScalarGridSpec(
            num_scalar_prefetch=1,
            grid=(1,),
            in_specs=[pl.BlockSpec(a.shape, lambda i, sc, n=a.ndim: (0,) * n) for a in args],
            out_specs=[pl.BlockSpec(o.shape, lambda i, sc, n=len(o.shape): (0,) * n) for o in outs],
            scratch_shapes=list(scratch),
        ),
        out_shape=list(outs),
        compiler_params=pltpu.CompilerParams(vmem_limit_bytes=VMEM_LIMIT),
        cost_estimate=pl.CostEstimate(flops=10**6, bytes_accessed=1 << 20, transcendentals=0),
        name=name,
    )(scal, *args)


def pair_body(scal, keep_ref, recv_ref, *outs):
    core, z = scal[0], scal[1]
    for i in range(4):
        q = lax.rem(z + i, 4)
        own = keep_ref[q]
        other = recv_ref[q].astype(F32)
        early = jnp.where(core == 0, own, other)
        late = jnp.where(core == 0, other, own)
        d_early, d_late = decay_of(early), decay_of(late)
        outs[i][0:STATE, :] = (d_late * early[0:STATE] + late[0:STATE]).astype(BF)
        outs[i][STATE:WROWS, :] = wire_rows(d_early * d_late).astype(BF)


def row_body(scal, r0, r1, r2, r3, total_o, pre_o, dpre_o, box):
    z = scal[1]
    for i, r in enumerate((r0, r1, r2, r3)):
        box[lax.rem(z - i + 4, 4)] = r[...].astype(F32)
    state = jnp.zeros((STATE, CHUNK), F32)
    decay = jnp.ones((1, CHUNK), F32)
    for k in range(4):
        pre_o[k] = state
        dpre_o[k] = jnp.broadcast_to(decay, (8, CHUNK))
        v = box[k]
        d = decay_of(v)
        state = d * state + v[0:STATE]
        decay = decay * d
    total_o[0:STATE, :] = state.astype(BF)
    total_o[STATE:WROWS, :] = wire_rows(decay).astype(BF)


def plane_body(scal, r0, r1, r2, r3, pre_ref, dpre_ref, o0, o1, o2, o3, box):
    z, y = scal[1], scal[2]
    for i, r in enumerate((r0, r1, r2, r3)):
        box[lax.rem(y - i + 4, 4)] = r[...].astype(F32)
    state = jnp.zeros((STATE, CHUNK), F32)
    for k in range(3):
        v = box[k]
        state = jnp.where(k < y, decay_of(v) * state + v[0:STATE], state)
    for i, o in enumerate((o0, o1, o2, o3)):
        q = lax.rem(z + i, 4)
        d = dpre_ref[q]
        o[...] = (pre_ref[q] + d[0:1] * state).astype(BF)


def spread_body(scal, r0, r1, r2, r3, keep_ref, recv_ref, send_o, stay_o, box):
    core, z = scal[0], scal[1]
    for i, r in enumerate((r0, r1, r2, r3)):
        box[lax.rem(z - i + 4, 4)] = r[...].astype(F32)
    for q in range(4):
        early = jnp.where(core == 0, keep_ref[q], recv_ref[q].astype(F32))
        a = box[q]
        b = decay_of(early) * a + early[0:STATE]
        send_o[q] = jnp.where(core == 0, b, a).astype(BF)
        stay_o[q] = jnp.where(core == 0, a, b).astype(BF)


def mix_body(xc0_ref, xc1_ref, bc0_ref, bc1_ref, z_ref, m2_ref, tl_ref, te_ref, dec_ref, yg_o, g2_o, sc):
    i = pl.program_id(0)
    xs = lambda c: xc0_ref[...] if c == 0 else xc1_ref[pl.ds((c - 1) * SPAN, SPAN), :]

    @pl.when(i == 0)
    def _():
        causal = iota((SPAN, SPAN), 0) >= iota((SPAN, SPAN), 1)
        for c in range(NB):
            v = bc0_ref[...] if c == 0 else bc1_ref[pl.ds((c - 1) * SPAN, SPAN), :]
            s = lax.dot_general(
                v[:, STATE:], v[:, :STATE], (((1,), (1,)), ((), ())), preferred_element_type=F32
            )
            sc[c] = jnp.where(causal, s, 0.0)

    sel = onehot(i * HPC, CHUNK, HD)
    wide = onehot(i * HPC, HPC * SPAN, SPAN)
    left = iota((SPAN, SPAN), 1) < HD
    skip = dec_ref[4:5, :]
    m2 = m2_ref[0]
    for c in range(NB):
        rows = pl.ds(c * SPAN, SPAN)
        x = xs(c)
        ex = dot(tl_ref[rows, :], wide)
        s = sc[c]
        parts = []
        for h in range(HPC):
            e = ex[:, h * SPAN : (h + 1) * SPAN] + m2[h : h + 1, c * SPAN : (c + 1) * SPAN]
            parts.append((s * jnp.exp2(jnp.minimum(e, 8.0))).astype(BF))
        ys = []
        for p in range(HPC // 2):
            xp = x[:, p * SPAN : (p + 1) * SPAN].astype(F32)
            rhs = jnp.concatenate([jnp.where(left, xp, 0.0), jnp.where(left, 0.0, xp)], axis=0).astype(BF)
            ys.append(dot(jnp.concatenate([parts[2 * p], parts[2 * p + 1]], axis=1), rhs))
        y = jnp.concatenate(ys, axis=1) + skip * x.astype(F32)
        gate = silu(z_ref[rows, :].astype(F32))
        yg_o[rows, :] = (y * gate).astype(BF)
        g2_o[rows, :] = (dot(te_ref[rows, :], sel) * gate).astype(BF)


def mix_call(xc0, xc1, bc0, bc1, z, m2, tl, te, dec):
    full = lambda *s: pl.BlockSpec(s, lambda i: (0,) * len(s))
    lanes = lambda rows: pl.BlockSpec((rows, CHUNK), lambda i: (0, i))
    return pl.pallas_call(
        mix_body,
        grid=(NCH,),
        in_specs=[
            lanes(SPAN),
            lanes(TOK - SPAN),
            full(SPAN, 256),
            full(TOK - SPAN, 256),
            lanes(TOK),
            pl.BlockSpec((1, 8, TOK), lambda i: (i, 0, 0)),
            full(TOK, 128),
            full(TOK, 128),
            lanes(16),
        ],
        out_specs=[lanes(TOK), lanes(TOK)],
        out_shape=[jax.ShapeDtypeStruct((TOK, INNER), BF)] * 2,
        scratch_shapes=[pltpu.VMEM((NB, SPAN, SPAN), F32)],
        compiler_params=pltpu.CompilerParams(vmem_limit_bytes=VMEM_LIMIT),
        cost_estimate=pl.CostEstimate(flops=2 * 10**9, bytes_accessed=10 << 20, transcendentals=4 * 10**6),
        name="mix",
    )(xc0, xc1, bc0, bc1, z, m2, tl, te, dec)


def gate_body(scal, yg_ref, g2_ref, bc0_ref, bc1_ref, pst_ref, dec_ref, stay_ref, recv_ref, gain_ref, n_o, inv_o, ss):
    i = pl.program_id(0)
    half = i // 4
    q = lax.rem(i, 4)
    own = (half == scal[0]).astype(F32)
    carried = own * stay_ref[q].astype(F32) + (1.0 - own) * recv_ref[q].astype(F32)
    gain = gain_ref[...]

    @pl.when(i == 0)
    def _():
        ss[...] = jnp.zeros_like(ss)

    dec = dec_ref[...]
    for c in range(NB):
        rows = pl.ds(c * SPAN, SPAN)
        cm = bc0_ref[...] if c == 0 else bc1_ref[pl.ds((c - 1) * SPAN, SPAN), :]
        ent = carried if c == 0 else pst_ref[c - 1] + carried
        g = yg_ref[rows, :].astype(F32) + dot(cm[:, STATE:], ent.astype(BF)) * g2_ref[rows, :].astype(F32)
        sq = g * g
        ss[rows, :] = ss[rows, :] + sq[:, :128] + sq[:, 128:]
        n_o[rows, :] = (g * gain).astype(BF)
        if c < NB - 1:
            carried = dec[c : c + 1] * carried

    @pl.when(i == NCH - 1)
    def _():
        m = jnp.sum(ss[...], axis=1, keepdims=True) * (1.0 / INNER)
        inv_o[...] = jnp.broadcast_to(lax.rsqrt(m + 1e-05), (TOK, 128))


def gate_call(scal, yg, g2, bc0, bc1, pst, dec, stay, recv, gain):
    full = lambda *s: pl.BlockSpec(s, lambda i, sc: (0,) * len(s))
    lanes = lambda rows: pl.BlockSpec((rows, CHUNK), lambda i, sc: (0, i))
    return pl.pallas_call(
        gate_body,
        grid_spec=pltpu.PrefetchScalarGridSpec(
            num_scalar_prefetch=1,
            grid=(NCH,),
            in_specs=[
                lanes(TOK),
                lanes(TOK),
                full(SPAN, 256),
                full(TOK - SPAN, 256),
                pl.BlockSpec((NB - 1, STATE, CHUNK), lambda i, sc: (0, 0, i)),
                lanes(16),
                full(4, STATE, CHUNK),
                full(4, STATE, CHUNK),
                lanes(1),
            ],
            out_specs=[lanes(TOK), full(TOK, 128)],
            scratch_shapes=[pltpu.VMEM((TOK, 128), F32)],
        ),
        out_shape=[jax.ShapeDtypeStruct((TOK, INNER), BF), jax.ShapeDtypeStruct((TOK, 128), F32)],
        compiler_params=pltpu.CompilerParams(vmem_limit_bytes=VMEM_LIMIT),
        cost_estimate=pl.CostEstimate(flops=5 * 10**8, bytes_accessed=8 << 20, transcendentals=0),
        name="gate",
    )(scal, yg, g2, bc0, bc1, pst, dec, stay, recv, gain)


def proj_body(scal, n_ref, inv_ref, w_ref, a_o, b_o):
    w = w_ref[...]
    for rows, o in ((pl.ds(0, 256), a_o), (pl.ds(256, 256), b_o)):
        inv = inv_ref[rows, 0:1]
        o[...] = (dot(n_ref[rows, :], w) * inv).astype(BF)


def proj_call(scal, n, inv, w, shift):
    step = QOUT // 256
    full = lambda *s: pl.BlockSpec(s, lambda i, sc: (0,) * len(s))
    return pl.pallas_call(
        proj_body,
        grid_spec=pltpu.PrefetchScalarGridSpec(
            num_scalar_prefetch=1,
            grid=(step,),
            in_specs=[
                full(TOK, INNER),
                full(TOK, 128),
                pl.BlockSpec((INNER, 256), lambda i, sc: (0, lax.rem(sc[3] + shift, 4) * step + i)),
            ],
            out_specs=[pl.BlockSpec((256, 256), lambda i, sc: (0, i))] * 2,
        ),
        out_shape=[jax.ShapeDtypeStruct((256, QOUT), BF)] * 2,
        compiler_params=pltpu.CompilerParams(vmem_limit_bytes=VMEM_LIMIT),
        cost_estimate=pl.CostEstimate(flops=2 * TOK * INNER * QOUT, bytes_accessed=7 << 20, transcendentals=0),
        name="proj",
    )(scal, n, inv, w)


def last_body(a0, a1, a2, b0, b1, b2, o):
    for k, refs in enumerate(((a0, a1, a2), (b0, b1, b2))):
        s = refs[0][...].astype(F32) + refs[1][...].astype(F32) + refs[2][...].astype(F32)
        o[:, k * 256 : (k + 1) * 256] = jnp.transpose(s).astype(BF)


def last_call(*parts):
    return pl.pallas_call(
        last_body,
        grid=(QOUT // 256,),
        in_specs=[pl.BlockSpec((256, 256), lambda i: (0, i))] * 6,
        out_specs=pl.BlockSpec((256, TOK), lambda i: (i, 0)),
        out_shape=jax.ShapeDtypeStruct((QOUT, TOK), BF),
        compiler_params=pltpu.CompilerParams(vmem_limit_bytes=VMEM_LIMIT),
        name="last",
    )(*parts)


def seq_perm(v, dy, dz, flip):
    pairs = []
    for src in range(32):
        y, z, c = src // 8, (src // 2) % 4, src % 2
        dst = (((y + dy) % 4) * 4 + (z + dz) % 4) * 2 + (1 - c if flip else c)
        pairs.append((src, dst))
    return lax.ppermute(v, "seq", pairs)


def head_perm(v, shift):
    return lax.ppermute(v, "head", [(s, (s + shift) % 4) for s in range(4)])


def on_device(x_in, bc_in, z_in, dt_raw, a_log, conv_x, conv_bc, d_skip, norm_gain, out_weight):
    bc = bc_in.reshape(TOK, 256)
    cwb = conv_bc.reshape(4, 256)
    halo = lax.ppermute(
        jnp.concatenate([x_in[TOK - 8 :], bc[TOK - 8 :]], axis=1), "seq", [(s, s + 1) for s in range(31)]
    )
    place = lax.axis_index("seq")
    scal = jnp.stack([place % 2, (place // 2) % 4, place // 8, lax.axis_index("head")]).astype(jnp.int32)
    step = jax.nn.softplus(dt_raw.astype(F32))
    lstep = jnp.log2(step)
    xc1, bc1, st, dec, m2, tl, te, tw = first_call(
        x_in, bc, conv_x, cwb, step, lstep, a_log.reshape(1, HEADS), d_skip.reshape(1, HEADS)
    )
    xc0, bc0, pst, send, keep = second_call(scal, x_in, halo, bc, conv_x, cwb, tw, st, dec)
    recv = seq_perm(send, 0, 0, True)
    piece = jax.ShapeDtypeStruct((WROWS, CHUNK), BF)
    plain = jax.ShapeDtypeStruct((STATE, CHUNK), BF)
    box = pltpu.VMEM((4, WROWS, CHUNK), F32)
    q = small_call(pair_body, "pair", scal, (keep, recv), [piece] * 4)
    rows = [q[0]] + [seq_perm(q[i], 0, i, False) for i in (1, 2, 3)]
    total, pre, dpre = small_call(
        row_body,
        "row",
        scal,
        rows,
        [piece, jax.ShapeDtypeStruct((4, STATE, CHUNK), F32), jax.ShapeDtypeStruct((4, 8, CHUNK), F32)],
        [box],
    )
    cols = [total] + [seq_perm(total, i, 0, False) for i in (1, 2, 3)]
    e = small_call(plane_body, "plane", scal, (*cols, pre, dpre), [plain] * 4, [box])
    back = [e[0]] + [seq_perm(e[i], 0, i, False) for i in (1, 2, 3)]
    half = jax.ShapeDtypeStruct((4, STATE, CHUNK), BF)
    give, stay = small_call(
        spread_body, "spread", scal, (*back, keep, recv), [half] * 2, [pltpu.VMEM((4, STATE, CHUNK), F32)]
    )
    take = seq_perm(give, 0, 0, True)
    yg, g2 = mix_call(xc0, xc1, bc0, bc1, z_in, m2, tl, te, dec)
    n, inv = gate_call(scal, yg, g2, bc0, bc1, pst, dec, stay, take, norm_gain.reshape(1, INNER))
    far_a, far_b = proj_call(scal, n, inv, out_weight, 2)
    from_left = head_perm(far_a, 1)
    from_right = head_perm(far_b, -1)
    right_a, right_b = proj_call(scal, n, inv, out_weight, 1)
    left_a, left_b = proj_call(scal, n, inv, out_weight, 3)
    near_b = head_perm(right_b, 1)
    near_a = head_perm(left_a, -1)
    add = lambda u, v: (u.astype(F32) + v.astype(F32)).astype(BF)
    sum_a = head_perm(add(right_a, from_left), 1)
    sum_b = head_perm(add(left_b, from_right), -1)
    own_a, own_b = proj_call(scal, n, inv, out_weight, 0)
    return last_call(own_a, near_a, sum_a, own_b, near_b, sum_b)


def solution(mesh):
    placed = (
        P("seq", "head"),
        P("seq", "head", None),
        P("seq", "head"),
        P("head", "seq"),
        P("head"),
        P(None, "head"),
        P(None, "head", None),
        P("head"),
        P("head"),
        P("head", None),
    )
    return jax.shard_map(
        on_device, mesh=mesh, in_specs=placed, out_specs=P("head", "seq"), check_vma=False
    )
```

```python
import functools

import jax
import jax.numpy as jnp
from jax import lax
from jax.experimental import pallas as pl
from jax.experimental.pallas import tpu as pltpu
from jax.sharding import PartitionSpec as P

SPAN = 128
HEADS = 32
HD = 64
STATE = 128
TOK = 512
NB = 4
INNER = 2048
CHUNK = 256
NCH = INNER // CHUNK
HPC = CHUNK // HD
DOUT = 4096
QOUT = 1024
WROWS = 144
LOG2E = 1.4426950408889634
BF = jnp.bfloat16
F32 = jnp.float32
VMEM_LIMIT = 48 << 20


def silu(u):
    half = 0.5 * u
    return half + half * jnp.tanh(half)


def dot(a, b):
    return jnp.dot(a, b, preferred_element_type=F32)


def iota(shape, axis):
    return lax.broadcasted_iota(jnp.int32, shape, axis)


def onehot(first_head, width, lanes):
    k = iota((128, width), 0) & 31
    h = first_head + (iota((128, width), 1) // lanes)
    return jnp.where(k == h, 1.0, 0.0).astype(BF)


def split2(v):
    hi = v.astype(BF).astype(F32)
    return hi, (v - hi).astype(BF).astype(F32)


def column(row, n):
    eye = iota((n, n), 0) == iota((n, n), 1)
    return jnp.sum(jnp.where(eye, jnp.broadcast_to(row, (n, n)), 0.0), axis=1, keepdims=True)


def call(body, name, args, outs, spaces=(), scratch=(), cost=(10**6, 1 << 20, 0), aliases=None, limit=VMEM_LIMIT):
    specs = [pl.BlockSpec(memory_space=spaces[k] if k < len(spaces) else pltpu.VMEM) for k in range(len(args))]
    return pl.pallas_call(
        body,
        in_specs=specs,
        out_specs=[pl.BlockSpec(memory_space=pltpu.VMEM)] * len(outs),
        out_shape=[jax.ShapeDtypeStruct(s, d) for s, d in outs],
        scratch_shapes=list(scratch),
        input_output_aliases=aliases or {},
        compiler_params=pltpu.CompilerParams(vmem_limit_bytes=limit),
        cost_estimate=pl.CostEstimate(flops=cost[0], bytes_accessed=cost[1], transcendentals=cost[2]),
        name=name,
    )(*args)


def conv_rows(buf, taps, start, rows):
    u = taps[0] * buf[pl.ds(start + 5, rows), :]
    for k in range(1, 4):
        u = u + taps[k] * buf[pl.ds(start + 5 + k, rows), :]
    return silu(u)


def taps_of(ref, lanes):
    return [ref[k : k + 1, lanes] for k in range(4)]


def edge_body(x_ref, bc_ref, o, sem):
    a = pltpu.make_async_copy(x_ref.at[pl.ds(TOK - 8, 8), :], o.at[:, pl.ds(0, INNER)], sem.at[0])
    b = pltpu.make_async_copy(bc_ref.at[pl.ds(TOK - 8, 8), :], o.at[:, pl.ds(INNER, 256)], sem.at[1])
    a.start()
    b.start()
    a.wait()
    b.wait()


def first_body(x_hbm, bc_hbm, cwx_hbm, cwb_hbm, dt_hbm, al_hbm, ds_hbm,
               xc_o, bc_o, pst_o, end_o, dec_o, m2_o, tl_o, te_o, tw0_o, x0_o, b0_o,
               xv, bcv, cwx, cwb, dtv, alv, dsv, buf, bufb, tw, dtab, sem):
    smalls = [(dt_hbm, dtv), (al_hbm, alv), (ds_hbm, dsv), (bc_hbm, bcv), (cwb_hbm, cwb), (cwx_hbm, cwx)]
    copies = [pltpu.make_async_copy(s, d, sem.at[k]) for k, (s, d) in enumerate(smalls)]
    for j in range(NCH):
        lanes = pl.ds(j * CHUNK, CHUNK)
        copies.append(pltpu.make_async_copy(x_hbm.at[:, lanes], xv.at[:, lanes], sem.at[6 + j]))
    for c in copies:
        c.start()
    for c in copies[:3]:
        c.wait()
    v = dtv[...].astype(F32)
    t = jnp.exp(-jnp.abs(v))
    u = 1.0 + t
    d = u - 1.0
    flat = d == 0.0
    step = jnp.maximum(v, 0.0) + jnp.where(flat, t, jnp.log(u) * t / jnp.where(flat, 1.0, d))
    a = column(alv[...], HEADS)
    L = (-LOG2E * jnp.exp(a)) * step
    lane = iota((HEADS, TOK), 1) & (SPAN - 1)
    for k in (1, 2, 4, 8, 16, 32, 64):
        L = L + jnp.where(lane >= k, pltpu.roll(L, k, 1), 0.0)
    M = jnp.log(step) * LOG2E - L
    end = jnp.concatenate(
        [jnp.broadcast_to(L[:, c * SPAN + SPAN - 1 : (c + 1) * SPAN], (HEADS, SPAN)) for c in range(NB)], axis=1
    )
    w_hi, w_lo = split2(jnp.exp2(end + M))
    e_hi, e_lo = split2(jnp.exp2(L))
    l_hi = L.astype(BF).astype(F32)
    rest = L - l_hi
    l_mid = rest.astype(BF).astype(F32)
    zero = jnp.zeros((HEADS, TOK), F32)
    twt = jnp.transpose(jnp.concatenate([w_hi, w_lo, zero, zero], axis=0)).astype(BF)
    tw[...] = twt
    tw0_o[...] = twt[0:16]
    tw[pl.ds(0, 16), :] = jnp.zeros((16, 128), BF)
    te = jnp.transpose(jnp.concatenate([e_hi, e_lo, zero, zero], axis=0))
    te_o[...] = te.astype(BF)
    tl_o[...] = jnp.transpose(jnp.concatenate([l_hi, l_mid, rest - l_mid, zero], axis=0)).astype(BF)
    for j in range(NCH):
        m2_o[j, 0:HPC, :] = M[j * HPC : (j + 1) * HPC, :]
    d_hi, d_lo = split2(column(dsv[...], HEADS))
    td = jnp.transpose(
        jnp.concatenate(
            [
                jnp.broadcast_to(d_hi, (HEADS, SPAN)),
                jnp.broadcast_to(d_lo, (HEADS, SPAN)),
                jnp.zeros((2 * HEADS, SPAN), F32),
            ],
            axis=0,
        )
    )
    rows = [te[(c + 1) * SPAN - 1 : (c + 1) * SPAN, :] for c in range(NB)]
    dtab[...] = jnp.concatenate(rows + [td[0:1, :], jnp.zeros((11, SPAN), F32)], axis=0).astype(BF)

    copies[3].wait()
    copies[4].wait()
    b0_o[...] = bcv[0:16, :]
    bufb[pl.ds(0, 8), :] = jnp.zeros((8, CHUNK), F32)
    bufb[pl.ds(8, TOK), :] = bcv[...].astype(F32)
    btaps = [cwb[k] for k in range(4)]
    bts = []
    for c in range(NB):
        v = conv_rows(bufb, btaps, c * SPAN, SPAN)
        bc_o[pl.ds(c * SPAN, SPAN), :] = v.astype(BF)
        bts.append(jnp.transpose(v[:, :STATE]).astype(BF))
    copies[5].wait()
    for j in range(NCH):
        lanes = pl.ds(j * CHUNK, CHUNK)
        sel = onehot(j * HPC, CHUNK, HD)
        dec = dot(dtab[...], sel)
        dec_o[:, lanes] = dec
        copies[6 + j].wait()
        box = buf.at[j % 2]
        box[pl.ds(0, 8), :] = jnp.zeros((8, CHUNK), F32)
        box[pl.ds(8, TOK), :] = xv[:, lanes].astype(F32)
        x0_o[:, lanes] = xv[0:16, lanes]
        taps = taps_of(cwx, lanes)
        state = None
        for c in range(NB):
            v = conv_rows(box, taps, c * SPAN, SPAN).astype(BF)
            xc_o[pl.ds(c * SPAN, SPAN), lanes] = v
            w = dot(tw[pl.ds(c * SPAN, SPAN), :], sel)
            s = dot(bts[c], (v.astype(F32) * w).astype(BF))
            state = s if c == 0 else dec[c : c + 1] * state + s
            if c < NB - 1:
                pst_o[c, :, lanes] = state
            else:
                end_o[:, lanes] = state


def first_call(x, bc, cwx, cwb, dt, al, ds):
    return call(
        first_body,
        "first",
        (x, bc, cwx, cwb, dt, al, ds),
        [
            ((TOK, INNER), BF),
            ((TOK, 256), BF),
            ((NB - 1, STATE, INNER), F32),
            ((STATE, INNER), F32),
            ((16, INNER), F32),
            ((NCH, 8, TOK), F32),
            ((TOK, 128), BF),
            ((TOK, 128), BF),
            ((16, 128), BF),
            ((16, INNER), BF),
            ((16, 256), BF),
        ],
        spaces=[pltpu.HBM] * 7,
        scratch=[
            pltpu.VMEM((TOK, INNER), BF),
            pltpu.VMEM((TOK, 256), BF),
            pltpu.VMEM((4, INNER), F32),
            pltpu.VMEM((4, 1, 256), F32),
            pltpu.VMEM((HEADS, TOK), BF),
            pltpu.VMEM((1, HEADS), F32),
            pltpu.VMEM((1, HEADS), F32),
            pltpu.VMEM((2, TOK + 8, CHUNK), F32),
            pltpu.VMEM((TOK + 8, CHUNK), F32),
            pltpu.VMEM((TOK, 128), BF),
            pltpu.VMEM((16, 128), BF),
            pltpu.SemaphoreType.DMA((6 + NCH,)),
        ],
        cost=(10**9, 4 << 20, 10**6),
    )


def wire_rows(decay):
    hi, lo = split2(decay)
    return jnp.concatenate([hi, lo, jnp.zeros((14, decay.shape[1]), F32)], axis=0)


def second_body(scal, h_ref, x0_ref, b0_ref, cwx_ref, cwb_ref, tw0_ref, end_ref, dec_ref, xc_in, bc_in,
                xc_o, bc_o, ds_o, send_o, keep_o, buf, bufb):
    bufb[pl.ds(0, 8), :] = h_ref[:, INNER:].astype(F32)
    bufb[pl.ds(8, 16), :] = b0_ref[...].astype(F32)
    v = conv_rows(bufb, [cwb_ref[k] for k in range(4)], 0, 16)
    bc_o[0:16, :] = v.astype(BF)
    b = jnp.concatenate([v[:, :STATE], jnp.zeros((SPAN - 16, STATE), F32)], axis=0)
    bt = jnp.transpose(b).astype(BF)
    buf[pl.ds(0, 8), :] = h_ref[:, :INNER].astype(F32)
    buf[pl.ds(8, 16), :] = x0_ref[...].astype(F32)
    for j in range(NCH):
        lanes = pl.ds(j * CHUNK, CHUNK)
        u = conv_rows(buf.at[:, lanes], taps_of(cwx_ref, lanes), 0, 16).astype(BF)
        xc_o[0:16, lanes] = u
        w = dot(tw0_ref[...], onehot(j * HPC, CHUNK, HD))
        xw = jnp.concatenate([u.astype(F32) * w, jnp.zeros((SPAN - 16, CHUNK), F32)], axis=0).astype(BF)
        ds_o[:, lanes] = dot(bt, xw)
    for slot in range(2):
        for q in range(4):
            half = scal[0] if slot else 1 - scal[0]
            lanes = pl.ds(pl.multiple_of((half * 4 + q) * CHUNK, CHUNK), CHUNK)
            dec = dec_ref[0:8, lanes]
            after = dec[1:2] * dec[2:3] * dec[3:4]
            state = end_ref[:, lanes] + after * ds_o[:, lanes]
            decay = dec[0:1] * after
            if slot:
                keep_o[q, 0:STATE, :] = state
                keep_o[q, STATE:WROWS, :] = jnp.concatenate([decay, jnp.zeros((15, CHUNK), F32)], axis=0)
            else:
                send_o[q, 0:STATE, :] = state.astype(BF)
                send_o[q, STATE:WROWS, :] = wire_rows(decay).astype(BF)


def second_call(scal, halo, x0, b0, cwx, cwb, tw0, end, dec, xc, bc):
    return call(
        second_body,
        "second",
        (scal, halo, x0, b0, cwx, cwb, tw0, end, dec, xc, bc),
        [
            ((TOK, INNER), BF),
            ((TOK, 256), BF),
            ((STATE, INNER), F32),
            ((4, WROWS, CHUNK), BF),
            ((4, WROWS, CHUNK), F32),
        ],
        spaces=[pltpu.SMEM],
        scratch=[pltpu.VMEM((24, INNER), F32), pltpu.VMEM((24, CHUNK), F32)],
        aliases={9: 0, 10: 1},
        cost=(10**8, 2 << 20, 10**5),
    )


def decay_of(v):
    return v[STATE : STATE + 1] + v[STATE + 1 : STATE + 2]


def small_call(body, name, scal, args, outs, scratch=()):
    return call(body, name, (scal, *args), [(o.shape, o.dtype) for o in outs], spaces=[pltpu.SMEM], scratch=scratch)


def pair_body(scal, keep_ref, recv_ref, *outs):
    core, z = scal[0], scal[1]
    for i in range(4):
        q = lax.rem(z + i, 4)
        own = keep_ref[q]
        other = recv_ref[q].astype(F32)
        early = jnp.where(core == 0, own, other)
        late = jnp.where(core == 0, other, own)
        d_early, d_late = decay_of(early), decay_of(late)
        outs[i][0:STATE, :] = (d_late * early[0:STATE] + late[0:STATE]).astype(BF)
        outs[i][STATE:WROWS, :] = wire_rows(d_early * d_late).astype(BF)


def row_body(scal, r0, r1, r2, r3, total_o, pre_o, dpre_o, box):
    z = scal[1]
    for i, r in enumerate((r0, r1, r2, r3)):
        box[lax.rem(z - i + 4, 4)] = r[...].astype(F32)
    state = jnp.zeros((STATE, CHUNK), F32)
    decay = jnp.ones((1, CHUNK), F32)
    for k in range(4):
        pre_o[k] = state
        dpre_o[k] = jnp.broadcast_to(decay, (8, CHUNK))
        v = box[k]
        d = decay_of(v)
        state = d * state + v[0:STATE]
        decay = decay * d
    total_o[0:STATE, :] = state.astype(BF)
    total_o[STATE:WROWS, :] = wire_rows(decay).astype(BF)


def plane_body(scal, r0, r1, r2, r3, pre_ref, dpre_ref, o0, o1, o2, o3, box):
    z, y = scal[1], scal[2]
    for i, r in enumerate((r0, r1, r2, r3)):
        box[lax.rem(y - i + 4, 4)] = r[...].astype(F32)
    state = jnp.zeros((STATE, CHUNK), F32)
    for k in range(3):
        v = box[k]
        state = jnp.where(k < y, decay_of(v) * state + v[0:STATE], state)
    for i, o in enumerate((o0, o1, o2, o3)):
        q = lax.rem(z + i, 4)
        d = dpre_ref[q]
        o[...] = (pre_ref[q] + d[0:1] * state).astype(BF)


def spread_body(scal, r0, r1, r2, r3, keep_ref, recv_ref, send_o, stay_o, box):
    core, z = scal[0], scal[1]
    for i, r in enumerate((r0, r1, r2, r3)):
        box[lax.rem(z - i + 4, 4)] = r[...].astype(F32)
    for q in range(4):
        early = jnp.where(core == 0, keep_ref[q], recv_ref[q].astype(F32))
        a = box[q]
        b = decay_of(early) * a + early[0:STATE]
        send_o[q] = jnp.where(core == 0, b, a).astype(BF)
        stay_o[q] = jnp.where(core == 0, a, b).astype(BF)


def mix_body(first_chunk, chunks, xc_ref, bc_ref, z_ref, m2_ref, tl_ref, te_ref, dec_ref, after_ref, yg_o, g2_o):
    causal = iota((SPAN, SPAN), 0) >= iota((SPAN, SPAN), 1)
    left = iota((SPAN, SPAN), 1) < HD
    sels = [onehot((first_chunk + k) * HPC, CHUNK, HD) for k in range(chunks)]
    wides = [onehot((first_chunk + k) * HPC, HPC * SPAN, SPAN) for k in range(chunks)]
    for c in range(NB):
        rows = pl.ds(c * SPAN, SPAN)
        bv = bc_ref[rows, :]
        s = lax.dot_general(bv[:, STATE:], bv[:, :STATE], (((1,), (1,)), ((), ())), preferred_element_type=F32)
        s = jnp.where(causal, s, 0.0)
        for k in range(chunks):
            j = first_chunk + k
            lanes = pl.ds(j * CHUNK, CHUNK)
            mine = pl.ds(k * CHUNK, CHUNK)
            x = xc_ref[rows, lanes]
            ex = dot(tl_ref[rows, :], wides[k])
            parts = []
            for h in range(HPC):
                m2 = m2_ref[j, h : h + 1, c * SPAN : (c + 1) * SPAN]
                e = ex[:, h * SPAN : (h + 1) * SPAN] + m2
                parts.append((s * jnp.exp2(jnp.minimum(e, 8.0))).astype(BF))
            ys = []
            for p in range(HPC // 2):
                xp = x[:, p * SPAN : (p + 1) * SPAN].astype(F32)
                rhs = jnp.concatenate([jnp.where(left, xp, 0.0), jnp.where(left, 0.0, xp)], axis=0).astype(BF)
                ys.append(dot(jnp.concatenate([parts[2 * p], parts[2 * p + 1]], axis=1), rhs))
            y = jnp.concatenate(ys, axis=1) + dec_ref[4:5, lanes] * x.astype(F32)
            gate = silu(z_ref[rows, lanes].astype(F32))
            yg_o[rows, mine] = (y * gate).astype(BF)
            g2_o[rows, mine] = (dot(te_ref[rows, :], sels[k]) * gate).astype(BF)


def mix_call(first_chunk, chunks, xc, bc, z, m2, tl, te, dec, after):
    return call(
        functools.partial(mix_body, first_chunk, chunks),
        "mix",
        (xc, bc, z, m2, tl, te, dec, after),
        [((TOK, chunks * CHUNK), BF)] * 2,
        spaces=[pltpu.VMEM] * 7 + [pl.ANY],
        cost=(chunks * 25 * 10**7, chunks << 20, chunks * 6 * 10**5),
    )


def gate_body(splits, scal, *refs):
    n = len(splits)
    ygs, g2s = refs[:n], refs[n : 2 * n]
    bc_ref, pst_ref, ds_ref, dec_ref, stay_ref, recv_ref, gain_ref, n_o, inv_o = refs[2 * n :]
    core = scal[0]
    place = [(p, k) for p, s in enumerate(splits) for k in range(s)]
    sums = [None] * NB
    for j in range(NCH):
        lanes = pl.ds(j * CHUNK, CHUNK)
        p, k = place[j]
        mine = pl.ds(k * CHUNK, CHUNK)
        half, q = j // 4, j % 4
        carried = jnp.where(core == half, stay_ref[q].astype(F32), recv_ref[q].astype(F32))
        gain = gain_ref[:, lanes]
        dec = dec_ref[0:8, lanes]
        for c in range(NB):
            rows = pl.ds(c * SPAN, SPAN)
            if c == 0:
                ent = carried
            else:
                carried = dec[0:1] * carried + ds_ref[:, lanes] if c == 1 else dec[c - 1 : c] * carried
                ent = carried + pst_ref[c - 1, :, lanes]
            g = ygs[p][rows, mine].astype(F32) + dot(bc_ref[rows, STATE:], ent.astype(BF)) * g2s[p][rows, mine].astype(F32)
            sq = g * g
            sq = sq[:, :128] + sq[:, 128:]
            sums[c] = sq if j == 0 else sums[c] + sq
            n_o[rows, lanes] = (g * gain).astype(BF)
    for c in range(NB):
        m = jnp.sum(sums[c], axis=1, keepdims=True) * (1.0 / INNER)
        inv_o[pl.ds(c * SPAN, SPAN), :] = jnp.broadcast_to(lax.rsqrt(m + 1e-05), (SPAN, 128))


def gate_call(splits, scal, ygs, g2s, bc, pst, ds, dec, stay, recv, gain):
    return call(
        functools.partial(gate_body, splits),
        "gate",
        (scal, *ygs, *g2s, bc, pst, ds, dec, stay, recv, gain),
        [((TOK, INNER), BF), ((TOK, 128), F32)],
        spaces=[pltpu.SMEM],
        cost=(5 * 10**8, 8 << 20, 0),
    )


def proj_body(shift, scal, n_ref, inv_ref, w_ref, a_o, b_o):
    base = lax.rem(scal[3] + shift, 4) * QOUT
    for k in range(QOUT // CHUNK):
        w = w_ref[:, pl.ds(pl.multiple_of(base + k * CHUNK, CHUNK), CHUNK)]
        y = dot(n_ref[...], w)
        for rows, o in ((pl.ds(0, 256), a_o), (pl.ds(256, 256), b_o)):
            o[:, k * CHUNK : (k + 1) * CHUNK] = (y[rows.start : rows.start + 256] * inv_ref[rows, 0:1]).astype(BF)


def proj_call(scal, n, inv, w, shift):
    return call(
        functools.partial(proj_body, shift),
        "proj",
        (scal, n, inv, w),
        [((256, QOUT), BF)] * 2,
        spaces=[pltpu.SMEM],
        cost=(2 * TOK * INNER * QOUT, 7 << 20, 0),
        limit=16 << 20,
    )


def last_body(a0, a1, a2, b0, b1, b2, o):
    for k, refs in enumerate(((a0, a1, a2), (b0, b1, b2))):
        for j in range(QOUT // CHUNK):
            lanes = pl.ds(j * CHUNK, CHUNK)
            s = refs[0][:, lanes].astype(F32) + refs[1][:, lanes].astype(F32) + refs[2][:, lanes].astype(F32)
            o[lanes, k * 256 : (k + 1) * 256] = jnp.transpose(s).astype(BF)


def last_call(*parts):
    return call(last_body, "last", parts, [((QOUT, TOK), BF)])[0]


def seq_perm(v, dy, dz, flip):
    pairs = []
    for src in range(32):
        y, z, c = src // 8, (src // 2) % 4, src % 2
        dst = (((y + dy) % 4) * 4 + (z + dz) % 4) * 2 + (1 - c if flip else c)
        pairs.append((src, dst))
    return lax.ppermute(v, "seq", pairs)


def head_perm(v, shift):
    return lax.ppermute(v, "head", [(s, (s + shift) % 4) for s in range(4)])


def on_device(x_in, bc_in, z_in, dt_raw, a_log, conv_x, conv_bc, d_skip, norm_gain, out_weight):
    bc = bc_in.reshape(TOK, 256)
    edge = call(
        edge_body,
        "edge",
        (x_in, bc),
        [((8, INNER + 256), BF)],
        spaces=[pltpu.HBM] * 2,
        scratch=[pltpu.SemaphoreType.DMA((2,))],
    )[0]
    halo = lax.ppermute(edge, "seq", [(s, s + 1) for s in range(31)])
    place = lax.axis_index("seq")
    scal = jnp.stack([place % 2, (place // 2) % 4, place // 8, lax.axis_index("head")]).astype(jnp.int32)
    xc, bcc, pst, end, dec, m2, tl, te, tw0, x0, b0 = first_call(
        x_in, bc, conv_x, conv_bc, dt_raw, a_log.reshape(1, HEADS), d_skip.reshape(1, HEADS)
    )
    xc, bcc, ds, send, keep = second_call(scal, halo, x0, b0, conv_x, conv_bc, tw0, end, dec, xc, bcc)
    recv = seq_perm(send, 0, 0, True)
    piece = jax.ShapeDtypeStruct((WROWS, CHUNK), BF)
    plain = jax.ShapeDtypeStruct((STATE, CHUNK), BF)
    box = pltpu.VMEM((4, WROWS, CHUNK), F32)
    splits = (3, 3, 2)
    work = lambda k, after: mix_call(sum(splits[:k]), splits[k], xc, bcc, z_in, m2, tl, te, dec, after)
    tie = lambda v, w: lax.optimization_barrier((v, w))
    q = small_call(pair_body, "pair", scal, (keep, recv), [piece] * 4)
    yg0, g20 = work(0, q[0])
    rows = [q[0]] + [seq_perm(q[i], 0, i, False) for i in (1, 2, 3)]
    total, pre, dpre = small_call(
        row_body,
        "row",
        scal,
        rows,
        [piece, jax.ShapeDtypeStruct((4, STATE, CHUNK), F32), jax.ShapeDtypeStruct((4, 8, CHUNK), F32)],
        [box],
    )
    yg1, g21 = work(1, total)
    cols = [total] + [seq_perm(total, i, 0, False) for i in (1, 2, 3)]
    e = small_call(plane_body, "plane", scal, (*cols, pre, dpre), [plain] * 4, [box])
    yg2, g22 = work(2, e[0])
    back = [e[0]] + [seq_perm(e[i], 0, i, False) for i in (1, 2, 3)]
    half = jax.ShapeDtypeStruct((4, STATE, CHUNK), BF)
    give, stay = small_call(
        spread_body, "spread", scal, (*back, keep, recv), [half] * 2, [pltpu.VMEM((4, STATE, CHUNK), F32)]
    )
    take = seq_perm(give, 0, 0, True)
    n, inv = gate_call(
        splits, scal, (yg0, yg1, yg2), (g20, g21, g22), bcc, pst, ds, dec, stay, take, norm_gain.reshape(1, INNER)
    )
    far_a, far_b = proj_call(scal, n, inv, out_weight, 2)
    from_left = head_perm(far_a, 1)
    from_right = head_perm(far_b, -1)
    right_a, right_b = proj_call(scal, n, inv, out_weight, 1)
    left_a, left_b = proj_call(scal, n, inv, out_weight, 3)
    near_b = head_perm(right_b, 1)
    near_a = head_perm(left_a, -1)
    add = lambda u, v: (u.astype(F32) + v.astype(F32)).astype(BF)
    sum_a = head_perm(add(right_a, from_left), 1)
    sum_b = head_perm(add(left_b, from_right), -1)
    own_a, own_b = proj_call(scal, n, inv, out_weight, 0)
    return last_call(own_a, near_a, sum_a, own_b, near_b, sum_b)


def solution(mesh):
    placed = (
        P("seq", "head"),
        P("seq", "head", None),
        P("seq", "head"),
        P("head", "seq"),
        P("head"),
        P(None, "head"),
        P(None, "head", None),
        P("head"),
        P("head"),
        P("head", None),
    )
    return jax.shard_map(
        on_device, mesh=mesh, in_specs=placed, out_specs=P("head", "seq"), check_vma=False
    )
```

```python
import functools

import jax
import jax.numpy as jnp
from jax import lax
from jax.experimental import pallas as pl
from jax.experimental.pallas import tpu as pltpu
from jax.sharding import PartitionSpec as P

SPAN = 128
HEADS = 32
HD = 64
STATE = 128
TOK = 512
NB = 4
INNER = 2048
CHUNK = 256
NCH = INNER // CHUNK
HPC = CHUNK // HD
DOUT = 4096
QOUT = 1024
WROWS = 144
LOG2E = 1.4426950408889634
BF = jnp.bfloat16
F32 = jnp.float32
VMEM_LIMIT = 8 << 20


def silu(u):
    half = 0.5 * u
    return half + half * jnp.tanh(half)


def dot(a, b):
    return jnp.dot(a, b, preferred_element_type=F32)


def iota(shape, axis):
    return lax.broadcasted_iota(jnp.int32, shape, axis)


def onehot(first_head, width, lanes, low=0, high=128):
    k = iota((128, width), 0)
    h = first_head + (iota((128, width), 1) // lanes)
    hit = ((k & 31) == h) & (k >= low) & (k < high)
    return jnp.where(hit, 1.0, 0.0).astype(BF)


def split2(v):
    hi = v.astype(BF).astype(F32)
    return hi, (v - hi).astype(BF).astype(F32)


def column(row, n):
    eye = iota((n, n), 0) == iota((n, n), 1)
    return jnp.sum(jnp.where(eye, jnp.broadcast_to(row, (n, n)), 0.0), axis=1, keepdims=True)


def call(body, name, args, outs, spaces=(), scratch=(), cost=(10**6, 1 << 20, 0), aliases=None, limit=VMEM_LIMIT):
    specs = [pl.BlockSpec(memory_space=spaces[k] if k < len(spaces) else pltpu.VMEM) for k in range(len(args))]
    return pl.pallas_call(
        body,
        in_specs=specs,
        out_specs=[pl.BlockSpec(memory_space=pltpu.VMEM)] * len(outs),
        out_shape=[jax.ShapeDtypeStruct(s, d) for s, d in outs],
        scratch_shapes=list(scratch),
        input_output_aliases=aliases or {},
        compiler_params=pltpu.CompilerParams(vmem_limit_bytes=limit),
        cost_estimate=pl.CostEstimate(flops=cost[0], bytes_accessed=cost[1], transcendentals=cost[2]),
        name=name,
    )(*args)


def conv(window, taps, rows):
    u = taps[3] * window[8:]
    for k in range(3):
        u = u + taps[k] * pltpu.roll(window, 3 - k, 0)[8:]
    return silu(u)


def taps_of(ref, lanes):
    return [ref[k : k + 1, lanes] for k in range(4)]


def split3(v):
    hi = v.astype(BF).astype(F32)
    rest = v - hi
    mid = rest.astype(BF).astype(F32)
    return hi, mid, rest - mid


def edge_body(x_ref, bc_ref, o, sem):
    a = pltpu.make_async_copy(x_ref.at[pl.ds(TOK - 8, 8), :], o.at[:, pl.ds(0, INNER)], sem.at[0])
    b = pltpu.make_async_copy(bc_ref.at[pl.ds(TOK - 8, 8), :], o.at[:, pl.ds(INNER, 256)], sem.at[1])
    a.start()
    b.start()
    a.wait()
    b.wait()


def first_body(x_hbm, bc_hbm, cwx_hbm, cwb_hbm, dt_hbm, al_hbm,
               xc_o, b_o, pst_o, end_o, dec_o, L_o, step_o, tw0_o, x0_o, b0_o,
               xv, bv, cwx, cwb, dtv, alv, buf, bufb, wbuf, tw, sem):
    smalls = [(dt_hbm, dtv), (al_hbm, alv), (bc_hbm.at[:, pl.ds(0, STATE)], bv), (cwb_hbm, cwb), (cwx_hbm, cwx)]
    copies = [pltpu.make_async_copy(s, d, sem.at[k]) for k, (s, d) in enumerate(smalls)]
    for j in range(NCH):
        lanes = pl.ds(j * CHUNK, CHUNK)
        copies.append(pltpu.make_async_copy(x_hbm.at[:, lanes], xv.at[:, lanes], sem.at[5 + j]))
    for c in copies:
        c.start()
    tri = jnp.where(iota((SPAN, SPAN), 0) <= iota((SPAN, SPAN), 1), 1.0, 0.0).astype(BF)
    copies[0].wait()
    copies[1].wait()
    v = dtv[...].astype(F32)
    t = jnp.exp(-jnp.abs(v))
    u = 1.0 + t
    d = u - 1.0
    flat = d == 0.0
    step = jnp.maximum(v, 0.0) + jnp.where(flat, t, jnp.log(u) * t / jnp.where(flat, 1.0, d))
    step_o[...] = step
    a = column(alv[...], HEADS)
    rate = jnp.concatenate(split3((-LOG2E * jnp.exp(a)) * step), axis=0).astype(BF)
    Ls, ends = [], []
    for c in range(NB):
        s = dot(rate[:, c * SPAN : (c + 1) * SPAN], tri)
        s = s[0:HEADS] + s[HEADS : 2 * HEADS] + s[2 * HEADS : 3 * HEADS]
        Ls.append(s)
        ends.append(jnp.broadcast_to(s[:, SPAN - 1 : SPAN], (HEADS, SPAN)))
    L = jnp.concatenate(Ls, axis=1)
    end = jnp.concatenate(ends, axis=1)
    L_o[...] = L
    w_hi, w_lo = split2(jnp.exp2(end - L) * step)
    d_hi, d_lo = split2(jnp.exp2(end))
    twt = jnp.transpose(jnp.concatenate([w_hi, w_lo, d_hi, d_lo], axis=0))
    tw[...] = twt.astype(BF)
    tw0_o[...] = twt[0:16].astype(BF)
    tw[pl.ds(0, 16), :] = jnp.zeros((16, 128), BF)
    rows = [twt[c * SPAN : c * SPAN + 1] for c in range(NB)]
    dtab = jnp.concatenate(rows + [jnp.zeros((12, SPAN), F32)], axis=0).astype(BF)
    wbuf[0] = dot(tw[...], onehot(0, CHUNK, HD, 0, 64))

    copies[2].wait()
    copies[3].wait()
    b0_o[...] = bv[0:16, :]
    bufb[pl.ds(0, 8), :] = jnp.zeros((8, STATE), F32)
    bufb[pl.ds(8, TOK), :] = bv[...].astype(F32)
    btaps = [cwb[k][:, :STATE] for k in range(4)]
    bts = []
    for c in range(NB):
        v = conv(bufb[pl.ds(c * SPAN, SPAN + 8), :], btaps, SPAN)
        b_o[pl.ds(c * SPAN, SPAN), :] = v.astype(BF)
        bts.append(jnp.transpose(v).astype(BF))
    copies[4].wait()
    for j in range(NCH):
        lanes = pl.ds(j * CHUNK, CHUNK)
        if j + 1 < NCH:
            wbuf[(j + 1) % 2] = dot(tw[...], onehot((j + 1) * HPC, CHUNK, HD, 0, 64))
        dec = dot(dtab, onehot(j * HPC, CHUNK, HD, 64, 128))
        dec_o[:, lanes] = dec
        copies[5 + j].wait()
        box = buf.at[j % 2]
        box[pl.ds(0, 8), :] = jnp.zeros((8, CHUNK), F32)
        box[pl.ds(8, TOK), :] = xv[:, lanes].astype(F32)
        x0_o[:, lanes] = xv[0:16, lanes]
        taps = taps_of(cwx, lanes)
        state = None
        for c in range(NB):
            v = conv(box[pl.ds(c * SPAN, SPAN + 8), :], taps, SPAN).astype(BF)
            xc_o[pl.ds(c * SPAN, SPAN), lanes] = v
            s = dot(bts[c], (v.astype(F32) * wbuf[j % 2, pl.ds(c * SPAN, SPAN), :]).astype(BF))
            state = s if c == 0 else dec[c : c + 1] * state + s
            if c < NB - 1:
                pst_o[c, :, lanes] = state
            else:
                end_o[:, lanes] = state


def first_call(x, bc, cwx, cwb, dt, al):
    return call(
        first_body,
        "first",
        (x, bc, cwx, cwb, dt, al),
        [
            ((TOK, INNER), BF),
            ((TOK, STATE), BF),
            ((NB - 1, STATE, INNER), F32),
            ((STATE, INNER), F32),
            ((16, INNER), F32),
            ((HEADS, TOK), F32),
            ((HEADS, TOK), F32),
            ((16, 128), BF),
            ((16, INNER), BF),
            ((16, STATE), BF),
        ],
        spaces=[pltpu.HBM] * 6,
        scratch=[
            pltpu.VMEM((TOK, INNER), BF),
            pltpu.VMEM((TOK, STATE), BF),
            pltpu.VMEM((4, INNER), F32),
            pltpu.VMEM((4, 1, 256), F32),
            pltpu.VMEM((HEADS, TOK), BF),
            pltpu.VMEM((1, HEADS), F32),
            pltpu.VMEM((2, TOK + 8, CHUNK), F32),
            pltpu.VMEM((TOK + 8, STATE), F32),
            pltpu.VMEM((2, TOK, CHUNK), F32),
            pltpu.VMEM((TOK, 128), BF),
            pltpu.SemaphoreType.DMA((5 + NCH,)),
        ],
        cost=(10**9, 4 << 20, 10**6),
        limit=12 << 20,
    )


def wire_rows(decay):
    hi, lo = split2(decay)
    return jnp.concatenate([hi, lo, jnp.zeros((14, decay.shape[1]), F32)], axis=0)


def second_body(scal, h_ref, x0_ref, b0_ref, cwx_ref, cwb_ref, tw0_ref, end_ref, dec_ref, xc_in, b_in,
                xc_o, b_o, ds_o, send_o, keep_o, buf):
    v = jnp.concatenate([h_ref[:, INNER : INNER + STATE].astype(F32), b0_ref[...].astype(F32)], axis=0)
    v = conv(v, [cwb_ref[k][:, :STATE] for k in range(4)], 16)
    b_o[0:16, :] = v.astype(BF)
    bt = jnp.transpose(jnp.concatenate([v, jnp.zeros((SPAN - 16, STATE), F32)], axis=0)).astype(BF)
    buf[pl.ds(0, 8), :] = h_ref[:, :INNER].astype(F32)
    buf[pl.ds(8, 16), :] = x0_ref[...].astype(F32)
    for j in range(NCH):
        lanes = pl.ds(j * CHUNK, CHUNK)
        u = conv(buf[:, lanes], taps_of(cwx_ref, lanes), 16).astype(BF)
        xc_o[0:16, lanes] = u
        w = dot(tw0_ref[...], onehot(j * HPC, CHUNK, HD, 0, 64))
        xw = jnp.concatenate([u.astype(F32) * w, jnp.zeros((SPAN - 16, CHUNK), F32)], axis=0).astype(BF)
        ds_o[:, lanes] = dot(bt, xw)
    for slot in range(2):
        for q in range(4):
            half = scal[0] if slot else 1 - scal[0]
            lanes = pl.ds(pl.multiple_of((half * 4 + q) * CHUNK, CHUNK), CHUNK)
            dec = dec_ref[0:8, lanes]
            after = dec[1:2] * dec[2:3] * dec[3:4]
            state = end_ref[:, lanes] + after * ds_o[:, lanes]
            decay = dec[0:1] * after
            if slot:
                keep_o[q, 0:STATE, :] = state
                keep_o[q, STATE:WROWS, :] = jnp.concatenate([decay, jnp.zeros((15, CHUNK), F32)], axis=0)
            else:
                send_o[q, 0:STATE, :] = state.astype(BF)
                send_o[q, STATE:WROWS, :] = wire_rows(decay).astype(BF)


def second_call(scal, halo, x0, b0, cwx, cwb, tw0, end, dec, xc, b):
    return call(
        second_body,
        "second",
        (scal, halo, x0, b0, cwx, cwb, tw0, end, dec, xc, b),
        [
            ((TOK, INNER), BF),
            ((TOK, STATE), BF),
            ((STATE, INNER), F32),
            ((4, WROWS, CHUNK), BF),
            ((4, WROWS, CHUNK), F32),
        ],
        spaces=[pltpu.SMEM],
        scratch=[pltpu.VMEM((24, INNER), F32)],
        aliases={9: 0, 10: 1},
        cost=(10**8, 2 << 20, 10**5),
    )


def table_body(L_ref, step_ref, ds_ref, h_ref, bc_ref, cwb_ref, b_ref, after_ref,
               c_o, sc_o, m2_o, tl_o, te_o, td_o, buf):
    L = L_ref[...]
    M = jnp.log(step_ref[...]) * LOG2E - L
    for j in range(NCH):
        m2_o[j, 0:HPC, :] = M[j * HPC : (j + 1) * HPC, :]
    zero = jnp.zeros((HEADS, TOK), F32)
    tl_o[...] = jnp.transpose(jnp.concatenate([*split3(L), zero], axis=0)).astype(BF)
    parts, before = [], jnp.zeros((HEADS, SPAN), F32)
    for c in range(NB):
        s = L[:, c * SPAN : (c + 1) * SPAN]
        parts.append(before + s)
        before = before + jnp.broadcast_to(s[:, SPAN - 1 : SPAN], (HEADS, SPAN))
    e = [*split2(jnp.exp2(L)), *split2(jnp.exp2(jnp.concatenate(parts, axis=1)))]
    te_o[...] = jnp.transpose(jnp.concatenate(e, axis=0)).astype(BF)
    d = [jnp.broadcast_to(p, (HEADS, SPAN)) for p in split2(column(ds_ref[...], HEADS))]
    d = jnp.concatenate([*d, jnp.zeros((2 * HEADS, SPAN), F32)], axis=0)
    td_o[...] = jnp.transpose(d)[0:16].astype(BF)
    buf[pl.ds(0, 8), :] = h_ref[:, INNER + STATE :].astype(F32)
    buf[pl.ds(8, TOK), :] = bc_ref[:, STATE:].astype(F32)
    taps = [cwb_ref[k][:, STATE:] for k in range(4)]
    causal = iota((SPAN, SPAN), 0) >= iota((SPAN, SPAN), 1)
    for c in range(NB):
        rows = pl.ds(c * SPAN, SPAN)
        v = conv(buf[pl.ds(c * SPAN, SPAN + 8), :], taps, SPAN).astype(BF)
        c_o[rows, :] = v
        s = lax.dot_general(v, b_ref[rows, :], (((1,), (1,)), ((), ())), preferred_element_type=F32)
        sc_o[c] = jnp.where(causal, s, 0.0)


def table_call(L, step, ds, halo, bc, cwb, b, after):
    return call(
        table_body,
        "table",
        (L, step, ds, halo, bc, cwb, b, after),
        [
            ((TOK, STATE), BF),
            ((NB, SPAN, SPAN), F32),
            ((NCH, 8, TOK), F32),
            ((TOK, 128), BF),
            ((TOK, 128), BF),
            ((16, 128), BF),
        ],
        spaces=[pltpu.VMEM] * 7 + [pl.ANY],
        scratch=[pltpu.VMEM((TOK + 8, STATE), F32)],
        cost=(10**8, 2 << 20, 10**5),
    )


def decay_of(v):
    return v[STATE : STATE + 1] + v[STATE + 1 : STATE + 2]


def small_call(body, name, scal, args, outs, scratch=(), after=()):
    n = 1 + len(args)
    m = len(after)

    def run(*refs):
        body(*refs[:n], *refs[n + m :])

    return call(
        run,
        name,
        (scal, *args, *after),
        [(o.shape, o.dtype) for o in outs],
        spaces=[pltpu.SMEM] + [pltpu.VMEM] * len(args) + [pl.ANY] * m,
        scratch=scratch,
    )


def pair_body(scal, keep_ref, recv_ref, *outs):
    core, z = scal[0], scal[1]
    for i in range(4):
        q = lax.rem(z + i, 4)
        own = keep_ref[q]
        other = recv_ref[q].astype(F32)
        early = jnp.where(core == 0, own, other)
        late = jnp.where(core == 0, other, own)
        d_early, d_late = decay_of(early), decay_of(late)
        outs[i][0:STATE, :] = (d_late * early[0:STATE] + late[0:STATE]).astype(BF)
        outs[i][STATE:WROWS, :] = wire_rows(d_early * d_late).astype(BF)


def row_body(scal, r0, r1, r2, r3, total_o, pre_o, dpre_o, box):
    z = scal[1]
    for i, r in enumerate((r0, r1, r2, r3)):
        box[lax.rem(z - i + 4, 4)] = r[...].astype(F32)
    state = jnp.zeros((STATE, CHUNK), F32)
    decay = jnp.ones((1, CHUNK), F32)
    for k in range(4):
        pre_o[k] = state
        dpre_o[k] = jnp.broadcast_to(decay, (8, CHUNK))
        v = box[k]
        d = decay_of(v)
        state = d * state + v[0:STATE]
        decay = decay * d
    total_o[0:STATE, :] = state.astype(BF)
    total_o[STATE:WROWS, :] = wire_rows(decay).astype(BF)


def plane_body(scal, r0, r1, r2, r3, pre_ref, dpre_ref, o0, o1, o2, o3, box):
    z, y = scal[1], scal[2]
    for i, r in enumerate((r0, r1, r2, r3)):
        box[lax.rem(y - i + 4, 4)] = r[...].astype(F32)
    state = jnp.zeros((STATE, CHUNK), F32)
    for k in range(3):
        v = box[k]
        state = jnp.where(k < y, decay_of(v) * state + v[0:STATE], state)
    for i, o in enumerate((o0, o1, o2, o3)):
        q = lax.rem(z + i, 4)
        d = dpre_ref[q]
        o[...] = (pre_ref[q] + d[0:1] * state).astype(BF)


def spread_body(scal, r0, r1, r2, r3, keep_ref, recv_ref, send_o, stay_o, box):
    core, z = scal[0], scal[1]
    for i, r in enumerate((r0, r1, r2, r3)):
        box[lax.rem(z - i + 4, 4)] = r[...].astype(F32)
    for q in range(4):
        early = jnp.where(core == 0, keep_ref[q], recv_ref[q].astype(F32))
        a = box[q]
        b = decay_of(early) * a + early[0:STATE]
        send_o[q] = jnp.where(core == 0, b, a).astype(BF)
        stay_o[q] = jnp.where(core == 0, a, b).astype(BF)


def mix_body(first_chunk, chunks, xc_ref, c_ref, sc_ref, z_ref, m2_ref, tl_ref, te_ref, td_ref, dec_ref, pst_ref,
             ds_ref, after_ref, yg_o, g2_o, ex, ee):
    left = iota((SPAN, SPAN), 1) < HD

    def expand(k):
        j = first_chunk + k
        ex[k % 2] = dot(tl_ref[...], onehot(j * HPC, HPC * SPAN, SPAN))
        ee[k % 2, :, 0:CHUNK] = dot(te_ref[...], onehot(j * HPC, CHUNK, HD, 0, 64))
        ee[k % 2, :, CHUNK:] = dot(te_ref[...], onehot(j * HPC, CHUNK, HD, 64, 128))

    expand(0)
    for k in range(chunks):
        j = first_chunk + k
        lanes = pl.ds(j * CHUNK, CHUNK)
        mine = pl.ds(k * CHUNK, CHUNK)
        if k + 1 < chunks:
            expand(k + 1)
        skip = dot(td_ref[...], onehot(j * HPC, CHUNK, HD))[0:1]
        fix = ds_ref[:, lanes]
        for c in range(NB):
            rows = pl.ds(c * SPAN, SPAN)
            s = sc_ref[c]
            x = xc_ref[rows, lanes]
            parts = []
            for h in range(HPC):
                m2 = m2_ref[j, h : h + 1, c * SPAN : (c + 1) * SPAN]
                e = ex[k % 2, rows, h * SPAN : (h + 1) * SPAN] + m2
                parts.append((s * jnp.exp2(jnp.minimum(e, 8.0))).astype(BF))
            ys = []
            for p in range(HPC // 2):
                xp = x[:, p * SPAN : (p + 1) * SPAN].astype(F32)
                rhs = jnp.concatenate([jnp.where(left, xp, 0.0), jnp.where(left, 0.0, xp)], axis=0).astype(BF)
                ys.append(dot(jnp.concatenate([parts[2 * p], parts[2 * p + 1]], axis=1), rhs))
            y = jnp.concatenate(ys, axis=1) + skip * x.astype(F32)
            if c > 0:
                if c > 1:
                    fix = dec_ref[c - 1 : c, lanes] * fix
                ent = (pst_ref[c - 1, :, lanes] + fix).astype(BF)
                y = y + ee[k % 2, rows, 0:CHUNK] * dot(c_ref[rows, :], ent)
            gate = silu(z_ref[rows, lanes].astype(F32))
            yg_o[rows, mine] = (y * gate).astype(BF)
            g2_o[rows, mine] = (ee[k % 2, rows, CHUNK:] * gate).astype(BF)


def mix_call(first_chunk, chunks, *args):
    return call(
        functools.partial(mix_body, first_chunk, chunks),
        "mix",
        args,
        [((TOK, chunks * CHUNK), BF)] * 2,
        spaces=[pltpu.VMEM] * (len(args) - 1) + [pl.ANY],
        scratch=[pltpu.VMEM((2, TOK, HPC * SPAN), F32), pltpu.VMEM((2, TOK, 2 * CHUNK), F32)],
        cost=(chunks * 25 * 10**7, chunks << 20, chunks * 6 * 10**5),
    )


def gate_body(splits, scal, *refs):
    n = len(splits)
    ygs, g2s = refs[:n], refs[n : 2 * n]
    c_ref, stay_ref, recv_ref, gain_ref, n_o, inv_o, ce = refs[2 * n :]
    core = scal[0]
    place = [(p, k) for p, s in enumerate(splits) for k in range(s)]
    sums = [None] * NB

    def carry(j):
        v = jnp.where(core == j // 4, stay_ref[j % 4].astype(F32), recv_ref[j % 4].astype(F32))
        ce[j % 2] = dot(c_ref[...], v.astype(BF))

    carry(0)
    for j in range(NCH):
        lanes = pl.ds(j * CHUNK, CHUNK)
        p, k = place[j]
        mine = pl.ds(k * CHUNK, CHUNK)
        if j + 1 < NCH:
            carry(j + 1)
        gain = gain_ref[:, lanes]
        for c in range(NB):
            rows = pl.ds(c * SPAN, SPAN)
            g = ygs[p][rows, mine].astype(F32) + ce[j % 2, rows, :] * g2s[p][rows, mine].astype(F32)
            sq = g * g
            sq = sq[:, :128] + sq[:, 128:]
            sums[c] = sq if j == 0 else sums[c] + sq
            n_o[rows, lanes] = (g * gain).astype(BF)
    for c in range(NB):
        m = jnp.sum(sums[c], axis=1, keepdims=True) * (1.0 / INNER)
        inv_o[pl.ds(c * SPAN, SPAN), :] = jnp.broadcast_to(lax.rsqrt(m + 1e-05), (SPAN, 128))


def gate_call(splits, scal, ygs, g2s, cm, stay, recv, gain):
    return call(
        functools.partial(gate_body, splits),
        "gate",
        (scal, *ygs, *g2s, cm, stay, recv, gain),
        [((TOK, INNER), BF), ((TOK, 128), F32)],
        spaces=[pltpu.SMEM],
        scratch=[pltpu.VMEM((2, TOK, CHUNK), F32)],
        cost=(5 * 10**8, 8 << 20, 0),
    )


def proj_body(shift, scal, n_ref, inv_ref, w_ref, a_o, b_o):
    base = lax.rem(scal[3] + shift, 4) * QOUT
    for k in range(QOUT // CHUNK):
        w = w_ref[:, pl.ds(pl.multiple_of(base + k * CHUNK, CHUNK), CHUNK)]
        y = dot(n_ref[...], w)
        for rows, o in ((pl.ds(0, 256), a_o), (pl.ds(256, 256), b_o)):
            o[:, k * CHUNK : (k + 1) * CHUNK] = (y[rows.start : rows.start + 256] * inv_ref[rows, 0:1]).astype(BF)


def proj_call(scal, n, inv, w, shift):
    return call(
        functools.partial(proj_body, shift),
        "proj",
        (scal, n, inv, w),
        [((256, QOUT), BF)] * 2,
        spaces=[pltpu.SMEM],
        cost=(2 * TOK * INNER * QOUT, 7 << 20, 0),
        limit=8 << 20,
    )


def last_body(a0, a1, a2, b0, b1, b2, o):
    for k, refs in enumerate(((a0, a1, a2), (b0, b1, b2))):
        for j in range(QOUT // CHUNK):
            lanes = pl.ds(j * CHUNK, CHUNK)
            s = refs[0][:, lanes].astype(F32) + refs[1][:, lanes].astype(F32) + refs[2][:, lanes].astype(F32)
            o[lanes, k * 256 : (k + 1) * 256] = jnp.transpose(s).astype(BF)


def last_call(*parts):
    return call(last_body, "last", parts, [((QOUT, TOK), BF)])[0]


def seq_perm(v, dy, dz, flip):
    pairs = []
    for src in range(32):
        y, z, c = src // 8, (src // 2) % 4, src % 2
        dst = (((y + dy) % 4) * 4 + (z + dz) % 4) * 2 + (1 - c if flip else c)
        pairs.append((src, dst))
    return lax.ppermute(v, "seq", pairs)


def head_perm(v, shift):
    return lax.ppermute(v, "head", [(s, (s + shift) % 4) for s in range(4)])


def on_device(x_in, bc_in, z_in, dt_raw, a_log, conv_x, conv_bc, d_skip, norm_gain, out_weight):
    bc = bc_in.reshape(TOK, 256)
    hbm = lambda v: pltpu.with_memory_space_constraint(v, pltpu.HBM)
    edge = call(
        edge_body,
        "edge",
        (hbm(x_in), hbm(bc)),
        [((8, INNER + 256), BF)],
        spaces=[pltpu.HBM] * 2,
        scratch=[pltpu.SemaphoreType.DMA((2,))],
    )[0]
    halo = lax.ppermute(edge, "seq", [(s, s + 1) for s in range(31)])
    place = lax.axis_index("seq")
    scal = jnp.stack([place % 2, (place // 2) % 4, place // 8, lax.axis_index("head")]).astype(jnp.int32)
    xc, b, pst, end, dec, L, step, tw0, x0, b0 = first_call(
        *(hbm(v) for v in (x_in, bc, conv_x, conv_bc, dt_raw, a_log.reshape(1, HEADS)))
    )
    xc, b, ds, send, keep = second_call(scal, halo, x0, b0, conv_x, conv_bc, tw0, end, dec, xc, b)
    recv = seq_perm(send, 0, 0, True)
    cm, sc, m2, tl, te, td = table_call(L, step, d_skip.reshape(1, HEADS), halo, bc, conv_bc, b, send)
    piece = jax.ShapeDtypeStruct((WROWS, CHUNK), BF)
    plain = jax.ShapeDtypeStruct((STATE, CHUNK), BF)
    box = pltpu.VMEM((4, WROWS, CHUNK), F32)
    splits = (3, 3, 2)
    work = lambda k, after: mix_call(
        sum(splits[:k]), splits[k], xc, cm, sc, z_in, m2, tl, te, td, dec, pst, ds, after
    )
    q = small_call(pair_body, "pair", scal, (keep, recv), [piece] * 4, (), (cm,))
    yg0, g20 = work(0, q[0])
    rows = [q[0]] + [seq_perm(q[i], 0, i, False) for i in (1, 2, 3)]
    total, pre, dpre = small_call(
        row_body,
        "row",
        scal,
        rows,
        [piece, jax.ShapeDtypeStruct((4, STATE, CHUNK), F32), jax.ShapeDtypeStruct((4, 8, CHUNK), F32)],
        [box],
        (yg0,),
    )
    yg1, g21 = work(1, total)
    cols = [total] + [seq_perm(total, i, 0, False) for i in (1, 2, 3)]
    e = small_call(plane_body, "plane", scal, (*cols, pre, dpre), [plain] * 4, [box], (yg1,))
    yg2, g22 = work(2, e[0])
    back = [e[0]] + [seq_perm(e[i], 0, i, False) for i in (1, 2, 3)]
    half = jax.ShapeDtypeStruct((4, STATE, CHUNK), BF)
    give, stay = small_call(
        spread_body, "spread", scal, (*back, keep, recv), [half] * 2, [pltpu.VMEM((4, STATE, CHUNK), F32)], (yg2,)
    )
    take = seq_perm(give, 0, 0, True)
    n, inv = gate_call(
        splits, scal, (yg0, yg1, yg2), (g20, g21, g22), cm, stay, take, norm_gain.reshape(1, INNER)
    )
    far_a, far_b = proj_call(scal, n, inv, out_weight, 2)
    from_left = head_perm(far_a, 1)
    from_right = head_perm(far_b, -1)
    right_a, right_b = proj_call(scal, n, inv, out_weight, 1)
    left_a, left_b = proj_call(scal, n, inv, out_weight, 3)
    near_b = head_perm(right_b, 1)
    near_a = head_perm(left_a, -1)
    add = lambda u, v: (u.astype(F32) + v.astype(F32)).astype(BF)
    sum_a = head_perm(add(right_a, from_left), 1)
    sum_b = head_perm(add(left_b, from_right), -1)
    own_a, own_b = proj_call(scal, n, inv, out_weight, 0)
    return last_call(own_a, near_a, sum_a, own_b, near_b, sum_b)


def solution(mesh):
    placed = (
        P("seq", "head"),
        P("seq", "head", None),
        P("seq", "head"),
        P("head", "seq"),
        P("head"),
        P(None, "head"),
        P(None, "head", None),
        P("head"),
        P("head"),
        P("head", None),
    )
    return jax.shard_map(
        on_device, mesh=mesh, in_specs=placed, out_specs=P("head", "seq"), check_vma=False
    )
```

```python
import functools

import jax
import jax.numpy as jnp
from jax import lax
from jax.experimental import pallas as pl
from jax.experimental.pallas import tpu as pltpu
from jax.sharding import PartitionSpec as P

SPAN = 128
HEADS = 32
HD = 64
STATE = 128
TOK = 512
HALF = 256
NB = 4
INNER = 2048
CHUNK = 256
NCH = INNER // CHUNK
HPC = CHUNK // HD
DOUT = 4096
QOUT = 1024
WROWS = 144
LOG2E = 1.4426950408889634
BF = jnp.bfloat16
F32 = jnp.float32
VMEM_LIMIT = 8 << 20


def silu(u):
    half = 0.5 * u
    return half + half * jnp.tanh(half)


def dot(a, b):
    return jnp.dot(a, b, preferred_element_type=F32)


def iota(shape, axis):
    return lax.broadcasted_iota(jnp.int32, shape, axis)


def onehot(first_head, width, lanes, low=0, high=128):
    k = iota((128, width), 0)
    h = first_head + (iota((128, width), 1) // lanes)
    hit = ((k & 31) == h) & (k >= low) & (k < high)
    return jnp.where(hit, 1.0, 0.0).astype(BF)


def split2(v):
    hi = v.astype(BF).astype(F32)
    return hi, (v - hi).astype(BF).astype(F32)


def column(row, n):
    eye = iota((n, n), 0) == iota((n, n), 1)
    return jnp.sum(jnp.where(eye, jnp.broadcast_to(row, (n, n)), 0.0), axis=1, keepdims=True)


def call(body, name, args, outs, spaces=(), scratch=(), cost=(10**6, 1 << 20, 0), aliases=None, limit=VMEM_LIMIT):
    specs = [pl.BlockSpec(memory_space=spaces[k] if k < len(spaces) else pltpu.VMEM) for k in range(len(args))]
    return pl.pallas_call(
        body,
        in_specs=specs,
        out_specs=[pl.BlockSpec(memory_space=pltpu.VMEM)] * len(outs),
        out_shape=[jax.ShapeDtypeStruct(s, d) for s, d in outs],
        scratch_shapes=list(scratch),
        input_output_aliases=aliases or {},
        compiler_params=pltpu.CompilerParams(vmem_limit_bytes=limit),
        cost_estimate=pl.CostEstimate(flops=cost[0], bytes_accessed=cost[1], transcendentals=cost[2]),
        name=name,
    )(*args)


def conv(window, taps, rows):
    u = taps[3] * window[8:]
    for k in range(3):
        u = u + taps[k] * pltpu.roll(window, 3 - k, 0)[8:]
    return silu(u)


def taps_of(ref, lanes):
    return [ref[k : k + 1, lanes] for k in range(4)]


def split3(v):
    hi = v.astype(BF).astype(F32)
    rest = v - hi
    mid = rest.astype(BF).astype(F32)
    return hi, mid, rest - mid


def edge_body(x_ref, bc_ref, o, sem):
    a = pltpu.make_async_copy(x_ref.at[pl.ds(TOK - 8, 8), :], o.at[:, pl.ds(0, INNER)], sem.at[0])
    b = pltpu.make_async_copy(bc_ref.at[pl.ds(TOK - 8, 8), :], o.at[:, pl.ds(INNER, 256)], sem.at[1])
    a.start()
    b.start()
    a.wait()
    b.wait()


def first_body(x_hbm, bv, cwx, cwb, dtv, alv,
               xc_o, b_o, pst_o, end_o, dec_o, L_o, step_o, tw0_o, x0_o, b0_o,
               xv, wbuf, tw, bts, xw, sem):
    copies = []
    for j in range(NCH):
        lanes = pl.ds(j * CHUNK, CHUNK)
        copies.append(pltpu.make_async_copy(x_hbm.at[:, lanes], xv.at[:, lanes], sem.at[j]))
        copies[j].start()
    tri = jnp.where(iota((SPAN, SPAN), 0) <= iota((SPAN, SPAN), 1), 1.0, 0.0).astype(BF)
    v = dtv[...].astype(F32)
    t = jnp.exp(-jnp.abs(v))
    u = 1.0 + t
    d = u - 1.0
    flat = d == 0.0
    step = jnp.maximum(v, 0.0) + jnp.where(flat, t, jnp.log(u) * t / jnp.where(flat, 1.0, d))
    step_o[...] = step
    a = column(alv[...], HEADS)
    rate = jnp.concatenate(split3((-LOG2E * jnp.exp(a)) * step), axis=0).astype(BF)
    Ls, ends = [], []
    for c in range(NB):
        s = dot(rate[:, c * SPAN : (c + 1) * SPAN], tri)
        s = s[0:HEADS] + s[HEADS : 2 * HEADS] + s[2 * HEADS : 3 * HEADS]
        Ls.append(s)
        ends.append(jnp.broadcast_to(s[:, SPAN - 1 : SPAN], (HEADS, SPAN)))
    L = jnp.concatenate(Ls, axis=1)
    end = jnp.concatenate(ends, axis=1)
    L_o[...] = L
    w_hi, w_lo = split2(jnp.exp2(end - L) * step)
    d_hi, d_lo = split2(jnp.exp2(end))
    twt = jnp.transpose(jnp.concatenate([w_hi, w_lo, d_hi, d_lo], axis=0))
    tw[...] = twt.astype(BF)
    tw0_o[...] = twt[0:16].astype(BF)
    tw[pl.ds(0, 16), :] = jnp.zeros((16, 128), BF)
    rows = [twt[c * SPAN : c * SPAN + 1] for c in range(NB)]
    dtab = jnp.concatenate(rows + [jnp.zeros((12, SPAN), F32)], axis=0).astype(BF)
    wbuf[0] = dot(tw[...], onehot(0, CHUNK, HD, 0, 64))

    b0_o[...] = bv[0:16, :STATE]
    btaps = [cwb[k][:, :STATE] for k in range(4)]
    nothing = jnp.zeros((8, STATE), F32)
    for c in range(NB):
        if c == 0:
            window = jnp.concatenate([nothing, bv[0:SPAN, :STATE].astype(F32)], axis=0)
        else:
            window = bv[pl.ds(c * SPAN - 8, SPAN + 8), :STATE].astype(F32)
        v = conv(window, btaps, SPAN)
        b_o[pl.ds(c * SPAN, SPAN), :] = v.astype(BF)
        bts[c] = jnp.transpose(v).astype(BF)
    decs = [None] * (NCH + 1)
    for j in range(NCH + 1):
        lanes = pl.ds(j * CHUNK, CHUNK)
        if j < NCH:
            if j + 1 < NCH:
                wbuf[(j + 1) % 2] = dot(tw[...], onehot((j + 1) * HPC, CHUNK, HD, 0, 64))
            dec_o[:, lanes] = dot(dtab, onehot(j * HPC, CHUNK, HD, 64, 128))
            copies[j].wait()
            x0_o[:, lanes] = xv[0:16, lanes]
        state = None
        for c in range(NB):
            if j < NCH:
                for r in (0, 64):
                    for l in (0, 128):
                        row = c * SPAN + r
                        part = pl.ds(j * CHUNK + l, 128)
                        if row == 0:
                            window = jnp.concatenate([nothing, xv[0:64, part].astype(F32)], axis=0)
                        else:
                            window = xv[pl.ds(row - 8, 72), part].astype(F32)
                        v = conv(window, taps_of(cwx, part), 64).astype(BF)
                        xc_o[pl.ds(row, 64), part] = v
                        w = wbuf[j % 2, pl.ds(row, 64), l : l + 128]
                        xw[j % 2, pl.ds(row, 64), l : l + 128] = (v.astype(F32) * w).astype(BF)
            if j > 0:
                before = pl.ds((j - 1) * CHUNK, CHUNK)
                s = dot(bts[c], xw[(j - 1) % 2, pl.ds(c * SPAN, SPAN), :])
                state = s if c == 0 else dec_o[c : c + 1, before] * state + s
                if c < NB - 1:
                    pst_o[c, :, before] = state
                else:
                    end_o[:, before] = state


def first_call(x, bc, cwx, cwb, dt, al):
    return call(
        first_body,
        "first",
        (x, bc, cwx, cwb, dt, al),
        [
            ((TOK, INNER), BF),
            ((TOK, STATE), BF),
            ((NB - 1, STATE, INNER), F32),
            ((STATE, INNER), F32),
            ((16, INNER), F32),
            ((HEADS, TOK), F32),
            ((HEADS, TOK), F32),
            ((16, 128), BF),
            ((16, INNER), BF),
            ((16, STATE), BF),
        ],
        spaces=[pltpu.HBM],
        scratch=[
            pltpu.VMEM((TOK, INNER), BF),
            pltpu.VMEM((2, TOK, CHUNK), F32),
            pltpu.VMEM((TOK, 128), BF),
            pltpu.VMEM((NB, STATE, SPAN), BF),
            pltpu.VMEM((2, TOK, CHUNK), BF),
            pltpu.SemaphoreType.DMA((NCH,)),
        ],
        cost=(10**9, 4 << 20, 10**6),
        limit=12 << 20,
    )


def wire_rows(decay):
    hi, lo = split2(decay)
    return jnp.concatenate([hi, lo, jnp.zeros((14, decay.shape[1]), F32)], axis=0)


def second_body(scal, h_ref, x0_ref, b0_ref, cwx_ref, cwb_ref, tw0_ref, end_ref, dec_ref, xc_in, b_in,
                xc_o, b_o, ds_o, send_o, keep_o, buf):
    v = jnp.concatenate([h_ref[:, INNER : INNER + STATE].astype(F32), b0_ref[...].astype(F32)], axis=0)
    v = conv(v, [cwb_ref[k][:, :STATE] for k in range(4)], 16)
    b_o[0:16, :] = v.astype(BF)
    bt = jnp.transpose(jnp.concatenate([v, jnp.zeros((SPAN - 16, STATE), F32)], axis=0)).astype(BF)
    buf[pl.ds(0, 8), :] = h_ref[:, :INNER].astype(F32)
    buf[pl.ds(8, 16), :] = x0_ref[...].astype(F32)
    for j in range(NCH):
        lanes = pl.ds(j * CHUNK, CHUNK)
        u = conv(buf[:, lanes], taps_of(cwx_ref, lanes), 16).astype(BF)
        xc_o[0:16, lanes] = u
        w = dot(tw0_ref[...], onehot(j * HPC, CHUNK, HD, 0, 64))
        xw = jnp.concatenate([u.astype(F32) * w, jnp.zeros((SPAN - 16, CHUNK), F32)], axis=0).astype(BF)
        ds_o[:, lanes] = dot(bt, xw)
    for slot in range(2):
        for q in range(4):
            half = scal[0] if slot else 1 - scal[0]
            lanes = pl.ds(pl.multiple_of((half * 4 + q) * CHUNK, CHUNK), CHUNK)
            dec = dec_ref[0:8, lanes]
            after = dec[1:2] * dec[2:3] * dec[3:4]
            state = end_ref[:, lanes] + after * ds_o[:, lanes]
            decay = dec[0:1] * after
            if slot:
                keep_o[q, 0:STATE, :] = state
                keep_o[q, STATE:WROWS, :] = jnp.concatenate([decay, jnp.zeros((15, CHUNK), F32)], axis=0)
            else:
                send_o[q, 0:STATE, :] = state.astype(BF)
                send_o[q, STATE:WROWS, :] = wire_rows(decay).astype(BF)


def second_call(scal, halo, x0, b0, cwx, cwb, tw0, end, dec, xc, b):
    return call(
        second_body,
        "second",
        (scal, halo, x0, b0, cwx, cwb, tw0, end, dec, xc, b),
        [
            ((TOK, INNER), BF),
            ((TOK, STATE), BF),
            ((STATE, INNER), F32),
            ((4, WROWS, CHUNK), BF),
            ((4, WROWS, CHUNK), F32),
        ],
        spaces=[pltpu.SMEM],
        scratch=[pltpu.VMEM((24, INNER), F32)],
        aliases={9: 0, 10: 1},
        cost=(10**8, 2 << 20, 10**5),
    )


def table_body(L_ref, step_ref, ds_ref, h_ref, bc_ref, cwb_ref, b_ref, after_ref,
               c_o, sc_o, m2_o, tl_o, te_o, td_o, buf):
    L = L_ref[...]
    M = jnp.log(step_ref[...]) * LOG2E - L
    for j in range(NCH):
        m2_o[j, 0:HPC, :] = M[j * HPC : (j + 1) * HPC, :]
    zero = jnp.zeros((HEADS, TOK), F32)
    tl_o[...] = jnp.transpose(jnp.concatenate([*split3(L), zero], axis=0)).astype(BF)
    parts, before = [], jnp.zeros((HEADS, SPAN), F32)
    for c in range(NB):
        s = L[:, c * SPAN : (c + 1) * SPAN]
        parts.append(before + s)
        before = before + jnp.broadcast_to(s[:, SPAN - 1 : SPAN], (HEADS, SPAN))
    e = [*split2(jnp.exp2(L)), *split2(jnp.exp2(jnp.concatenate(parts, axis=1)))]
    te_o[...] = jnp.transpose(jnp.concatenate(e, axis=0)).astype(BF)
    d = [jnp.broadcast_to(p, (HEADS, SPAN)) for p in split2(column(ds_ref[...], HEADS))]
    d = jnp.concatenate([*d, jnp.zeros((2 * HEADS, SPAN), F32)], axis=0)
    td_o[...] = jnp.transpose(d)[0:16].astype(BF)
    buf[pl.ds(0, 8), :] = h_ref[:, INNER + STATE :].astype(F32)
    buf[pl.ds(8, TOK), :] = bc_ref[:, STATE:].astype(F32)
    taps = [cwb_ref[k][:, STATE:] for k in range(4)]
    causal = iota((SPAN, SPAN), 0) >= iota((SPAN, SPAN), 1)
    for c in range(NB):
        rows = pl.ds(c * SPAN, SPAN)
        v = conv(buf[pl.ds(c * SPAN, SPAN + 8), :], taps, SPAN).astype(BF)
        c_o[rows, :] = v
        s = lax.dot_general(v, b_ref[rows, :], (((1,), (1,)), ((), ())), preferred_element_type=F32)
        sc_o[c] = jnp.where(causal, s, 0.0)


def table_call(L, step, ds, halo, bc, cwb, b, after):
    return call(
        table_body,
        "table",
        (L, step, ds, halo, bc, cwb, b, after),
        [
            ((TOK, STATE), BF),
            ((NB, SPAN, SPAN), F32),
            ((NCH, 8, TOK), F32),
            ((TOK, 128), BF),
            ((TOK, 128), BF),
            ((16, 128), BF),
        ],
        spaces=[pltpu.VMEM] * 7 + [pl.ANY],
        scratch=[pltpu.VMEM((TOK + 8, STATE), F32)],
        cost=(10**8, 2 << 20, 10**5),
    )


def decay_of(v):
    return v[STATE : STATE + 1] + v[STATE + 1 : STATE + 2]


def small_call(body, name, scal, args, outs, scratch=(), after=()):
    n = 1 + len(args)
    m = len(after)

    def run(*refs):
        body(*refs[:n], *refs[n + m :])

    return call(
        run,
        name,
        (scal, *args, *after),
        [(o.shape, o.dtype) for o in outs],
        spaces=[pltpu.SMEM] + [pltpu.VMEM] * len(args) + [pl.ANY] * m,
        scratch=scratch,
    )


def pair_body(scal, keep_ref, recv_ref, *outs):
    core, z = scal[0], scal[1]
    for i in range(4):
        q = lax.rem(z + i, 4)
        own = keep_ref[q]
        other = recv_ref[q].astype(F32)
        early = jnp.where(core == 0, own, other)
        late = jnp.where(core == 0, other, own)
        d_early, d_late = decay_of(early), decay_of(late)
        outs[i][0:STATE, :] = (d_late * early[0:STATE] + late[0:STATE]).astype(BF)
        outs[i][STATE:WROWS, :] = wire_rows(d_early * d_late).astype(BF)


def row_body(scal, r0, r1, r2, r3, total_o, pre_o, dpre_o, box):
    z = scal[1]
    for i, r in enumerate((r0, r1, r2, r3)):
        box[lax.rem(z - i + 4, 4)] = r[...].astype(F32)
    state = jnp.zeros((STATE, CHUNK), F32)
    decay = jnp.ones((1, CHUNK), F32)
    for k in range(4):
        pre_o[k] = state
        dpre_o[k] = jnp.broadcast_to(decay, (8, CHUNK))
        v = box[k]
        d = decay_of(v)
        state = d * state + v[0:STATE]
        decay = decay * d
    total_o[0:STATE, :] = state.astype(BF)
    total_o[STATE:WROWS, :] = wire_rows(decay).astype(BF)


def plane_body(scal, r0, r1, r2, r3, pre_ref, dpre_ref, o0, o1, o2, o3, box):
    z, y = scal[1], scal[2]
    for i, r in enumerate((r0, r1, r2, r3)):
        box[lax.rem(y - i + 4, 4)] = r[...].astype(F32)
    state = jnp.zeros((STATE, CHUNK), F32)
    for k in range(3):
        v = box[k]
        state = jnp.where(k < y, decay_of(v) * state + v[0:STATE], state)
    for i, o in enumerate((o0, o1, o2, o3)):
        q = lax.rem(z + i, 4)
        d = dpre_ref[q]
        o[...] = (pre_ref[q] + d[0:1] * state).astype(BF)


def spread_body(scal, r0, r1, r2, r3, keep_ref, recv_ref, send_o, stay_o, box):
    core, z = scal[0], scal[1]
    for i, r in enumerate((r0, r1, r2, r3)):
        box[lax.rem(z - i + 4, 4)] = r[...].astype(F32)
    for q in range(4):
        early = jnp.where(core == 0, keep_ref[q], recv_ref[q].astype(F32))
        a = box[q]
        b = decay_of(early) * a + early[0:STATE]
        send_o[q] = jnp.where(core == 0, b, a).astype(BF)
        stay_o[q] = jnp.where(core == 0, a, b).astype(BF)


def mix_body(first_chunk, chunks, xc_ref, c_ref, sc_ref, z_ref, m2_ref, tl_ref, te_ref, td_ref, dec_ref, pst_ref,
             ds_ref, after_ref, yg_o, g2_o, ex, ee):
    left = iota((SPAN, SPAN), 1) < HD

    def expand(k):
        j = first_chunk + k
        ex[k % 2] = dot(tl_ref[...], onehot(j * HPC, HPC * SPAN, SPAN))
        ee[k % 2, :, 0:CHUNK] = dot(te_ref[...], onehot(j * HPC, CHUNK, HD, 0, 64))
        ee[k % 2, :, CHUNK:] = dot(te_ref[...], onehot(j * HPC, CHUNK, HD, 64, 128))

    expand(0)
    for k in range(chunks):
        j = first_chunk + k
        lanes = pl.ds(j * CHUNK, CHUNK)
        mine = pl.ds(k * CHUNK, CHUNK)
        if k + 1 < chunks:
            expand(k + 1)
        skip = dot(td_ref[...], onehot(j * HPC, CHUNK, HD))[0:1]
        fix = ds_ref[:, lanes]
        for c in range(NB):
            rows = pl.ds(c * SPAN, SPAN)
            s = sc_ref[c]
            x = xc_ref[rows, lanes]
            parts = []
            for h in range(HPC):
                m2 = m2_ref[j, h : h + 1, c * SPAN : (c + 1) * SPAN]
                e = ex[k % 2, rows, h * SPAN : (h + 1) * SPAN] + m2
                parts.append((s * jnp.exp2(jnp.minimum(e, 8.0))).astype(BF))
            ys = []
            for p in range(HPC // 2):
                xp = x[:, p * SPAN : (p + 1) * SPAN].astype(F32)
                rhs = jnp.concatenate([jnp.where(left, xp, 0.0), jnp.where(left, 0.0, xp)], axis=0).astype(BF)
                ys.append(dot(jnp.concatenate([parts[2 * p], parts[2 * p + 1]], axis=1), rhs))
            y = jnp.concatenate(ys, axis=1) + skip * x.astype(F32)
            if c > 0:
                if c > 1:
                    fix = dec_ref[c - 1 : c, lanes] * fix
                ent = (pst_ref[c - 1, :, lanes] + fix).astype(BF)
                y = y + ee[k % 2, rows, 0:CHUNK] * dot(c_ref[rows, :], ent)
            gate = silu(z_ref[rows, lanes].astype(F32))
            yg_o[rows, mine] = (y * gate).astype(BF)
            g2_o[rows, mine] = (ee[k % 2, rows, CHUNK:] * gate).astype(BF)


def mix_call(first_chunk, chunks, *args):
    return call(
        functools.partial(mix_body, first_chunk, chunks),
        "mix",
        args,
        [((TOK, chunks * CHUNK), BF)] * 2,
        spaces=[pltpu.VMEM] * (len(args) - 1) + [pl.ANY],
        scratch=[pltpu.VMEM((2, TOK, HPC * SPAN), F32), pltpu.VMEM((2, TOK, 2 * CHUNK), F32)],
        cost=(chunks * 25 * 10**7, chunks << 20, chunks * 6 * 10**5),
    )


def gate_body(splits, base, scal, *refs):
    n = len(splits)
    ygs, g2s = refs[:n], refs[n : 2 * n]
    c_ref, stay_ref, recv_ref, gain_ref, after_ref, n_o, inv_o, ce = refs[2 * n :]
    core = scal[0]
    place = [(p, k) for p, s in enumerate(splits) for k in range(s)]
    sums = [None, None]

    def carry(j):
        v = jnp.where(core == j // 4, stay_ref[j % 4].astype(F32), recv_ref[j % 4].astype(F32))
        ce[j % 2] = dot(c_ref[pl.ds(base, HALF), :], v.astype(BF))

    carry(0)
    for j in range(NCH):
        lanes = pl.ds(j * CHUNK, CHUNK)
        p, k = place[j]
        mine = pl.ds(k * CHUNK, CHUNK)
        if j + 1 < NCH:
            carry(j + 1)
        gain = gain_ref[:, lanes]
        for c in range(2):
            rows = pl.ds(c * SPAN, SPAN)
            here = pl.ds(base + c * SPAN, SPAN)
            g = ygs[p][here, mine].astype(F32) + ce[j % 2, rows, :] * g2s[p][here, mine].astype(F32)
            sq = g * g
            sq = sq[:, :128] + sq[:, 128:]
            sums[c] = sq if j == 0 else sums[c] + sq
            n_o[rows, lanes] = (g * gain).astype(BF)
    for c in range(2):
        m = jnp.sum(sums[c], axis=1, keepdims=True) * (1.0 / INNER)
        inv_o[pl.ds(c * SPAN, SPAN), :] = jnp.broadcast_to(lax.rsqrt(m + 1e-05), (SPAN, 128))


def gate_call(splits, base, scal, ygs, g2s, cm, stay, recv, gain, after):
    return call(
        functools.partial(gate_body, splits, base),
        "gate",
        (scal, *ygs, *g2s, cm, stay, recv, gain, after),
        [((HALF, INNER), BF), ((HALF, 128), F32)],
        spaces=[pltpu.SMEM] + [pltpu.VMEM] * (2 * len(ygs) + 4) + [pl.ANY],
        scratch=[pltpu.VMEM((2, HALF, CHUNK), F32)],
        cost=(25 * 10**7, 4 << 20, 0),
    )


def proj_body(shift, halves, scal, *refs):
    ns, w_ref, r_o, l_o = refs[: 2 * halves], refs[2 * halves], refs[2 * halves + 1], refs[2 * halves + 2]
    base = lax.rem(scal[3] + shift, 4) * QOUT
    for k in range(QOUT // CHUNK):
        w = w_ref[:, pl.ds(pl.multiple_of(base + k * CHUNK, CHUNK), CHUNK)]
        o = (r_o, l_o)[k // 2]
        for h in range(halves):
            y = dot(ns[2 * h][...], w) * ns[2 * h + 1][:, 0:1]
            o[pl.ds((k % 2) * CHUNK, CHUNK), pl.ds(h * HALF, HALF)] = jnp.transpose(y).astype(BF)


def proj_call(shift, scal, parts, w):
    halves = len(parts) // 2
    return call(
        functools.partial(proj_body, shift, halves),
        "proj",
        (scal, *parts, w),
        [((QOUT // 2, halves * HALF), BF)] * 2,
        spaces=[pltpu.SMEM],
        cost=(2 * HALF * halves * INNER * QOUT, 7 << 20, 0),
    )


def relay_body(mine, a, b, o):
    o[:, 0:HALF] = (mine[:, 0:HALF].astype(F32) + a[...].astype(F32)).astype(BF)
    o[:, HALF:] = (mine[:, HALF:].astype(F32) + b[...].astype(F32)).astype(BF)


def last_body(own_r, own_l, near_r, near_l, sum_r, sum_l, o):
    for k, refs in enumerate(((own_r, near_r, sum_r), (own_l, near_l, sum_l))):
        s = refs[0][...].astype(F32) + refs[1][...].astype(F32) + refs[2][...].astype(F32)
        o[pl.ds(k * (QOUT // 2), QOUT // 2), :] = s.astype(BF)


def seq_perm(v, dy, dz, flip):
    pairs = []
    for src in range(32):
        y, z, c = src // 8, (src // 2) % 4, src % 2
        dst = (((y + dy) % 4) * 4 + (z + dz) % 4) * 2 + (1 - c if flip else c)
        pairs.append((src, dst))
    return lax.ppermute(v, "seq", pairs)


def head_perm(v, shift):
    return lax.ppermute(v, "head", [(s, (s + shift) % 4) for s in range(4)])


def on_device(x_in, bc_in, z_in, dt_raw, a_log, conv_x, conv_bc, d_skip, norm_gain, out_weight):
    bc = bc_in.reshape(TOK, 256)
    hbm = lambda v: pltpu.with_memory_space_constraint(v, pltpu.HBM)
    edge = call(
        edge_body,
        "edge",
        (hbm(x_in), hbm(bc)),
        [((8, INNER + 256), BF)],
        spaces=[pltpu.HBM] * 2,
        scratch=[pltpu.SemaphoreType.DMA((2,))],
    )[0]
    halo = lax.ppermute(edge, "seq", [(s, s + 1) for s in range(31)])
    place = lax.axis_index("seq")
    scal = jnp.stack([place % 2, (place // 2) % 4, place // 8, lax.axis_index("head")]).astype(jnp.int32)
    xc, b, pst, end, dec, L, step, tw0, x0, b0 = first_call(
        hbm(x_in), bc, conv_x, conv_bc, dt_raw, a_log.reshape(1, HEADS)
    )
    xc, b, ds, send, keep = second_call(scal, halo, x0, b0, conv_x, conv_bc, tw0, end, dec, xc, b)
    recv = seq_perm(send, 0, 0, True)
    cm, sc, m2, tl, te, td = table_call(L, step, d_skip.reshape(1, HEADS), halo, bc, conv_bc, b, send)
    piece = jax.ShapeDtypeStruct((WROWS, CHUNK), BF)
    plain = jax.ShapeDtypeStruct((STATE, CHUNK), BF)
    box = pltpu.VMEM((4, WROWS, CHUNK), F32)
    splits = (3, 3, 2)
    work = lambda k, after: mix_call(
        sum(splits[:k]), splits[k], xc, cm, sc, z_in, m2, tl, te, td, dec, pst, ds, after
    )
    q = small_call(pair_body, "pair", scal, (keep, recv), [piece] * 4, (), (cm,))
    yg0, g20 = work(0, q[0])
    rows = [q[0]] + [seq_perm(q[i], 0, i, False) for i in (1, 2, 3)]
    total, pre, dpre = small_call(
        row_body,
        "row",
        scal,
        rows,
        [piece, jax.ShapeDtypeStruct((4, STATE, CHUNK), F32), jax.ShapeDtypeStruct((4, 8, CHUNK), F32)],
        [box],
        (yg0,),
    )
    yg1, g21 = work(1, total)
    cols = [total] + [seq_perm(total, i, 0, False) for i in (1, 2, 3)]
    e = small_call(plane_body, "plane", scal, (*cols, pre, dpre), [plain] * 4, [box], (yg1,))
    yg2, g22 = work(2, e[0])
    back = [e[0]] + [seq_perm(e[i], 0, i, False) for i in (1, 2, 3)]
    half = jax.ShapeDtypeStruct((4, STATE, CHUNK), BF)
    give, stay = small_call(
        spread_body, "spread", scal, (*back, keep, recv), [half] * 2, [pltpu.VMEM((4, STATE, CHUNK), F32)], (yg2,)
    )
    take = seq_perm(give, 0, 0, True)
    gain = norm_gain.reshape(1, INNER)
    gated = lambda base, after: gate_call(
        splits, base, scal, (yg0, yg1, yg2), (g20, g21, g22), cm, stay, take, gain, after
    )
    top = gated(0, take)
    far_ra, far_la = proj_call(2, scal, top, out_weight)
    low = gated(HALF, far_ra)
    far_rb, far_lb = proj_call(2, scal, low, out_weight)
    far = [head_perm(far_ra, 1), head_perm(far_la, -1), head_perm(far_rb, 1), head_perm(far_lb, -1)]
    both = (*top, *low)
    right_r, right_l = proj_call(1, scal, both, out_weight)
    left_r, left_l = proj_call(3, scal, both, out_weight)
    near_l = head_perm(right_l, 1)
    near_r = head_perm(left_r, -1)
    shape = ((QOUT // 2, TOK), BF)
    sum_r = head_perm(call(relay_body, "relay", (right_r, far[0], far[2]), [shape])[0], 1)
    sum_l = head_perm(call(relay_body, "relay", (left_l, far[1], far[3]), [shape])[0], -1)
    own_r, own_l = proj_call(0, scal, both, out_weight)
    return call(last_body, "last", (own_r, own_l, near_r, near_l, sum_r, sum_l), [((QOUT, TOK), BF)])[0]


def solution(mesh):
    placed = (
        P("seq", "head"),
        P("seq", "head", None),
        P("seq", "head"),
        P("head", "seq"),
        P("head"),
        P(None, "head"),
        P(None, "head", None),
        P("head"),
        P("head"),
        P("head", None),
    )
    return jax.shard_map(
        on_device, mesh=mesh, in_specs=placed, out_specs=P("head", "seq"), check_vma=False
    )
```

```python
import functools

import jax
import jax.numpy as jnp
from jax import lax
from jax.experimental import pallas as pl
from jax.experimental.pallas import tpu as pltpu
from jax.sharding import PartitionSpec as P

SPAN = 128
HEADS = 32
HD = 64
STATE = 128
TOK = 512
NB = 4
INNER = 2048
CHUNK = 256
NCH = INNER // CHUNK
HPC = CHUNK // HD
DOUT = 4096
QOUT = 1024
WROWS = 144
LOG2E = 1.4426950408889634
BF = jnp.bfloat16
F32 = jnp.float32
VMEM_LIMIT = 8 << 20


def silu(u):
    half = 0.5 * u
    return half + half * jnp.tanh(half)


def dot(a, b):
    return jnp.dot(a, b, preferred_element_type=F32)


def iota(shape, axis):
    return lax.broadcasted_iota(jnp.int32, shape, axis)


def onehot(first_head, width, lanes, low=0, high=128):
    k = iota((128, width), 0)
    h = first_head + (iota((128, width), 1) // lanes)
    hit = ((k & 31) == h) & (k >= low) & (k < high)
    return jnp.where(hit, 1.0, 0.0).astype(BF)


def split2(v):
    hi = v.astype(BF).astype(F32)
    return hi, (v - hi).astype(BF).astype(F32)


def column(row, n):
    eye = iota((n, n), 0) == iota((n, n), 1)
    return jnp.sum(jnp.where(eye, jnp.broadcast_to(row, (n, n)), 0.0), axis=1, keepdims=True)


def call(body, name, args, outs, spaces=(), scratch=(), cost=(10**6, 1 << 20, 0), aliases=None, limit=VMEM_LIMIT):
    specs = [pl.BlockSpec(memory_space=spaces[k] if k < len(spaces) else pltpu.VMEM) for k in range(len(args))]
    return pl.pallas_call(
        body,
        in_specs=specs,
        out_specs=[pl.BlockSpec(memory_space=pltpu.VMEM)] * len(outs),
        out_shape=[jax.ShapeDtypeStruct(s, d) for s, d in outs],
        scratch_shapes=list(scratch),
        input_output_aliases=aliases or {},
        compiler_params=pltpu.CompilerParams(vmem_limit_bytes=limit),
        cost_estimate=pl.CostEstimate(flops=cost[0], bytes_accessed=cost[1], transcendentals=cost[2]),
        name=name,
    )(*args)


def conv(window, taps, rows):
    u = taps[3] * window[8:]
    for k in range(3):
        u = u + taps[k] * pltpu.roll(window, 3 - k, 0)[8:]
    return silu(u)


def taps_of(ref, lanes):
    return [ref[k : k + 1, lanes] for k in range(4)]


def split3(v):
    hi = v.astype(BF).astype(F32)
    rest = v - hi
    mid = rest.astype(BF).astype(F32)
    return hi, mid, rest - mid


def spot():
    place = lax.axis_index("seq")
    return place & 1, (place >> 1) & 3, place >> 3, lax.axis_index("head")


def edge_body(x_ref, bc_ref, o, sem):
    a = pltpu.make_async_copy(x_ref.at[pl.ds(TOK - 8, 8), :], o.at[:, pl.ds(0, INNER)], sem.at[0])
    b = pltpu.make_async_copy(bc_ref.at[pl.ds(TOK - 8, 8), :], o.at[:, pl.ds(INNER, 256)], sem.at[1])
    a.start()
    b.start()
    a.wait()
    b.wait()


def first_body(x_hbm, bv, cwx, cwb, dtv, alv,
               xc_o, b_o, pst_o, end_o, dec_o, L_o, step_o, tw0_o, x0_o, b0_o,
               xv, wbuf, tw, bts, xw, sem):
    copies = []
    for j in range(NCH):
        lanes = pl.ds(j * CHUNK, CHUNK)
        copies.append(pltpu.make_async_copy(x_hbm.at[:, lanes], xv.at[:, lanes], sem.at[j]))
        copies[j].start()
    tri = jnp.where(iota((SPAN, SPAN), 0) <= iota((SPAN, SPAN), 1), 1.0, 0.0).astype(BF)
    v = dtv[...].astype(F32)
    t = jnp.exp(-jnp.abs(v))
    u = 1.0 + t
    d = u - 1.0
    flat = d == 0.0
    step = jnp.maximum(v, 0.0) + jnp.where(flat, t, jnp.log(u) * t / jnp.where(flat, 1.0, d))
    step_o[...] = step
    a = column(alv[...], HEADS)
    rate = jnp.concatenate(split3((-LOG2E * jnp.exp(a)) * step), axis=0).astype(BF)
    Ls, ends = [], []
    for c in range(NB):
        s = dot(rate[:, c * SPAN : (c + 1) * SPAN], tri)
        s = s[0:HEADS] + s[HEADS : 2 * HEADS] + s[2 * HEADS : 3 * HEADS]
        Ls.append(s)
        ends.append(jnp.broadcast_to(s[:, SPAN - 1 : SPAN], (HEADS, SPAN)))
    L = jnp.concatenate(Ls, axis=1)
    end = jnp.concatenate(ends, axis=1)
    L_o[...] = L
    w_hi, w_lo = split2(jnp.exp2(end - L) * step)
    d_hi, d_lo = split2(jnp.exp2(end))
    twt = jnp.transpose(jnp.concatenate([w_hi, w_lo, d_hi, d_lo], axis=0))
    tw[...] = twt.astype(BF)
    tw0_o[...] = twt[0:16].astype(BF)
    tw[pl.ds(0, 16), :] = jnp.zeros((16, 128), BF)
    rows = [twt[c * SPAN : c * SPAN + 1] for c in range(NB)]
    dtab = jnp.concatenate(rows + [jnp.zeros((12, SPAN), F32)], axis=0).astype(BF)
    wbuf[0] = dot(tw[...], onehot(0, CHUNK, HD, 0, 64))

    b0_o[...] = bv[0:16, :STATE]
    btaps = [cwb[k][:, :STATE] for k in range(4)]
    nothing = jnp.zeros((8, STATE), F32)
    for c in range(NB):
        if c == 0:
            window = jnp.concatenate([nothing, bv[0:SPAN, :STATE].astype(F32)], axis=0)
        else:
            window = bv[pl.ds(c * SPAN - 8, SPAN + 8), :STATE].astype(F32)
        v = conv(window, btaps, SPAN)
        b_o[pl.ds(c * SPAN, SPAN), :] = v.astype(BF)
        bts[c] = jnp.transpose(v).astype(BF)
    decs = [None] * (NCH + 1)
    for j in range(NCH + 1):
        lanes = pl.ds(j * CHUNK, CHUNK)
        if j < NCH:
            if j + 1 < NCH:
                wbuf[(j + 1) % 2] = dot(tw[...], onehot((j + 1) * HPC, CHUNK, HD, 0, 64))
            dec_o[:, lanes] = dot(dtab, onehot(j * HPC, CHUNK, HD, 64, 128))
            copies[j].wait()
            x0_o[:, lanes] = xv[0:16, lanes]
        state = None
        for c in range(NB):
            if j < NCH:
                for r in (0, 64):
                    for l in (0, 128):
                        row = c * SPAN + r
                        part = pl.ds(j * CHUNK + l, 128)
                        if row == 0:
                            window = jnp.concatenate([nothing, xv[0:64, part].astype(F32)], axis=0)
                        else:
                            window = xv[pl.ds(row - 8, 72), part].astype(F32)
                        v = conv(window, taps_of(cwx, part), 64).astype(BF)
                        xc_o[pl.ds(row, 64), part] = v
                        w = wbuf[j % 2, pl.ds(row, 64), l : l + 128]
                        xw[j % 2, pl.ds(row, 64), l : l + 128] = (v.astype(F32) * w).astype(BF)
            if j > 0:
                before = pl.ds((j - 1) * CHUNK, CHUNK)
                s = dot(bts[c], xw[(j - 1) % 2, pl.ds(c * SPAN, SPAN), :])
                state = s if c == 0 else dec_o[c : c + 1, before] * state + s
                if c < NB - 1:
                    pst_o[c, :, before] = state
                else:
                    end_o[:, before] = state


def first_call(x, bc, cwx, cwb, dt, al):
    return call(
        first_body,
        "first",
        (x, bc, cwx, cwb, dt, al),
        [
            ((TOK, INNER), BF),
            ((TOK, STATE), BF),
            ((NB - 1, STATE, INNER), F32),
            ((STATE, INNER), F32),
            ((16, INNER), F32),
            ((HEADS, TOK), F32),
            ((HEADS, TOK), F32),
            ((16, 128), BF),
            ((16, INNER), BF),
            ((16, STATE), BF),
        ],
        spaces=[pltpu.HBM],
        scratch=[
            pltpu.VMEM((TOK, INNER), BF),
            pltpu.VMEM((2, TOK, CHUNK), F32),
            pltpu.VMEM((TOK, 128), BF),
            pltpu.VMEM((NB, STATE, SPAN), BF),
            pltpu.VMEM((2, TOK, CHUNK), BF),
            pltpu.SemaphoreType.DMA((NCH,)),
        ],
        cost=(10**9, 4 << 20, 10**6),
        limit=12 << 20,
    )


def wire_rows(decay):
    hi, lo = split2(decay)
    return jnp.concatenate([hi, lo, jnp.zeros((14, decay.shape[1]), F32)], axis=0)


def second_body(h_ref, x0_ref, b0_ref, cwx_ref, cwb_ref, tw0_ref, end_ref, dec_ref, xc_in, b_in,
                xc_o, b_o, ds_o, send_o, keep_o, buf):
    v = jnp.concatenate([h_ref[:, INNER : INNER + STATE].astype(F32), b0_ref[...].astype(F32)], axis=0)
    v = conv(v, [cwb_ref[k][:, :STATE] for k in range(4)], 16)
    b_o[0:16, :] = v.astype(BF)
    bt = jnp.transpose(jnp.concatenate([v, jnp.zeros((SPAN - 16, STATE), F32)], axis=0)).astype(BF)
    buf[pl.ds(0, 8), :] = h_ref[:, :INNER].astype(F32)
    buf[pl.ds(8, 16), :] = x0_ref[...].astype(F32)
    for j in range(NCH):
        lanes = pl.ds(j * CHUNK, CHUNK)
        u = conv(buf[:, lanes], taps_of(cwx_ref, lanes), 16).astype(BF)
        xc_o[0:16, lanes] = u
        w = dot(tw0_ref[...], onehot(j * HPC, CHUNK, HD, 0, 64))
        xw = jnp.concatenate([u.astype(F32) * w, jnp.zeros((SPAN - 16, CHUNK), F32)], axis=0).astype(BF)
        ds_o[:, lanes] = dot(bt, xw)
    core = spot()[0]
    for slot in range(2):
        for q in range(4):
            half = core if slot else 1 - core
            lanes = pl.ds(pl.multiple_of((half * 4 + q) * CHUNK, CHUNK), CHUNK)
            dec = dec_ref[0:8, lanes]
            after = dec[1:2] * dec[2:3] * dec[3:4]
            state = end_ref[:, lanes] + after * ds_o[:, lanes]
            decay = dec[0:1] * after
            if slot:
                keep_o[q, 0:STATE, :] = state
                keep_o[q, STATE:WROWS, :] = jnp.concatenate([decay, jnp.zeros((15, CHUNK), F32)], axis=0)
            else:
                send_o[q, 0:STATE, :] = state.astype(BF)
                send_o[q, STATE:WROWS, :] = wire_rows(decay).astype(BF)


def second_call(halo, x0, b0, cwx, cwb, tw0, end, dec, xc, b):
    return call(
        second_body,
        "second",
        (halo, x0, b0, cwx, cwb, tw0, end, dec, xc, b),
        [
            ((TOK, INNER), BF),
            ((TOK, STATE), BF),
            ((STATE, INNER), F32),
            ((4, WROWS, CHUNK), BF),
            ((4, WROWS, CHUNK), F32),
        ],
        scratch=[pltpu.VMEM((24, INNER), F32)],
        aliases={8: 0, 9: 1},
        cost=(10**8, 2 << 20, 10**5),
    )


def table_body(L_ref, step_ref, ds_ref, h_ref, bc_ref, cwb_ref, b_ref, after_ref,
               c_o, sc_o, m2_o, tl_o, te_o, td_o, buf):
    L = L_ref[...]
    M = jnp.log(step_ref[...]) * LOG2E - L
    for j in range(NCH):
        m2_o[j, 0:HPC, :] = M[j * HPC : (j + 1) * HPC, :]
    zero = jnp.zeros((HEADS, TOK), F32)
    tl_o[...] = jnp.transpose(jnp.concatenate([*split3(L), zero], axis=0)).astype(BF)
    parts, before = [], jnp.zeros((HEADS, SPAN), F32)
    for c in range(NB):
        s = L[:, c * SPAN : (c + 1) * SPAN]
        parts.append(before + s)
        before = before + jnp.broadcast_to(s[:, SPAN - 1 : SPAN], (HEADS, SPAN))
    e = [*split2(jnp.exp2(L)), *split2(jnp.exp2(jnp.concatenate(parts, axis=1)))]
    te_o[...] = jnp.transpose(jnp.concatenate(e, axis=0)).astype(BF)
    d = [jnp.broadcast_to(p, (HEADS, SPAN)) for p in split2(column(ds_ref[...], HEADS))]
    d = jnp.concatenate([*d, jnp.zeros((2 * HEADS, SPAN), F32)], axis=0)
    td_o[...] = jnp.transpose(d)[0:16].astype(BF)
    buf[pl.ds(0, 8), :] = h_ref[:, INNER + STATE :].astype(F32)
    buf[pl.ds(8, TOK), :] = bc_ref[:, STATE:].astype(F32)
    taps = [cwb_ref[k][:, STATE:] for k in range(4)]
    causal = iota((SPAN, SPAN), 0) >= iota((SPAN, SPAN), 1)
    for c in range(NB):
        rows = pl.ds(c * SPAN, SPAN)
        v = conv(buf[pl.ds(c * SPAN, SPAN + 8), :], taps, SPAN).astype(BF)
        c_o[rows, :] = v
        s = lax.dot_general(v, b_ref[rows, :], (((1,), (1,)), ((), ())), preferred_element_type=F32)
        sc_o[c] = jnp.where(causal, s, 0.0)


def table_call(L, step, ds, halo, bc, cwb, b, after):
    return call(
        table_body,
        "table",
        (L, step, ds, halo, bc, cwb, b, after),
        [
            ((TOK, STATE), BF),
            ((NB, SPAN, SPAN), F32),
            ((NCH, 8, TOK), F32),
            ((TOK, 128), BF),
            ((TOK, 128), BF),
            ((16, 128), BF),
        ],
        spaces=[pltpu.VMEM] * 7 + [pl.ANY],
        scratch=[pltpu.VMEM((TOK + 8, STATE), F32)],
        cost=(10**8, 2 << 20, 10**5),
    )


def decay_of(v):
    return v[STATE : STATE + 1] + v[STATE + 1 : STATE + 2]


def small_call(body, name, args, outs, scratch=(), after=()):
    n = len(args)
    m = len(after)

    def run(*refs):
        body(*refs[:n], *refs[n + m :])

    return call(
        run,
        name,
        (*args, *after),
        [(o.shape, o.dtype) for o in outs],
        spaces=[pltpu.VMEM] * n + [pl.ANY] * m,
        scratch=scratch,
    )


def pair_body(keep_ref, recv_ref, *outs):
    core, z = spot()[:2]
    for i in range(4):
        q = lax.rem(z + i, 4)
        own = keep_ref[q]
        other = recv_ref[q].astype(F32)
        early = jnp.where(core == 0, own, other)
        late = jnp.where(core == 0, other, own)
        d_early, d_late = decay_of(early), decay_of(late)
        outs[i][0:STATE, :] = (d_late * early[0:STATE] + late[0:STATE]).astype(BF)
        outs[i][STATE:WROWS, :] = wire_rows(d_early * d_late).astype(BF)


def row_body(r0, r1, r2, r3, total_o, pre_o, dpre_o, box):
    z = spot()[1]
    for i, r in enumerate((r0, r1, r2, r3)):
        box[lax.rem(z - i + 4, 4)] = r[...].astype(F32)
    state = jnp.zeros((STATE, CHUNK), F32)
    decay = jnp.ones((1, CHUNK), F32)
    for k in range(4):
        pre_o[k] = state
        dpre_o[k] = jnp.broadcast_to(decay, (8, CHUNK))
        v = box[k]
        d = decay_of(v)
        state = d * state + v[0:STATE]
        decay = decay * d
    total_o[0:STATE, :] = state.astype(BF)
    total_o[STATE:WROWS, :] = wire_rows(decay).astype(BF)


def plane_body(r0, r1, r2, r3, pre_ref, dpre_ref, o0, o1, o2, o3, box):
    z, y = spot()[1:3]
    for i, r in enumerate((r0, r1, r2, r3)):
        box[lax.rem(y - i + 4, 4)] = r[...].astype(F32)
    state = jnp.zeros((STATE, CHUNK), F32)
    for k in range(3):
        v = box[k]
        state = jnp.where(k < y, decay_of(v) * state + v[0:STATE], state)
    for i, o in enumerate((o0, o1, o2, o3)):
        q = lax.rem(z + i, 4)
        d = dpre_ref[q]
        o[...] = (pre_ref[q] + d[0:1] * state).astype(BF)


def spread_body(r0, r1, r2, r3, keep_ref, recv_ref, send_o, stay_o, box):
    core, z = spot()[:2]
    for i, r in enumerate((r0, r1, r2, r3)):
        box[lax.rem(z - i + 4, 4)] = r[...].astype(F32)
    for q in range(4):
        early = jnp.where(core == 0, keep_ref[q], recv_ref[q].astype(F32))
        a = box[q]
        b = decay_of(early) * a + early[0:STATE]
        send_o[q] = jnp.where(core == 0, b, a).astype(BF)
        stay_o[q] = jnp.where(core == 0, a, b).astype(BF)


def mix_body(first_chunk, chunks, xc_ref, c_ref, sc_ref, z_ref, m2_ref, tl_ref, te_ref, td_ref, dec_ref, pst_ref,
             ds_ref, *rest):
    yg_o, g2_o, ex, ee = rest[-4:]
    left = iota((SPAN, SPAN), 1) < HD

    def expand(k):
        j = first_chunk + k
        ex[k % 2] = dot(tl_ref[...], onehot(j * HPC, HPC * SPAN, SPAN))
        ee[k % 2, :, 0:CHUNK] = dot(te_ref[...], onehot(j * HPC, CHUNK, HD, 0, 64))
        ee[k % 2, :, CHUNK:] = dot(te_ref[...], onehot(j * HPC, CHUNK, HD, 64, 128))

    expand(0)
    for k in range(chunks):
        j = first_chunk + k
        lanes = pl.ds(j * CHUNK, CHUNK)
        if k + 1 < chunks:
            expand(k + 1)
        skip = dot(td_ref[...], onehot(j * HPC, CHUNK, HD))[0:1]
        fix = ds_ref[:, lanes]
        for c in range(NB):
            rows = pl.ds(c * SPAN, SPAN)
            s = sc_ref[c]
            x = xc_ref[rows, lanes]
            parts = []
            for h in range(HPC):
                m2 = m2_ref[j, h : h + 1, c * SPAN : (c + 1) * SPAN]
                e = ex[k % 2, rows, h * SPAN : (h + 1) * SPAN] + m2
                parts.append((s * jnp.exp2(jnp.minimum(e, 8.0))).astype(BF))
            ys = []
            for p in range(HPC // 2):
                xp = x[:, p * SPAN : (p + 1) * SPAN].astype(F32)
                rhs = jnp.concatenate([jnp.where(left, xp, 0.0), jnp.where(left, 0.0, xp)], axis=0).astype(BF)
                ys.append(dot(jnp.concatenate([parts[2 * p], parts[2 * p + 1]], axis=1), rhs))
            y = jnp.concatenate(ys, axis=1) + skip * x.astype(F32)
            if c > 0:
                if c > 1:
                    fix = dec_ref[c - 1 : c, lanes] * fix
                ent = (pst_ref[c - 1, :, lanes] + fix).astype(BF)
                y = y + ee[k % 2, rows, 0:CHUNK] * dot(c_ref[rows, :], ent)
            gate = silu(z_ref[rows, lanes].astype(F32))
            yg_o[rows, lanes] = (y * gate).astype(BF)
            g2_o[rows, lanes] = (ee[k % 2, rows, CHUNK:] * gate).astype(BF)


def mix_call(first_chunk, chunks, args, after, before):
    n = len(args)
    return call(
        functools.partial(mix_body, first_chunk, chunks),
        "mix",
        (*args, after, *before),
        [((TOK, INNER), BF)] * 2,
        spaces=[pltpu.VMEM] * n + [pl.ANY],
        scratch=[pltpu.VMEM((2, TOK, HPC * SPAN), F32), pltpu.VMEM((2, TOK, 2 * CHUNK), F32)],
        aliases={n + 1: 0, n + 2: 1} if before else None,
        cost=(chunks * 25 * 10**7, chunks << 20, chunks * 6 * 10**5),
    )


def gated(yg_ref, g2_ref, c_ref, e_ref, gain_ref, half, blocks, n_o, ce, sums):
    at = lambda q: pl.ds(pl.multiple_of(half * (INNER // 2) + q * CHUNK, CHUNK), CHUNK)

    def carry(q):
        ce[q % 2] = dot(c_ref[...], e_ref[q])

    carry(0)
    for q in range(4):
        lanes = at(q)
        if q < 3:
            carry(q + 1)
        gain = gain_ref[:, lanes]
        for c in range(blocks):
            rows = pl.ds(c * SPAN, SPAN)
            g = yg_ref[rows, lanes].astype(F32) + ce[q % 2, rows, :] * g2_ref[rows, lanes].astype(F32)
            sq = g * g
            sq = sq[:, :128] + sq[:, 128:]
            sums[c] = sq if sums[c] is None else sums[c] + sq
            n_o[rows, q * CHUNK : (q + 1) * CHUNK] = (g * gain).astype(BF)


def near_gate_body(yg_ref, g2_ref, c_ref, e_ref, gain_ref, after_ref, n_o, ss_o, ce):
    sums = [None] * NB
    gated(yg_ref, g2_ref, c_ref, e_ref, gain_ref, spot()[0], NB, n_o, ce, sums)
    for c in range(NB):
        ss_o[pl.ds(c * SPAN, SPAN), :] = sums[c]


def far_gate_body(yg_ref, g2_ref, c_ref, e_ref, gain_ref, ss_ref, after_ref, n_o, inv_o, ce):
    sums = [ss_ref[pl.ds(c * SPAN, SPAN), :] for c in range(NB)]
    gated(yg_ref, g2_ref, c_ref, e_ref, gain_ref, 1 - spot()[0], NB, n_o, ce, sums)
    for c in range(NB):
        m = jnp.sum(sums[c], axis=1, keepdims=True) * (1.0 / INNER)
        inv_o[pl.ds(c * SPAN, SPAN), :] = jnp.broadcast_to(lax.rsqrt(m + 1e-05), (SPAN, 128))


def near_gate_call(yg, g2, cm, e, gain, after):
    return call(
        near_gate_body,
        "gate",
        (yg, g2, cm, e, gain, after),
        [((TOK, INNER // 2), BF), ((TOK, 128), F32)],
        spaces=[pltpu.VMEM] * 5 + [pl.ANY],
        scratch=[pltpu.VMEM((2, TOK, CHUNK), F32)],
        cost=(25 * 10**7, 4 << 20, 0),
    )


def far_gate_call(yg, g2, cm, e, gain, ss, after):
    return call(
        far_gate_body,
        "gate",
        (yg, g2, cm, e, gain, ss, after),
        [((TOK, INNER // 2), BF), ((TOK, 128), F32)],
        spaces=[pltpu.VMEM] * 6 + [pl.ANY],
        scratch=[pltpu.VMEM((2, TOK, CHUNK), F32)],
        cost=(25 * 10**7, 4 << 20, 0),
    )


def weight_block(w_ref, half, shift, k):
    lane = lax.rem(spot()[3] + shift, 4) * QOUT + k * CHUNK
    rows = pl.ds(pl.multiple_of(half * (INNER // 2), INNER // 2), INNER // 2)
    return w_ref[rows, pl.ds(pl.multiple_of(lane, CHUNK), CHUNK)]


def part_body(n_ref, w_ref, after_ref, p_o):
    core = spot()[0]
    for k in range(QOUT // CHUNK):
        p_o[:, k * CHUNK : (k + 1) * CHUNK] = dot(n_ref[...], weight_block(w_ref, core, 2, k))


def far_body(p_ref, n_ref, inv_ref, w_ref, r_o, l_o):
    core = spot()[0]
    for k in range(QOUT // CHUNK):
        y = p_ref[:, k * CHUNK : (k + 1) * CHUNK] + dot(n_ref[...], weight_block(w_ref, 1 - core, 2, k))
        o = (r_o, l_o)[k // 2]
        o[pl.ds((k % 2) * CHUNK, CHUNK), :] = jnp.transpose(y * inv_ref[:, 0:1]).astype(BF)


def proj_body(shift, first, count, near_ref, n_ref, inv_ref, w_ref, after_ref, o):
    core = spot()[0]
    for k in range(count):
        y = dot(near_ref[...], weight_block(w_ref, core, shift, first + k))
        y = y + dot(n_ref[...], weight_block(w_ref, 1 - core, shift, first + k))
        o[pl.ds(k * CHUNK, CHUNK), :] = jnp.transpose(y * inv_ref[:, 0:1]).astype(BF)


def part_call(near, w, after):
    return call(
        part_body,
        "part",
        (near, w, after),
        [((TOK, QOUT), F32)],
        spaces=[pltpu.VMEM] * 2 + [pl.ANY],
        cost=(TOK * INNER * QOUT, 5 << 20, 0),
    )[0]


def far_call(p, n, inv, w):
    return call(
        far_body,
        "far",
        (p, n, inv, w),
        [((QOUT // 2, TOK), BF)] * 2,
        cost=(TOK * INNER * QOUT, 5 << 20, 0),
    )


def proj_call(shift, side, near, n, inv, w, after):
    count = 2 if side < 2 else 4
    return call(
        functools.partial(proj_body, shift, 2 * side if side < 2 else 0, count),
        "proj",
        (near, n, inv, w, after),
        [((count * CHUNK, TOK), BF)],
        spaces=[pltpu.VMEM] * 4 + [pl.ANY],
        cost=(2 * TOK * INNER * count * CHUNK, 5 << 20, 0),
    )[0]


def relay_body(mine, a, o):
    o[...] = (mine[...].astype(F32) + a[...].astype(F32)).astype(BF)


def last_body(own, near_r, near_l, sum_r, sum_l, o_hbm, o, sem):
    copies = []
    for k in range(4):
        rows = pl.ds(k * CHUNK, CHUNK)
        side = pl.ds((k % 2) * CHUNK, CHUNK)
        near, total = ((near_r, sum_r), (near_l, sum_l))[k // 2]
        s = own[rows, :].astype(F32) + near[side, :].astype(F32) + total[side, :].astype(F32)
        o[rows, :] = s.astype(BF)
        copies.append(pltpu.make_async_copy(o.at[rows, :], o_hbm.at[rows, :], sem.at[k]))
        copies[k].start()
    for c in copies:
        c.wait()


def last_call(*args):
    return pl.pallas_call(
        last_body,
        in_specs=[pl.BlockSpec(memory_space=pltpu.VMEM)] * len(args),
        out_specs=pl.BlockSpec(memory_space=pltpu.HBM),
        out_shape=jax.ShapeDtypeStruct((QOUT, TOK), BF),
        scratch_shapes=[pltpu.VMEM((QOUT, TOK), BF), pltpu.SemaphoreType.DMA((4,))],
        compiler_params=pltpu.CompilerParams(vmem_limit_bytes=VMEM_LIMIT),
        name="last",
    )(*args)


def seq_perm(v, dy, dz, flip):
    pairs = []
    for src in range(32):
        y, z, c = src // 8, (src // 2) % 4, src % 2
        dst = (((y + dy) % 4) * 4 + (z + dz) % 4) * 2 + (1 - c if flip else c)
        pairs.append((src, dst))
    return lax.ppermute(v, "seq", pairs)


def head_perm(v, shift):
    return lax.ppermute(v, "head", [(s, (s + shift) % 4) for s in range(4)])


def on_device(x_in, bc_in, z_in, dt_raw, a_log, conv_x, conv_bc, d_skip, norm_gain, out_weight):
    bc = bc_in.reshape(TOK, 256)
    hbm = lambda v: pltpu.with_memory_space_constraint(v, pltpu.HBM)
    edge = call(
        edge_body,
        "edge",
        (hbm(x_in), hbm(bc)),
        [((8, INNER + 256), BF)],
        spaces=[pltpu.HBM] * 2,
        scratch=[pltpu.SemaphoreType.DMA((2,))],
    )[0]
    halo = lax.ppermute(edge, "seq", [(s, s + 1) for s in range(31)])
    xc, b, pst, end, dec, L, step, tw0, x0, b0 = first_call(
        hbm(x_in), bc, conv_x, conv_bc, dt_raw, a_log.reshape(1, HEADS)
    )
    xc, b, ds, send, keep = second_call(halo, x0, b0, conv_x, conv_bc, tw0, end, dec, xc, b)
    recv = seq_perm(send, 0, 0, True)
    cm, sc, m2, tl, te, td = table_call(L, step, d_skip.reshape(1, HEADS), halo, bc, conv_bc, b, send)
    piece = jax.ShapeDtypeStruct((WROWS, CHUNK), BF)
    plain = jax.ShapeDtypeStruct((STATE, CHUNK), BF)
    box = pltpu.VMEM((4, WROWS, CHUNK), F32)
    splits = (3, 3, 2)
    known = (xc, cm, sc, z_in, m2, tl, te, td, dec, pst, ds)
    work = lambda k, after, before: mix_call(sum(splits[:k]), splits[k], known, after, before)
    q = small_call(pair_body, "pair", (keep, recv), [piece] * 4, (), (cm,))
    mixed = work(0, q[0], ())
    rows = [q[0]] + [seq_perm(q[i], 0, i, False) for i in (1, 2, 3)]
    total, pre, dpre = small_call(
        row_body,
        "row",
        rows,
        [piece, jax.ShapeDtypeStruct((4, STATE, CHUNK), F32), jax.ShapeDtypeStruct((4, 8, CHUNK), F32)],
        [box],
        (mixed[0],),
    )
    mixed = work(1, total, mixed)
    cols = [total] + [seq_perm(total, i, 0, False) for i in (1, 2, 3)]
    e = small_call(plane_body, "plane", (*cols, pre, dpre), [plain] * 4, [box], (mixed[0],))
    mixed = work(2, e[0], mixed)
    back = [e[0]] + [seq_perm(e[i], 0, i, False) for i in (1, 2, 3)]
    half = jax.ShapeDtypeStruct((4, STATE, CHUNK), BF)
    give, stay = small_call(
        spread_body, "spread", (*back, keep, recv), [half] * 2, [pltpu.VMEM((4, STATE, CHUNK), F32)], (mixed[0],)
    )
    take = seq_perm(give, 0, 0, True)
    gain = norm_gain.reshape(1, INNER)
    near, ss = near_gate_call(*mixed, cm, stay, gain, give)
    p = part_call(near, out_weight, ss)
    other, inv = far_gate_call(*mixed, cm, take, gain, ss, p)
    far_r, far_l = far_call(p, other, inv, out_weight)
    from_left, from_right = head_perm(far_r, 1), head_perm(far_l, -1)
    proj = lambda shift, side, after: proj_call(shift, side, near, other, inv, out_weight, after)
    right_l = proj(1, 1, far_r)
    near_l = head_perm(right_l, 1)
    left_r = proj(3, 0, right_l)
    near_r = head_perm(left_r, -1)
    right_r = proj(1, 0, left_r)
    left_l = proj(3, 1, right_r)
    shape = ((QOUT // 2, TOK), BF)
    sum_r = head_perm(call(relay_body, "relay", (right_r, from_left), [shape])[0], 1)
    sum_l = head_perm(call(relay_body, "relay", (left_l, from_right), [shape])[0], -1)
    own = proj(0, 2, left_l)
    return last_call(own, near_r, near_l, sum_r, sum_l)


def solution(mesh):
    placed = (
        P("seq", "head"),
        P("seq", "head", None),
        P("seq", "head"),
        P("head", "seq"),
        P("head"),
        P(None, "head"),
        P(None, "head", None),
        P("head"),
        P("head"),
        P("head", None),
    )
    return jax.shard_map(
        on_device, mesh=mesh, in_specs=placed, out_specs=P("head", "seq"), check_vma=False
    )
```

```python
import functools

import jax
import jax.numpy as jnp
from jax import lax
from jax.experimental import pallas as pl
from jax.experimental.pallas import tpu as pltpu
from jax.sharding import PartitionSpec as P

SPAN = 128
HEADS = 32
HD = 64
STATE = 128
TOK = 512
NB = 4
INNER = 2048
CHUNK = 256
NCH = INNER // CHUNK
HPC = CHUNK // HD
DOUT = 4096
QOUT = 1024
WROWS = 144
LOG2E = 1.4426950408889634
BF = jnp.bfloat16
F32 = jnp.float32
VMEM_LIMIT = 8 << 20


def silu(u):
    half = 0.5 * u
    return half + half * jnp.tanh(half)


def dot(a, b):
    return jnp.dot(a, b, preferred_element_type=F32)


def iota(shape, axis):
    return lax.broadcasted_iota(jnp.int32, shape, axis)


def onehot(first_head, width, lanes, low=0, high=128):
    k = iota((128, width), 0)
    h = first_head + (iota((128, width), 1) // lanes)
    hit = ((k & 31) == h) & (k >= low) & (k < high)
    return jnp.where(hit, 1.0, 0.0).astype(BF)


def split2(v):
    hi = v.astype(BF).astype(F32)
    return hi, (v - hi).astype(BF).astype(F32)


def column(row, n):
    eye = iota((n, n), 0) == iota((n, n), 1)
    return jnp.sum(jnp.where(eye, jnp.broadcast_to(row, (n, n)), 0.0), axis=1, keepdims=True)


def call(body, name, args, outs, spaces=(), scratch=(), cost=(10**6, 1 << 20, 0), aliases=None, limit=VMEM_LIMIT):
    specs = [pl.BlockSpec(memory_space=spaces[k] if k < len(spaces) else pltpu.VMEM) for k in range(len(args))]
    return pl.pallas_call(
        body,
        in_specs=specs,
        out_specs=[pl.BlockSpec(memory_space=pltpu.VMEM)] * len(outs),
        out_shape=[jax.ShapeDtypeStruct(s, d) for s, d in outs],
        scratch_shapes=list(scratch),
        input_output_aliases=aliases or {},
        compiler_params=pltpu.CompilerParams(vmem_limit_bytes=limit),
        cost_estimate=pl.CostEstimate(flops=cost[0], bytes_accessed=cost[1], transcendentals=cost[2]),
        name=name,
    )(*args)


def conv(window, taps, rows):
    u = taps[3] * window[8:]
    for k in range(3):
        u = u + taps[k] * pltpu.roll(window, 3 - k, 0)[8:]
    return silu(u)


def taps_of(ref, lanes):
    return [ref[k : k + 1, lanes] for k in range(4)]


def split3(v):
    hi = v.astype(BF).astype(F32)
    rest = v - hi
    mid = rest.astype(BF).astype(F32)
    return hi, mid, rest - mid


def spot():
    place = lax.axis_index("seq")
    return place & 1, (place >> 1) & 3, place >> 3, lax.axis_index("head")


def edge_body(x_ref, bc_ref, o, sem):
    a = pltpu.make_async_copy(x_ref.at[pl.ds(TOK - 8, 8), :], o.at[:, pl.ds(0, INNER)], sem.at[0])
    b = pltpu.make_async_copy(bc_ref.at[pl.ds(TOK - 8, 8), :], o.at[:, pl.ds(INNER, 256)], sem.at[1])
    a.start()
    b.start()
    a.wait()
    b.wait()


def halo_rows(h_ref, lanes):
    return jnp.where(lax.axis_index("seq") == 0, 0.0, h_ref[:, lanes].astype(F32))


def first_body(x_hbm, bv, cwx, cwb, dtv, alv,
               xc_o, b_o, pst_o, end_o, dec_o, L_o, step_o, tw0_o, x0_o, b0_o,
               xv, wbuf, tw, bts, xw, sem):
    copies = []
    for j in range(NCH):
        lanes = pl.ds(j * CHUNK, CHUNK)
        copies.append(pltpu.make_async_copy(x_hbm.at[:, lanes], xv.at[:, lanes], sem.at[j]))
        copies[j].start()
    tri = jnp.where(iota((SPAN, SPAN), 0) <= iota((SPAN, SPAN), 1), 1.0, 0.0).astype(BF)
    v = dtv[...].astype(F32)
    t = jnp.exp(-jnp.abs(v))
    u = 1.0 + t
    d = u - 1.0
    flat = d == 0.0
    step = jnp.maximum(v, 0.0) + jnp.where(flat, t, jnp.log(u) * t / jnp.where(flat, 1.0, d))
    step_o[...] = step
    a = column(alv[...], HEADS)
    rate = jnp.concatenate(split3((-LOG2E * jnp.exp(a)) * step), axis=0).astype(BF)
    Ls, ends = [], []
    for c in range(NB):
        s = dot(rate[:, c * SPAN : (c + 1) * SPAN], tri)
        s = s[0:HEADS] + s[HEADS : 2 * HEADS] + s[2 * HEADS : 3 * HEADS]
        Ls.append(s)
        ends.append(jnp.broadcast_to(s[:, SPAN - 1 : SPAN], (HEADS, SPAN)))
    L = jnp.concatenate(Ls, axis=1)
    end = jnp.concatenate(ends, axis=1)
    L_o[...] = L
    w_hi, w_lo = split2(jnp.exp2(end - L) * step)
    d_hi, d_lo = split2(jnp.exp2(end))
    twt = jnp.transpose(jnp.concatenate([w_hi, w_lo, d_hi, d_lo], axis=0))
    tw[...] = twt.astype(BF)
    tw0_o[...] = twt[0:16].astype(BF)
    tw[pl.ds(0, 16), :] = jnp.zeros((16, 128), BF)
    rows = [twt[c * SPAN : c * SPAN + 1] for c in range(NB)]
    dtab = jnp.concatenate(rows + [jnp.zeros((12, SPAN), F32)], axis=0).astype(BF)
    wbuf[0] = dot(tw[...], onehot(0, CHUNK, HD, 0, 64))

    b0_o[...] = bv[0:16, :STATE]
    btaps = [cwb[k][:, :STATE] for k in range(4)]
    nothing = jnp.zeros((8, STATE), F32)
    for c in range(NB):
        if c == 0:
            window = jnp.concatenate([nothing, bv[0:SPAN, :STATE].astype(F32)], axis=0)
        else:
            window = bv[pl.ds(c * SPAN - 8, SPAN + 8), :STATE].astype(F32)
        v = conv(window, btaps, SPAN)
        b_o[pl.ds(c * SPAN, SPAN), :] = v.astype(BF)
        bts[c] = jnp.transpose(v).astype(BF)
    decs = [None] * (NCH + 1)
    for j in range(NCH + 1):
        lanes = pl.ds(j * CHUNK, CHUNK)
        if j < NCH:
            if j + 1 < NCH:
                wbuf[(j + 1) % 2] = dot(tw[...], onehot((j + 1) * HPC, CHUNK, HD, 0, 64))
            dec_o[:, lanes] = dot(dtab, onehot(j * HPC, CHUNK, HD, 64, 128))
            copies[j].wait()
            x0_o[:, lanes] = xv[0:16, lanes]
        state = None
        for c in range(NB):
            if j < NCH:
                for r in (0, 64):
                    for l in (0, 128):
                        row = c * SPAN + r
                        part = pl.ds(j * CHUNK + l, 128)
                        if row == 0:
                            window = jnp.concatenate([nothing, xv[0:64, part].astype(F32)], axis=0)
                        else:
                            window = xv[pl.ds(row - 8, 72), part].astype(F32)
                        v = conv(window, taps_of(cwx, part), 64).astype(BF)
                        xc_o[pl.ds(row, 64), part] = v
                        w = wbuf[j % 2, pl.ds(row, 64), l : l + 128]
                        xw[j % 2, pl.ds(row, 64), l : l + 128] = (v.astype(F32) * w).astype(BF)
            if j > 0:
                before = pl.ds((j - 1) * CHUNK, CHUNK)
                s = dot(bts[c], xw[(j - 1) % 2, pl.ds(c * SPAN, SPAN), :])
                state = s if c == 0 else dec_o[c : c + 1, before] * state + s
                if c < NB - 1:
                    pst_o[c, :, before] = state
                else:
                    end_o[:, before] = state


def first_call(x, bc, cwx, cwb, dt, al):
    return call(
        first_body,
        "first",
        (x, bc, cwx, cwb, dt, al),
        [
            ((TOK, INNER), BF),
            ((TOK, STATE), BF),
            ((NB - 1, STATE, INNER), F32),
            ((STATE, INNER), F32),
            ((16, INNER), F32),
            ((HEADS, TOK), F32),
            ((HEADS, TOK), F32),
            ((16, 128), BF),
            ((16, INNER), BF),
            ((16, STATE), BF),
        ],
        spaces=[pltpu.HBM],
        scratch=[
            pltpu.VMEM((TOK, INNER), BF),
            pltpu.VMEM((2, TOK, CHUNK), F32),
            pltpu.VMEM((TOK, 128), BF),
            pltpu.VMEM((NB, STATE, SPAN), BF),
            pltpu.VMEM((2, TOK, CHUNK), BF),
            pltpu.SemaphoreType.DMA((NCH,)),
        ],
        cost=(10**9, 4 << 20, 10**6),
        limit=12 << 20,
    )


def wire_rows(decay):
    hi, lo = split2(decay)
    return jnp.concatenate([hi, lo, jnp.zeros((14, decay.shape[1]), F32)], axis=0)


def second_body(h_ref, x0_ref, b0_ref, cwx_ref, cwb_ref, tw0_ref, end_ref, dec_ref, xc_in, b_in,
                xc_o, b_o, ds_o, send_o, keep_o, buf):
    v = jnp.concatenate([halo_rows(h_ref, pl.ds(INNER, STATE)), b0_ref[...].astype(F32)], axis=0)
    v = conv(v, [cwb_ref[k][:, :STATE] for k in range(4)], 16)
    b_o[0:16, :] = v.astype(BF)
    bt = jnp.transpose(jnp.concatenate([v, jnp.zeros((SPAN - 16, STATE), F32)], axis=0)).astype(BF)
    buf[pl.ds(0, 8), :] = halo_rows(h_ref, pl.ds(0, INNER))
    buf[pl.ds(8, 16), :] = x0_ref[...].astype(F32)
    for j in range(NCH):
        lanes = pl.ds(j * CHUNK, CHUNK)
        u = conv(buf[:, lanes], taps_of(cwx_ref, lanes), 16).astype(BF)
        xc_o[0:16, lanes] = u
        w = dot(tw0_ref[...], onehot(j * HPC, CHUNK, HD, 0, 64))
        xw = jnp.concatenate([u.astype(F32) * w, jnp.zeros((SPAN - 16, CHUNK), F32)], axis=0).astype(BF)
        ds_o[:, lanes] = dot(bt, xw)
    core = spot()[0]
    for slot in range(2):
        for q in range(4):
            half = core if slot else 1 - core
            lanes = pl.ds(pl.multiple_of((half * 4 + q) * CHUNK, CHUNK), CHUNK)
            dec = dec_ref[0:8, lanes]
            after = dec[1:2] * dec[2:3] * dec[3:4]
            state = end_ref[:, lanes] + after * ds_o[:, lanes]
            decay = dec[0:1] * after
            if slot:
                keep_o[q, 0:STATE, :] = state
                keep_o[q, STATE:WROWS, :] = jnp.concatenate([decay, jnp.zeros((15, CHUNK), F32)], axis=0)
            else:
                send_o[q, 0:STATE, :] = state.astype(BF)
                send_o[q, STATE:WROWS, :] = wire_rows(decay).astype(BF)


def second_call(halo, x0, b0, cwx, cwb, tw0, end, dec, xc, b):
    return call(
        second_body,
        "second",
        (halo, x0, b0, cwx, cwb, tw0, end, dec, xc, b),
        [
            ((TOK, INNER), BF),
            ((TOK, STATE), BF),
            ((STATE, INNER), F32),
            ((4, WROWS, CHUNK), BF),
            ((4, WROWS, CHUNK), F32),
        ],
        scratch=[pltpu.VMEM((24, INNER), F32)],
        aliases={8: 0, 9: 1},
        cost=(10**8, 2 << 20, 10**5),
    )


def table_body(L_ref, step_ref, ds_ref, h_ref, bc_ref, cwb_ref, b_ref, after_ref,
               c_o, sc_o, m2_o, tl_o, te_o, td_o, buf):
    L = L_ref[...]
    M = jnp.log(step_ref[...]) * LOG2E - L
    for j in range(NCH):
        m2_o[j, 0:HPC, :] = M[j * HPC : (j + 1) * HPC, :]
    zero = jnp.zeros((HEADS, TOK), F32)
    tl_o[...] = jnp.transpose(jnp.concatenate([*split3(L), zero], axis=0)).astype(BF)
    parts, before = [], jnp.zeros((HEADS, SPAN), F32)
    for c in range(NB):
        s = L[:, c * SPAN : (c + 1) * SPAN]
        parts.append(before + s)
        before = before + jnp.broadcast_to(s[:, SPAN - 1 : SPAN], (HEADS, SPAN))
    e = [*split2(jnp.exp2(L)), *split2(jnp.exp2(jnp.concatenate(parts, axis=1)))]
    te_o[...] = jnp.transpose(jnp.concatenate(e, axis=0)).astype(BF)
    d = [jnp.broadcast_to(p, (HEADS, SPAN)) for p in split2(column(ds_ref[...], HEADS))]
    d = jnp.concatenate([*d, jnp.zeros((2 * HEADS, SPAN), F32)], axis=0)
    td_o[...] = jnp.transpose(d)[0:16].astype(BF)
    buf[pl.ds(0, 8), :] = halo_rows(h_ref, pl.ds(INNER + STATE, STATE))
    buf[pl.ds(8, TOK), :] = bc_ref[:, STATE:].astype(F32)
    taps = [cwb_ref[k][:, STATE:] for k in range(4)]
    causal = iota((SPAN, SPAN), 0) >= iota((SPAN, SPAN), 1)
    for c in range(NB):
        rows = pl.ds(c * SPAN, SPAN)
        v = conv(buf[pl.ds(c * SPAN, SPAN + 8), :], taps, SPAN).astype(BF)
        c_o[rows, :] = v
        s = lax.dot_general(v, b_ref[rows, :], (((1,), (1,)), ((), ())), preferred_element_type=F32)
        sc_o[c] = jnp.where(causal, s, 0.0)


def table_call(L, step, ds, halo, bc, cwb, b, after):
    return call(
        table_body,
        "table",
        (L, step, ds, halo, bc, cwb, b, after),
        [
            ((TOK, STATE), BF),
            ((NB, SPAN, SPAN), F32),
            ((NCH, 8, TOK), F32),
            ((TOK, 128), BF),
            ((TOK, 128), BF),
            ((16, 128), BF),
        ],
        spaces=[pltpu.VMEM] * 7 + [pl.ANY],
        scratch=[pltpu.VMEM((TOK + 8, STATE), F32)],
        cost=(10**8, 2 << 20, 10**5),
    )


def decay_of(v):
    return v[STATE : STATE + 1] + v[STATE + 1 : STATE + 2]


def small_call(body, name, args, outs, scratch=(), after=()):
    n = len(args)
    m = len(after)

    def run(*refs):
        body(*refs[:n], *refs[n + m :])

    return call(
        run,
        name,
        (*args, *after),
        [(o.shape, o.dtype) for o in outs],
        spaces=[pltpu.VMEM] * n + [pl.ANY] * m,
        scratch=scratch,
    )


def pair_body(keep_ref, recv_ref, *outs):
    core, z = spot()[:2]
    for i in range(4):
        q = z ^ i
        own = keep_ref[q]
        other = recv_ref[q].astype(F32)
        early = jnp.where(core == 0, own, other)
        late = jnp.where(core == 0, other, own)
        d_early, d_late = decay_of(early), decay_of(late)
        outs[i][0:STATE, :] = (d_late * early[0:STATE] + late[0:STATE]).astype(BF)
        outs[i][STATE:WROWS, :] = wire_rows(d_early * d_late).astype(BF)


def row_body(r0, r1, r2, r3, total_o, pre_o, dpre_o, box):
    z = spot()[1]
    for i, r in enumerate((r0, r1, r2, r3)):
        box[z ^ i] = r[...].astype(F32)
    state = jnp.zeros((STATE, CHUNK), F32)
    decay = jnp.ones((1, CHUNK), F32)
    for k in range(4):
        pre_o[k] = state
        dpre_o[k] = jnp.broadcast_to(decay, (8, CHUNK))
        v = box[k]
        d = decay_of(v)
        state = d * state + v[0:STATE]
        decay = decay * d
    total_o[0:STATE, :] = state.astype(BF)
    total_o[STATE:WROWS, :] = wire_rows(decay).astype(BF)


def plane_body(r0, r1, r2, r3, pre_ref, dpre_ref, o0, o1, o2, o3, box):
    z, y = spot()[1:3]
    for i, r in enumerate((r0, r1, r2, r3)):
        box[y ^ i] = r[...].astype(F32)
    state = jnp.zeros((STATE, CHUNK), F32)
    for k in range(3):
        v = box[k]
        state = jnp.where(k < y, decay_of(v) * state + v[0:STATE], state)
    for i, o in enumerate((o0, o1, o2, o3)):
        q = z ^ i
        d = dpre_ref[q]
        o[...] = (pre_ref[q] + d[0:1] * state).astype(BF)


def spread_body(r0, r1, r2, r3, keep_ref, recv_ref, send_o, stay_o, box):
    core, z = spot()[:2]
    for i, r in enumerate((r0, r1, r2, r3)):
        box[z ^ i] = r[...].astype(F32)
    for q in range(4):
        early = jnp.where(core == 0, keep_ref[q], recv_ref[q].astype(F32))
        a = box[q]
        b = decay_of(early) * a + early[0:STATE]
        send_o[q] = jnp.where(core == 0, b, a).astype(BF)
        stay_o[q] = jnp.where(core == 0, a, b).astype(BF)


def mix_body(first_chunk, chunks, xc_ref, c_ref, sc_ref, z_ref, m2_ref, tl_ref, te_ref, td_ref, dec_ref, pst_ref,
             ds_ref, *rest):
    yg_o, g2_o, ex, ee = rest[-4:]
    left = iota((SPAN, SPAN), 1) < HD

    def expand(k):
        j = first_chunk + k
        ex[k % 2] = dot(tl_ref[...], onehot(j * HPC, HPC * SPAN, SPAN))
        ee[k % 2, :, 0:CHUNK] = dot(te_ref[...], onehot(j * HPC, CHUNK, HD, 0, 64))
        ee[k % 2, :, CHUNK:] = dot(te_ref[...], onehot(j * HPC, CHUNK, HD, 64, 128))

    expand(0)
    for k in range(chunks):
        j = first_chunk + k
        lanes = pl.ds(j * CHUNK, CHUNK)
        if k + 1 < chunks:
            expand(k + 1)
        skip = dot(td_ref[...], onehot(j * HPC, CHUNK, HD))[0:1]
        fix = ds_ref[:, lanes]
        for c in range(NB):
            rows = pl.ds(c * SPAN, SPAN)
            s = sc_ref[c]
            x = xc_ref[rows, lanes]
            parts = []
            for h in range(HPC):
                m2 = m2_ref[j, h : h + 1, c * SPAN : (c + 1) * SPAN]
                e = ex[k % 2, rows, h * SPAN : (h + 1) * SPAN] + m2
                parts.append((s * jnp.exp2(jnp.minimum(e, 8.0))).astype(BF))
            ys = []
            for p in range(HPC // 2):
                xp = x[:, p * SPAN : (p + 1) * SPAN].astype(F32)
                rhs = jnp.concatenate([jnp.where(left, xp, 0.0), jnp.where(left, 0.0, xp)], axis=0).astype(BF)
                ys.append(dot(jnp.concatenate([parts[2 * p], parts[2 * p + 1]], axis=1), rhs))
            y = jnp.concatenate(ys, axis=1) + skip * x.astype(F32)
            if c > 0:
                if c > 1:
                    fix = dec_ref[c - 1 : c, lanes] * fix
                ent = (pst_ref[c - 1, :, lanes] + fix).astype(BF)
                y = y + ee[k % 2, rows, 0:CHUNK] * dot(c_ref[rows, :], ent)
            gate = silu(z_ref[rows, lanes].astype(F32))
            yg_o[rows, lanes] = (y * gate).astype(BF)
            g2_o[rows, lanes] = (ee[k % 2, rows, CHUNK:] * gate).astype(BF)


def mix_call(first_chunk, chunks, args, after, before):
    n = len(args)
    return call(
        functools.partial(mix_body, first_chunk, chunks),
        "mix",
        (*args, after, *before),
        [((TOK, INNER), BF)] * 2,
        spaces=[pltpu.VMEM] * n + [pl.ANY],
        scratch=[pltpu.VMEM((2, TOK, HPC * SPAN), F32), pltpu.VMEM((2, TOK, 2 * CHUNK), F32)],
        aliases={n + 1: 0, n + 2: 1} if before else None,
        cost=(chunks * 25 * 10**7, chunks << 20, chunks * 6 * 10**5),
    )


def gated(yg_ref, g2_ref, c_ref, e_ref, gain_ref, half, blocks, n_o, ce, sums):
    at = lambda q: pl.ds(pl.multiple_of(half * (INNER // 2) + q * CHUNK, CHUNK), CHUNK)

    def carry(q):
        ce[q % 2] = dot(c_ref[...], e_ref[q])

    carry(0)
    for q in range(4):
        lanes = at(q)
        if q < 3:
            carry(q + 1)
        gain = gain_ref[:, lanes]
        for c in range(blocks):
            rows = pl.ds(c * SPAN, SPAN)
            g = yg_ref[rows, lanes].astype(F32) + ce[q % 2, rows, :] * g2_ref[rows, lanes].astype(F32)
            sq = g * g
            sq = sq[:, :128] + sq[:, 128:]
            sums[c] = sq if sums[c] is None else sums[c] + sq
            n_o[rows, q * CHUNK : (q + 1) * CHUNK] = (g * gain).astype(BF)


def near_gate_body(yg_ref, g2_ref, c_ref, e_ref, gain_ref, after_ref, n_o, ss_o, ce):
    sums = [None] * NB
    gated(yg_ref, g2_ref, c_ref, e_ref, gain_ref, spot()[0], NB, n_o, ce, sums)
    for c in range(NB):
        ss_o[pl.ds(c * SPAN, SPAN), :] = sums[c]


def far_gate_body(yg_ref, g2_ref, c_ref, e_ref, gain_ref, ss_ref, after_ref, n_o, inv_o, ce):
    sums = [ss_ref[pl.ds(c * SPAN, SPAN), :] for c in range(NB)]
    gated(yg_ref, g2_ref, c_ref, e_ref, gain_ref, 1 - spot()[0], NB, n_o, ce, sums)
    for c in range(NB):
        m = jnp.sum(sums[c], axis=1, keepdims=True) * (1.0 / INNER)
        inv_o[pl.ds(c * SPAN, SPAN), :] = jnp.broadcast_to(lax.rsqrt(m + 1e-05), (SPAN, 128))


def near_gate_call(yg, g2, cm, e, gain, after):
    return call(
        near_gate_body,
        "gate",
        (yg, g2, cm, e, gain, after),
        [((TOK, INNER // 2), BF), ((TOK, 128), F32)],
        spaces=[pltpu.VMEM] * 5 + [pl.ANY],
        scratch=[pltpu.VMEM((2, TOK, CHUNK), F32)],
        cost=(25 * 10**7, 4 << 20, 0),
    )


def far_gate_call(yg, g2, cm, e, gain, ss, after):
    return call(
        far_gate_body,
        "gate",
        (yg, g2, cm, e, gain, ss, after),
        [((TOK, INNER // 2), BF), ((TOK, 128), F32)],
        spaces=[pltpu.VMEM] * 6 + [pl.ANY],
        scratch=[pltpu.VMEM((2, TOK, CHUNK), F32)],
        cost=(25 * 10**7, 4 << 20, 0),
    )


def weight_block(w_ref, half, shift, k):
    lane = lax.rem(spot()[3] + shift, 4) * QOUT + k * CHUNK
    rows = pl.ds(pl.multiple_of(half * (INNER // 2), INNER // 2), INNER // 2)
    return w_ref[rows, pl.ds(pl.multiple_of(lane, CHUNK), CHUNK)]


def part_body(n_ref, w_ref, after_ref, p_o):
    core = spot()[0]
    for k in range(QOUT // CHUNK):
        p_o[:, k * CHUNK : (k + 1) * CHUNK] = dot(n_ref[...], weight_block(w_ref, core, 2, k))


def far_body(p_ref, n_ref, inv_ref, w_ref, r_o, l_o):
    core = spot()[0]
    for k in range(QOUT // CHUNK):
        y = p_ref[:, k * CHUNK : (k + 1) * CHUNK] + dot(n_ref[...], weight_block(w_ref, 1 - core, 2, k))
        o = (r_o, l_o)[k // 2]
        o[pl.ds((k % 2) * CHUNK, CHUNK), :] = jnp.transpose(y * inv_ref[:, 0:1]).astype(BF)


def proj_body(shift, first, count, near_ref, n_ref, inv_ref, w_ref, after_ref, o):
    core = spot()[0]
    for k in range(count):
        y = dot(near_ref[...], weight_block(w_ref, core, shift, first + k))
        y = y + dot(n_ref[...], weight_block(w_ref, 1 - core, shift, first + k))
        o[pl.ds(k * CHUNK, CHUNK), :] = jnp.transpose(y * inv_ref[:, 0:1]).astype(BF)


def part_call(near, w, after):
    return call(
        part_body,
        "part",
        (near, w, after),
        [((TOK, QOUT), F32)],
        spaces=[pltpu.VMEM] * 2 + [pl.ANY],
        cost=(TOK * INNER * QOUT, 5 << 20, 0),
    )[0]


def far_call(p, n, inv, w):
    return call(
        far_body,
        "far",
        (p, n, inv, w),
        [((QOUT // 2, TOK), BF)] * 2,
        cost=(TOK * INNER * QOUT, 5 << 20, 0),
    )


def proj_call(shift, side, near, n, inv, w, after):
    count = 2 if side < 2 else 4
    return call(
        functools.partial(proj_body, shift, 2 * side if side < 2 else 0, count),
        "proj",
        (near, n, inv, w, after),
        [((count * CHUNK, TOK), BF)],
        spaces=[pltpu.VMEM] * 4 + [pl.ANY],
        cost=(2 * TOK * INNER * count * CHUNK, 5 << 20, 0),
    )[0]


def relay_body(mine, a, o):
    o[...] = (mine[...].astype(F32) + a[...].astype(F32)).astype(BF)


def last_body(own, near_r, near_l, sum_r, sum_l, o_hbm, o, sem):
    copies = []
    for k in range(4):
        rows = pl.ds(k * CHUNK, CHUNK)
        side = pl.ds((k % 2) * CHUNK, CHUNK)
        near, total = ((near_r, sum_r), (near_l, sum_l))[k // 2]
        s = own[rows, :].astype(F32) + near[side, :].astype(F32) + total[side, :].astype(F32)
        o[rows, :] = s.astype(BF)
        copies.append(pltpu.make_async_copy(o.at[rows, :], o_hbm.at[rows, :], sem.at[k]))
        copies[k].start()
    for c in copies:
        c.wait()


def last_call(*args):
    return pl.pallas_call(
        last_body,
        in_specs=[pl.BlockSpec(memory_space=pltpu.VMEM)] * len(args),
        out_specs=pl.BlockSpec(memory_space=pltpu.HBM),
        out_shape=jax.ShapeDtypeStruct((QOUT, TOK), BF),
        scratch_shapes=[pltpu.VMEM((QOUT, TOK), BF), pltpu.SemaphoreType.DMA((4,))],
        compiler_params=pltpu.CompilerParams(vmem_limit_bytes=VMEM_LIMIT),
        name="last",
    )(*args)


def seq_perm(v, y, z, core):
    return lax.ppermute(v, "seq", [(src, src ^ (y * 8 + z * 2 + core)) for src in range(32)])


def head_perm(v, shift):
    return lax.ppermute(v, "head", [(s, (s + shift) % 4) for s in range(4)])


def on_device(x_in, bc_in, z_in, dt_raw, a_log, conv_x, conv_bc, d_skip, norm_gain, out_weight):
    bc = bc_in.reshape(TOK, 256)
    hbm = lambda v: pltpu.with_memory_space_constraint(v, pltpu.HBM)
    edge = call(
        edge_body,
        "edge",
        (hbm(x_in), hbm(bc)),
        [((8, INNER + 256), BF)],
        spaces=[pltpu.HBM] * 2,
        scratch=[pltpu.SemaphoreType.DMA((2,))],
    )[0]
    halo = lax.ppermute(edge, "seq", [(s, (s + 1) % 32) for s in range(32)])
    xc, b, pst, end, dec, L, step, tw0, x0, b0 = first_call(
        hbm(x_in), bc, conv_x, conv_bc, dt_raw, a_log.reshape(1, HEADS)
    )
    xc, b, ds, send, keep = second_call(halo, x0, b0, conv_x, conv_bc, tw0, end, dec, xc, b)
    recv = seq_perm(send, 0, 0, 1)
    cm, sc, m2, tl, te, td = table_call(L, step, d_skip.reshape(1, HEADS), halo, bc, conv_bc, b, send)
    piece = jax.ShapeDtypeStruct((WROWS, CHUNK), BF)
    plain = jax.ShapeDtypeStruct((STATE, CHUNK), BF)
    box = pltpu.VMEM((4, WROWS, CHUNK), F32)
    splits = (3, 3, 2)
    known = (xc, cm, sc, z_in, m2, tl, te, td, dec, pst, ds)
    work = lambda k, after, before: mix_call(sum(splits[:k]), splits[k], known, after, before)
    q = small_call(pair_body, "pair", (keep, recv), [piece] * 4, (), (cm,))
    mixed = work(0, q[0], ())
    rows = [q[0]] + [seq_perm(q[i], 0, i, 0) for i in (1, 2, 3)]
    total, pre, dpre = small_call(
        row_body,
        "row",
        rows,
        [piece, jax.ShapeDtypeStruct((4, STATE, CHUNK), F32), jax.ShapeDtypeStruct((4, 8, CHUNK), F32)],
        [box],
        (mixed[0],),
    )
    mixed = work(1, total, mixed)
    cols = [total] + [seq_perm(total, i, 0, 0) for i in (1, 2, 3)]
    e = small_call(plane_body, "plane", (*cols, pre, dpre), [plain] * 4, [box], (mixed[0],))
    mixed = work(2, e[0], mixed)
    back = [e[0]] + [seq_perm(e[i], 0, i, 0) for i in (1, 2, 3)]
    half = jax.ShapeDtypeStruct((4, STATE, CHUNK), BF)
    give, stay = small_call(
        spread_body, "spread", (*back, keep, recv), [half] * 2, [pltpu.VMEM((4, STATE, CHUNK), F32)], (mixed[0],)
    )
    take = seq_perm(give, 0, 0, 1)
    gain = norm_gain.reshape(1, INNER)
    near, ss = near_gate_call(*mixed, cm, stay, gain, give)
    p = part_call(near, out_weight, ss)
    other, inv = far_gate_call(*mixed, cm, take, gain, ss, p)
    far_r, far_l = far_call(p, other, inv, out_weight)
    from_left, from_right = head_perm(far_r, 1), head_perm(far_l, -1)
    proj = lambda shift, side, after: proj_call(shift, side, near, other, inv, out_weight, after)
    right_l = proj(1, 1, far_r)
    near_l = head_perm(right_l, 1)
    left_r = proj(3, 0, right_l)
    near_r = head_perm(left_r, -1)
    right_r = proj(1, 0, left_r)
    left_l = proj(3, 1, right_r)
    shape = ((QOUT // 2, TOK), BF)
    sum_r = head_perm(call(relay_body, "relay", (right_r, from_left), [shape])[0], 1)
    sum_l = head_perm(call(relay_body, "relay", (left_l, from_right), [shape])[0], -1)
    own = proj(0, 2, left_l)
    return last_call(own, near_r, near_l, sum_r, sum_l)


def solution(mesh):
    placed = (
        P("seq", "head"),
        P("seq", "head", None),
        P("seq", "head"),
        P("head", "seq"),
        P("head"),
        P(None, "head"),
        P(None, "head", None),
        P("head"),
        P("head"),
        P("head", None),
    )
    return jax.shard_map(
        on_device, mesh=mesh, in_specs=placed, out_specs=P("head", "seq"), check_vma=False
    )
```

```python
import functools

import jax
import jax.numpy as jnp
from jax import lax
from jax.experimental import pallas as pl
from jax.experimental.pallas import tpu as pltpu
from jax.sharding import PartitionSpec as P

SPAN = 128
HEADS = 32
HD = 64
STATE = 128
TOK = 512
NB = 4
INNER = 2048
CHUNK = 256
NCH = INNER // CHUNK
HPC = CHUNK // HD
DOUT = 4096
QOUT = 1024
WROWS = 144
LOG2E = 1.4426950408889634
BF = jnp.bfloat16
F32 = jnp.float32
VMEM_LIMIT = 10 << 20


def silu(u):
    half = 0.5 * u
    return half + half * jnp.tanh(half)


def dot(a, b):
    return jnp.dot(a, b, preferred_element_type=F32)


def iota(shape, axis):
    return lax.broadcasted_iota(jnp.int32, shape, axis)


def onehot(first_head, width, lanes, low=0, high=128):
    k = iota((128, width), 0)
    h = first_head + (iota((128, width), 1) // lanes)
    hit = ((k & 31) == h) & (k >= low) & (k < high)
    return jnp.where(hit, 1.0, 0.0).astype(BF)


def split2(v):
    hi = v.astype(BF).astype(F32)
    return hi, (v - hi).astype(BF).astype(F32)


def column(row, n):
    eye = iota((n, n), 0) == iota((n, n), 1)
    return jnp.sum(jnp.where(eye, jnp.broadcast_to(row, (n, n)), 0.0), axis=1, keepdims=True)


def call(body, name, args, outs, spaces=(), scratch=(), cost=(10**6, 1 << 20, 0), aliases=None, limit=VMEM_LIMIT):
    specs = [pl.BlockSpec(memory_space=spaces[k] if k < len(spaces) else pltpu.VMEM) for k in range(len(args))]
    return pl.pallas_call(
        body,
        in_specs=specs,
        out_specs=[pl.BlockSpec(memory_space=pltpu.VMEM)] * len(outs),
        out_shape=[jax.ShapeDtypeStruct(s, d) for s, d in outs],
        scratch_shapes=list(scratch),
        input_output_aliases=aliases or {},
        compiler_params=pltpu.CompilerParams(vmem_limit_bytes=limit),
        cost_estimate=pl.CostEstimate(flops=cost[0], bytes_accessed=cost[1], transcendentals=cost[2]),
        name=name,
    )(*args)


def conv(window, taps, rows):
    u = taps[3] * window[8:]
    for k in range(3):
        u = u + taps[k] * pltpu.roll(window, 3 - k, 0)[8:]
    return silu(u)


def taps_of(ref, lanes):
    return [ref[k : k + 1, lanes] for k in range(4)]


def split3(v):
    hi = v.astype(BF).astype(F32)
    rest = v - hi
    mid = rest.astype(BF).astype(F32)
    return hi, mid, rest - mid


def spot():
    place = lax.axis_index("seq")
    return place & 1, (place >> 1) & 3, place >> 3, lax.axis_index("head")


def edge_body(x_ref, bc_ref, o, sem):
    a = pltpu.make_async_copy(x_ref.at[pl.ds(TOK - 8, 8), :], o.at[:, pl.ds(0, INNER)], sem.at[0])
    b = pltpu.make_async_copy(bc_ref.at[pl.ds(TOK - 8, 8), :], o.at[:, pl.ds(INNER, 256)], sem.at[1])
    a.start()
    b.start()
    a.wait()
    b.wait()


def halo_rows(h_ref, lanes):
    return jnp.where(lax.axis_index("seq") == 0, 0.0, h_ref[:, lanes].astype(F32))


def half_lanes(half, k, width=CHUNK):
    return pl.ds(pl.multiple_of(half * (INNER // 2) + k, 128), width)


def states(half, fetch, xv, cwx, tw, dtab, bts, wbuf, xw, xc_o, pst_o, end_o, dec_o, x0_o):
    nothing = jnp.zeros((8, 128), F32)
    head = lambda q: half * (HEADS // 2) + q * HPC
    wbuf[0] = dot(tw[...], onehot(head(0), CHUNK, HD, 0, 64))
    for q in range(5):
        if q < 4:
            if q < 3:
                wbuf[(q + 1) % 2] = dot(tw[...], onehot(head(q + 1), CHUNK, HD, 0, 64))
            dec_o[:, half_lanes(half, q * CHUNK)] = dot(dtab[...], onehot(head(q), CHUNK, HD, 64, 128))
            fetch[q].wait()
            x0_o[:, half_lanes(half, q * CHUNK)] = xv[0:16, q * CHUNK : (q + 1) * CHUNK]
        state = None
        for c in range(NB):
            if q < 4:
                for r in (0, 64):
                    for l in (0, 128):
                        row = c * SPAN + r
                        part = half_lanes(half, q * CHUNK + l, 128)
                        here = pl.ds(q * CHUNK + l, 128)
                        if row == 0:
                            window = jnp.concatenate([nothing, xv[0:64, here].astype(F32)], axis=0)
                        else:
                            window = xv[pl.ds(row - 8, 72), here].astype(F32)
                        v = conv(window, taps_of(cwx, part), 64).astype(BF)
                        xc_o[pl.ds(row, 64), part] = v
                        w = wbuf[q % 2, pl.ds(row, 64), l : l + 128]
                        xw[q % 2, pl.ds(row, 64), l : l + 128] = (v.astype(F32) * w).astype(BF)
            if q > 0:
                before = half_lanes(half, (q - 1) * CHUNK)
                t = dot(bts[c], xw[(q - 1) % 2, pl.ds(c * SPAN, SPAN), :])
                state = t if c == 0 else dec_o[c : c + 1, before] * state + t
                if c < NB - 1:
                    pst_o[c, :, before] = state
                else:
                    end_o[:, (q - 1) * CHUNK : q * CHUNK] = state


def fetch_half(x_hbm, xv, half, sem):
    copies = []
    for q in range(4):
        here = pl.ds(q * CHUNK, CHUNK)
        copies.append(pltpu.make_async_copy(x_hbm.at[:, half_lanes(half, q * CHUNK)], xv.at[:, here], sem.at[q]))
        copies[q].start()
    return copies


def first_body(x_hbm, bv, cwx, cwb, dtv, alv,
               xc_o, pst_o, dec_o, x0_o, end_o, b_o, L_o, step_o, tw0_o, b0_o, tw, bts, dtab_o,
               xv, wbuf, xw, sem):
    half = 1 - spot()[0]
    copies = fetch_half(x_hbm, xv, half, sem)
    tri = jnp.where(iota((SPAN, SPAN), 0) <= iota((SPAN, SPAN), 1), 1.0, 0.0).astype(BF)
    v = dtv[...].astype(F32)
    t = jnp.exp(-jnp.abs(v))
    u = 1.0 + t
    d = u - 1.0
    flat = d == 0.0
    step = jnp.maximum(v, 0.0) + jnp.where(flat, t, jnp.log(u) * t / jnp.where(flat, 1.0, d))
    step_o[...] = step
    a = column(alv[...], HEADS)
    rate = jnp.concatenate(split3((-LOG2E * jnp.exp(a)) * step), axis=0).astype(BF)
    Ls, ends = [], []
    for c in range(NB):
        s = dot(rate[:, c * SPAN : (c + 1) * SPAN], tri)
        s = s[0:HEADS] + s[HEADS : 2 * HEADS] + s[2 * HEADS : 3 * HEADS]
        Ls.append(s)
        ends.append(jnp.broadcast_to(s[:, SPAN - 1 : SPAN], (HEADS, SPAN)))
    L = jnp.concatenate(Ls, axis=1)
    end = jnp.concatenate(ends, axis=1)
    L_o[...] = L
    w_hi, w_lo = split2(jnp.exp2(end - L) * step)
    d_hi, d_lo = split2(jnp.exp2(end))
    twt = jnp.transpose(jnp.concatenate([w_hi, w_lo, d_hi, d_lo], axis=0))
    tw[...] = twt.astype(BF)
    tw0_o[...] = twt[0:16].astype(BF)
    tw[pl.ds(0, 16), :] = jnp.zeros((16, 128), BF)
    rows = [twt[c * SPAN : c * SPAN + 1] for c in range(NB)]
    dtab = jnp.concatenate(rows + [jnp.zeros((12, SPAN), F32)], axis=0).astype(BF)
    dtab_o[...] = dtab
    b0_o[...] = bv[0:16, :STATE]
    btaps = [cwb[k][:, :STATE] for k in range(4)]
    nothing = jnp.zeros((8, STATE), F32)
    for c in range(NB):
        if c == 0:
            window = jnp.concatenate([nothing, bv[0:SPAN, :STATE].astype(F32)], axis=0)
        else:
            window = bv[pl.ds(c * SPAN - 8, SPAN + 8), :STATE].astype(F32)
        v = conv(window, btaps, SPAN)
        b_o[pl.ds(c * SPAN, SPAN), :] = v.astype(BF)
        bts[c] = jnp.transpose(v).astype(BF)
    states(half, copies, xv, cwx, tw, dtab_o, bts, wbuf, xw, xc_o, pst_o, end_o, dec_o, x0_o)


def rest_body(x_hbm, cwx, tw, bts, dtab, xc_i, pst_i, dec_i, x0_i, after,
              xc_o, pst_o, dec_o, x0_o, end_o, xv, wbuf, xw, sem):
    half = spot()[0]
    copies = fetch_half(x_hbm, xv, half, sem)
    states(half, copies, xv, cwx, tw, dtab, bts, wbuf, xw, xc_o, pst_o, end_o, dec_o, x0_o)


SHARED = [
    ((TOK, INNER), BF),
    ((NB - 1, STATE, INNER), F32),
    ((16, INNER), F32),
    ((16, INNER), BF),
    ((STATE, INNER // 2), F32),
]
ROOM = [
    pltpu.VMEM((TOK, INNER // 2), BF),
    pltpu.VMEM((2, TOK, CHUNK), F32),
    pltpu.VMEM((2, TOK, CHUNK), BF),
    pltpu.SemaphoreType.DMA((4,)),
]


def first_call(x, bc, cwx, cwb, dt, al):
    return call(
        first_body,
        "first",
        (x, bc, cwx, cwb, dt, al),
        SHARED
        + [
            ((TOK, STATE), BF),
            ((HEADS, TOK), F32),
            ((HEADS, TOK), F32),
            ((16, 128), BF),
            ((16, STATE), BF),
            ((TOK, 128), BF),
            ((NB, STATE, SPAN), BF),
            ((16, 128), BF),
        ],
        spaces=[pltpu.HBM],
        scratch=ROOM,
        cost=(10**5, 1 << 14, 0),
    )


def rest_call(x, cwx, tw, bts, dtab, xc, pst, dec, x0, after):
    return call(
        rest_body,
        "rest",
        (x, cwx, tw, bts, dtab, xc, pst, dec, x0, after),
        SHARED,
        spaces=[pltpu.HBM] + [pltpu.VMEM] * 8 + [pl.ANY],
        scratch=ROOM,
        aliases={5: 0, 6: 1, 7: 2, 8: 3},
        cost=(10**5, 1 << 14, 0),
    )


def wire_rows(decay):
    hi, lo = split2(decay)
    return jnp.concatenate([hi, lo, jnp.zeros((14, decay.shape[1]), F32)], axis=0)


def correct(half, bt, h_ref, x0_ref, cwx_ref, tw0_ref, end_ref, dec_ref, xc_o, ds_o, emit):
    for q in range(4):
        lanes = half_lanes(half, q * CHUNK)
        window = jnp.concatenate([halo_rows(h_ref, lanes), x0_ref[:, lanes].astype(F32)], axis=0)
        u = conv(window, taps_of(cwx_ref, lanes), 16).astype(BF)
        xc_o[0:16, lanes] = u
        w = dot(tw0_ref[...], onehot(half * (HEADS // 2) + q * HPC, CHUNK, HD, 0, 64))
        xw = jnp.concatenate([u.astype(F32) * w, jnp.zeros((SPAN - 16, CHUNK), F32)], axis=0).astype(BF)
        fix = dot(bt, xw)
        ds_o[:, lanes] = fix
        dec = dec_ref[0:8, lanes]
        after = dec[1:2] * dec[2:3] * dec[3:4]
        emit(q, end_ref[:, q * CHUNK : (q + 1) * CHUNK] + after * fix, dec[0:1] * after)


def second_body(h_ref, x0_ref, b0_ref, cwx_ref, cwb_ref, tw0_ref, end_ref, dec_ref, xc_in, b_in,
                xc_o, b_o, ds_o, send_o, bt_o):
    v = jnp.concatenate([halo_rows(h_ref, pl.ds(INNER, STATE)), b0_ref[...].astype(F32)], axis=0)
    v = conv(v, [cwb_ref[k][:, :STATE] for k in range(4)], 16)
    b_o[0:16, :] = v.astype(BF)
    bt = jnp.transpose(jnp.concatenate([v, jnp.zeros((SPAN - 16, STATE), F32)], axis=0)).astype(BF)
    bt_o[...] = bt

    def emit(q, state, decay):
        send_o[q, 0:STATE, :] = state.astype(BF)
        send_o[q, STATE:WROWS, :] = wire_rows(decay).astype(BF)

    correct(1 - spot()[0], bt, h_ref, x0_ref, cwx_ref, tw0_ref, end_ref, dec_ref, xc_o, ds_o, emit)


def third_body(h_ref, x0_ref, bt_ref, cwx_ref, tw0_ref, end_ref, dec_ref, xc_in, ds_in, xc_o, ds_o, keep_o):
    def emit(q, state, decay):
        keep_o[q, 0:STATE, :] = state
        keep_o[q, STATE:WROWS, :] = jnp.concatenate([decay, jnp.zeros((15, CHUNK), F32)], axis=0)

    correct(spot()[0], bt_ref[...], h_ref, x0_ref, cwx_ref, tw0_ref, end_ref, dec_ref, xc_o, ds_o, emit)


def second_call(halo, x0, b0, cwx, cwb, tw0, end, dec, xc, b):
    return call(
        second_body,
        "second",
        (halo, x0, b0, cwx, cwb, tw0, end, dec, xc, b),
        [
            ((TOK, INNER), BF),
            ((TOK, STATE), BF),
            ((STATE, INNER), F32),
            ((4, WROWS, CHUNK), BF),
            ((STATE, 128), BF),
        ],
        aliases={8: 0, 9: 1},
        cost=(10**5, 1 << 14, 0),
    )


def third_call(halo, x0, bt, cwx, tw0, end, dec, xc, ds):
    return call(
        third_body,
        "third",
        (halo, x0, bt, cwx, tw0, end, dec, xc, ds),
        [((TOK, INNER), BF), ((STATE, INNER), F32), ((4, WROWS, CHUNK), F32)],
        aliases={7: 0, 8: 1},
        cost=(10**5, 1 << 14, 0),
    )


def table_body(L_ref, step_ref, ds_ref, h_ref, bc_ref, cwb_ref, b_ref, after_ref,
               c_o, sc_o, m2_o, tl_o, te_o, td_o, buf):
    L = L_ref[...]
    M = jnp.log(step_ref[...]) * LOG2E - L
    for j in range(NCH):
        m2_o[j, 0:HPC, :] = M[j * HPC : (j + 1) * HPC, :]
    zero = jnp.zeros((HEADS, TOK), F32)
    tl_o[...] = jnp.transpose(jnp.concatenate([*split3(L), zero], axis=0)).astype(BF)
    parts, before = [], jnp.zeros((HEADS, SPAN), F32)
    for c in range(NB):
        s = L[:, c * SPAN : (c + 1) * SPAN]
        parts.append(before + s)
        before = before + jnp.broadcast_to(s[:, SPAN - 1 : SPAN], (HEADS, SPAN))
    e = [*split2(jnp.exp2(L)), *split2(jnp.exp2(jnp.concatenate(parts, axis=1)))]
    te_o[...] = jnp.transpose(jnp.concatenate(e, axis=0)).astype(BF)
    d = [jnp.broadcast_to(p, (HEADS, SPAN)) for p in split2(column(ds_ref[...], HEADS))]
    d = jnp.concatenate([*d, jnp.zeros((2 * HEADS, SPAN), F32)], axis=0)
    td_o[...] = jnp.transpose(d)[0:16].astype(BF)
    buf[pl.ds(0, 8), :] = halo_rows(h_ref, pl.ds(INNER + STATE, STATE))
    buf[pl.ds(8, TOK), :] = bc_ref[:, STATE:].astype(F32)
    taps = [cwb_ref[k][:, STATE:] for k in range(4)]
    causal = iota((SPAN, SPAN), 0) >= iota((SPAN, SPAN), 1)
    for c in range(NB):
        rows = pl.ds(c * SPAN, SPAN)
        v = conv(buf[pl.ds(c * SPAN, SPAN + 8), :], taps, SPAN).astype(BF)
        c_o[rows, :] = v
        s = lax.dot_general(v, b_ref[rows, :], (((1,), (1,)), ((), ())), preferred_element_type=F32)
        sc_o[c] = jnp.where(causal, s, 0.0)


def table_call(L, step, ds, halo, bc, cwb, b, after):
    return call(
        table_body,
        "table",
        (L, step, ds, halo, bc, cwb, b, after),
        [
            ((TOK, STATE), BF),
            ((NB, SPAN, SPAN), F32),
            ((NCH, 8, TOK), F32),
            ((TOK, 128), BF),
            ((TOK, 128), BF),
            ((16, 128), BF),
        ],
        spaces=[pltpu.VMEM] * 7 + [pl.ANY],
        scratch=[pltpu.VMEM((TOK + 8, STATE), F32)],
        cost=(10**8, 2 << 20, 10**5),
    )


def decay_of(v):
    return v[STATE : STATE + 1] + v[STATE + 1 : STATE + 2]


def small_call(body, name, args, outs, scratch=(), after=()):
    n = len(args)
    m = len(after)

    def run(*refs):
        body(*refs[:n], *refs[n + m :])

    return call(
        run,
        name,
        (*args, *after),
        [(o.shape, o.dtype) for o in outs],
        spaces=[pltpu.VMEM] * n + [pl.ANY] * m,
        scratch=scratch,
    )


def pair_body(keep_ref, recv_ref, *outs):
    core, z = spot()[:2]
    for i in range(4):
        q = z ^ i
        own = keep_ref[q]
        other = recv_ref[q].astype(F32)
        early = jnp.where(core == 0, own, other)
        late = jnp.where(core == 0, other, own)
        d_early, d_late = decay_of(early), decay_of(late)
        outs[i][0:STATE, :] = (d_late * early[0:STATE] + late[0:STATE]).astype(BF)
        outs[i][STATE:WROWS, :] = wire_rows(d_early * d_late).astype(BF)


def row_body(r0, r1, r2, r3, total_o, pre_o, dpre_o, box):
    z = spot()[1]
    for i, r in enumerate((r0, r1, r2, r3)):
        box[z ^ i] = r[...].astype(F32)
    state = jnp.zeros((STATE, CHUNK), F32)
    decay = jnp.ones((1, CHUNK), F32)
    for k in range(4):
        pre_o[k] = state
        dpre_o[k] = jnp.broadcast_to(decay, (8, CHUNK))
        v = box[k]
        d = decay_of(v)
        state = d * state + v[0:STATE]
        decay = decay * d
    total_o[0:STATE, :] = state.astype(BF)
    total_o[STATE:WROWS, :] = wire_rows(decay).astype(BF)


def plane_body(r0, r1, r2, r3, pre_ref, dpre_ref, o0, o1, o2, o3, box):
    z, y = spot()[1:3]
    for i, r in enumerate((r0, r1, r2, r3)):
        box[y ^ i] = r[...].astype(F32)
    state = jnp.zeros((STATE, CHUNK), F32)
    for k in range(3):
        v = box[k]
        state = jnp.where(k < y, decay_of(v) * state + v[0:STATE], state)
    for i, o in enumerate((o0, o1, o2, o3)):
        q = z ^ i
        d = dpre_ref[q]
        o[...] = (pre_ref[q] + d[0:1] * state).astype(BF)


def spread_body(r0, r1, r2, r3, keep_ref, recv_ref, send_o, stay_o, box):
    core, z = spot()[:2]
    for i, r in enumerate((r0, r1, r2, r3)):
        box[z ^ i] = r[...].astype(F32)
    for q in range(4):
        early = jnp.where(core == 0, keep_ref[q], recv_ref[q].astype(F32))
        a = box[q]
        b = decay_of(early) * a + early[0:STATE]
        send_o[q] = jnp.where(core == 0, b, a).astype(BF)
        stay_o[q] = jnp.where(core == 0, a, b).astype(BF)


def mix_body(first_chunk, chunks, xc_ref, c_ref, sc_ref, z_ref, m2_ref, tl_ref, te_ref, td_ref, dec_ref, pst_ref,
             ds_ref, *rest):
    yg_o, g2_o, ex, ee = rest[-4:]
    left = iota((SPAN, SPAN), 1) < HD

    def expand(k):
        j = first_chunk + k
        ex[k % 2] = dot(tl_ref[...], onehot(j * HPC, HPC * SPAN, SPAN))
        ee[k % 2, :, 0:CHUNK] = dot(te_ref[...], onehot(j * HPC, CHUNK, HD, 0, 64))
        ee[k % 2, :, CHUNK:] = dot(te_ref[...], onehot(j * HPC, CHUNK, HD, 64, 128))

    expand(0)
    for k in range(chunks):
        j = first_chunk + k
        lanes = pl.ds(j * CHUNK, CHUNK)
        if k + 1 < chunks:
            expand(k + 1)
        skip = dot(td_ref[...], onehot(j * HPC, CHUNK, HD))[0:1]
        fix = ds_ref[:, lanes]
        for c in range(NB):
            rows = pl.ds(c * SPAN, SPAN)
            s = sc_ref[c]
            x = xc_ref[rows, lanes]
            parts = []
            for h in range(HPC):
                m2 = m2_ref[j, h : h + 1, c * SPAN : (c + 1) * SPAN]
                e = ex[k % 2, rows, h * SPAN : (h + 1) * SPAN] + m2
                parts.append((s * jnp.exp2(jnp.minimum(e, 8.0))).astype(BF))
            ys = []
            for p in range(HPC // 2):
                xp = x[:, p * SPAN : (p + 1) * SPAN].astype(F32)
                rhs = jnp.concatenate([jnp.where(left, xp, 0.0), jnp.where(left, 0.0, xp)], axis=0).astype(BF)
                ys.append(dot(jnp.concatenate([parts[2 * p], parts[2 * p + 1]], axis=1), rhs))
            y = jnp.concatenate(ys, axis=1) + skip * x.astype(F32)
            if c > 0:
                if c > 1:
                    fix = dec_ref[c - 1 : c, lanes] * fix
                ent = (pst_ref[c - 1, :, lanes] + fix).astype(BF)
                y = y + ee[k % 2, rows, 0:CHUNK] * dot(c_ref[rows, :], ent)
            gate = silu(z_ref[rows, lanes].astype(F32))
            yg_o[rows, lanes] = (y * gate).astype(BF)
            g2_o[rows, lanes] = (ee[k % 2, rows, CHUNK:] * gate).astype(BF)


def mix_call(first_chunk, chunks, args, after, before):
    n = len(args)
    return call(
        functools.partial(mix_body, first_chunk, chunks),
        "mix",
        (*args, after, *before),
        [((TOK, INNER), BF)] * 2,
        spaces=[pltpu.VMEM] * n + [pl.ANY],
        scratch=[pltpu.VMEM((2, TOK, HPC * SPAN), F32), pltpu.VMEM((2, TOK, 2 * CHUNK), F32)],
        aliases={n + 1: 0, n + 2: 1} if before else None,
        cost=(chunks * 25 * 10**7, chunks << 20, chunks * 6 * 10**5),
    )


def gated(yg_ref, g2_ref, c_ref, e_ref, gain_ref, half, blocks, n_o, ce, sums):
    at = lambda q: pl.ds(pl.multiple_of(half * (INNER // 2) + q * CHUNK, CHUNK), CHUNK)

    def carry(q):
        ce[q % 2] = dot(c_ref[...], e_ref[q])

    carry(0)
    for q in range(4):
        lanes = at(q)
        if q < 3:
            carry(q + 1)
        gain = gain_ref[:, lanes]
        for c in range(blocks):
            rows = pl.ds(c * SPAN, SPAN)
            g = yg_ref[rows, lanes].astype(F32) + ce[q % 2, rows, :] * g2_ref[rows, lanes].astype(F32)
            sq = g * g
            sq = sq[:, :128] + sq[:, 128:]
            sums[c] = sq if sums[c] is None else sums[c] + sq
            n_o[rows, q * CHUNK : (q + 1) * CHUNK] = (g * gain).astype(BF)


def near_gate_body(yg_ref, g2_ref, c_ref, e_ref, gain_ref, after_ref, n_o, ss_o, ce):
    sums = [None] * NB
    gated(yg_ref, g2_ref, c_ref, e_ref, gain_ref, spot()[0], NB, n_o, ce, sums)
    for c in range(NB):
        ss_o[pl.ds(c * SPAN, SPAN), :] = sums[c]


def far_gate_body(yg_ref, g2_ref, c_ref, e_ref, gain_ref, ss_ref, after_ref, n_o, inv_o, ce):
    sums = [ss_ref[pl.ds(c * SPAN, SPAN), :] for c in range(NB)]
    gated(yg_ref, g2_ref, c_ref, e_ref, gain_ref, 1 - spot()[0], NB, n_o, ce, sums)
    for c in range(NB):
        m = jnp.sum(sums[c], axis=1, keepdims=True) * (1.0 / INNER)
        inv_o[pl.ds(c * SPAN, SPAN), :] = jnp.broadcast_to(lax.rsqrt(m + 1e-05), (SPAN, 128))


def near_gate_call(yg, g2, cm, e, gain, after):
    return call(
        near_gate_body,
        "gate",
        (yg, g2, cm, e, gain, after),
        [((TOK, INNER // 2), BF), ((TOK, 128), F32)],
        spaces=[pltpu.VMEM] * 5 + [pl.ANY],
        scratch=[pltpu.VMEM((2, TOK, CHUNK), F32)],
        cost=(25 * 10**7, 4 << 20, 0),
    )


def far_gate_call(yg, g2, cm, e, gain, ss, after):
    return call(
        far_gate_body,
        "gate",
        (yg, g2, cm, e, gain, ss, after),
        [((TOK, INNER // 2), BF), ((TOK, 128), F32)],
        spaces=[pltpu.VMEM] * 6 + [pl.ANY],
        scratch=[pltpu.VMEM((2, TOK, CHUNK), F32)],
        cost=(25 * 10**7, 4 << 20, 0),
    )


def weight_block(w_ref, half, shift, k):
    lane = lax.rem(spot()[3] + shift, 4) * QOUT + k * CHUNK
    rows = pl.ds(pl.multiple_of(half * (INNER // 2), INNER // 2), INNER // 2)
    return w_ref[rows, pl.ds(pl.multiple_of(lane, CHUNK), CHUNK)]


def part_body(n_ref, w_ref, after_ref, p_o):
    core = spot()[0]
    for k in range(QOUT // CHUNK):
        p_o[:, k * CHUNK : (k + 1) * CHUNK] = dot(n_ref[...], weight_block(w_ref, core, 2, k))


def far_body(p_ref, n_ref, inv_ref, w_ref, r_o, l_o):
    core = spot()[0]
    for k in range(QOUT // CHUNK):
        y = p_ref[:, k * CHUNK : (k + 1) * CHUNK] + dot(n_ref[...], weight_block(w_ref, 1 - core, 2, k))
        o = (r_o, l_o)[k // 2]
        o[pl.ds((k % 2) * CHUNK, CHUNK), :] = jnp.transpose(y * inv_ref[:, 0:1]).astype(BF)


def proj_body(shift, first, count, near_ref, n_ref, inv_ref, w_ref, after_ref, o):
    core = spot()[0]
    for k in range(count):
        y = dot(near_ref[...], weight_block(w_ref, core, shift, first + k))
        y = y + dot(n_ref[...], weight_block(w_ref, 1 - core, shift, first + k))
        o[pl.ds(k * CHUNK, CHUNK), :] = jnp.transpose(y * inv_ref[:, 0:1]).astype(BF)


def part_call(near, w, after):
    return call(
        part_body,
        "part",
        (near, w, after),
        [((TOK, QOUT), F32)],
        spaces=[pltpu.VMEM] * 2 + [pl.ANY],
        cost=(TOK * INNER * QOUT, 5 << 20, 0),
    )[0]


def far_call(p, n, inv, w):
    return call(
        far_body,
        "far",
        (p, n, inv, w),
        [((QOUT // 2, TOK), BF)] * 2,
        cost=(TOK * INNER * QOUT, 5 << 20, 0),
    )


def proj_call(shift, side, near, n, inv, w, after):
    count = 2 if side < 2 else 4
    return call(
        functools.partial(proj_body, shift, 2 * side if side < 2 else 0, count),
        "proj",
        (near, n, inv, w, after),
        [((count * CHUNK, TOK), BF)],
        spaces=[pltpu.VMEM] * 4 + [pl.ANY],
        cost=(2 * TOK * INNER * count * CHUNK, 5 << 20, 0),
    )[0]


def relay_body(mine, a, o):
    o[...] = (mine[...].astype(F32) + a[...].astype(F32)).astype(BF)


def last_body(own, near_r, near_l, sum_r, sum_l, o_hbm, o, sem):
    copies = []
    for k in range(4):
        rows = pl.ds(k * CHUNK, CHUNK)
        side = pl.ds((k % 2) * CHUNK, CHUNK)
        near, total = ((near_r, sum_r), (near_l, sum_l))[k // 2]
        s = own[rows, :].astype(F32) + near[side, :].astype(F32) + total[side, :].astype(F32)
        o[rows, :] = s.astype(BF)
        copies.append(pltpu.make_async_copy(o.at[rows, :], o_hbm.at[rows, :], sem.at[k]))
        copies[k].start()
    for c in copies:
        c.wait()


def last_call(*args):
    return pl.pallas_call(
        last_body,
        in_specs=[pl.BlockSpec(memory_space=pltpu.VMEM)] * len(args),
        out_specs=pl.BlockSpec(memory_space=pltpu.HBM),
        out_shape=jax.ShapeDtypeStruct((QOUT, TOK), BF),
        scratch_shapes=[pltpu.VMEM((QOUT, TOK), BF), pltpu.SemaphoreType.DMA((4,))],
        compiler_params=pltpu.CompilerParams(vmem_limit_bytes=VMEM_LIMIT),
        name="last",
    )(*args)


def seq_perm(v, y, z, core):
    return lax.ppermute(v, "seq", [(src, src ^ (y * 8 + z * 2 + core)) for src in range(32)])


def head_perm(v, shift):
    return lax.ppermute(v, "head", [(s, (s + shift) % 4) for s in range(4)])


def on_device(x_in, bc_in, z_in, dt_raw, a_log, conv_x, conv_bc, d_skip, norm_gain, out_weight):
    bc = bc_in.reshape(TOK, 256)
    hbm = lambda v: pltpu.with_memory_space_constraint(v, pltpu.HBM)
    edge = call(
        edge_body,
        "edge",
        (hbm(x_in), hbm(bc)),
        [((8, INNER + 256), BF)],
        spaces=[pltpu.HBM] * 2,
        scratch=[pltpu.SemaphoreType.DMA((2,))],
    )[0]
    halo = lax.ppermute(edge, "seq", [(s, (s + 1) % 32) for s in range(32)])
    xc, pst, dec, x0, end, b, L, step, tw0, b0, tw, bts, dtab = first_call(
        hbm(x_in), bc, conv_x, conv_bc, dt_raw, a_log.reshape(1, HEADS)
    )
    xc, b, ds, send, bt = second_call(halo, x0, b0, conv_x, conv_bc, tw0, end, dec, xc, b)
    recv = seq_perm(send, 0, 0, 1)
    xc, pst, dec, x0, end = rest_call(hbm(x_in), conv_x, tw, bts, dtab, xc, pst, dec, x0, send)
    xc, ds, keep = third_call(halo, x0, bt, conv_x, tw0, end, dec, xc, ds)
    piece = jax.ShapeDtypeStruct((WROWS, CHUNK), BF)
    plain = jax.ShapeDtypeStruct((STATE, CHUNK), BF)
    box = pltpu.VMEM((4, WROWS, CHUNK), F32)
    splits = (3, 3, 2)
    q = small_call(pair_body, "pair", (keep, recv), [piece] * 4)
    cm, sc, m2, tl, te, td = table_call(L, step, d_skip.reshape(1, HEADS), halo, bc, conv_bc, b, q[0])
    known = (xc, cm, sc, z_in, m2, tl, te, td, dec, pst, ds)
    work = lambda k, after, before: mix_call(sum(splits[:k]), splits[k], known, after, before)
    mixed = work(0, q[0], ())
    rows = [q[0]] + [seq_perm(q[i], 0, i, 0) for i in (1, 2, 3)]
    total, pre, dpre = small_call(
        row_body,
        "row",
        rows,
        [piece, jax.ShapeDtypeStruct((4, STATE, CHUNK), F32), jax.ShapeDtypeStruct((4, 8, CHUNK), F32)],
        [box],
        (mixed[0],),
    )
    mixed = work(1, total, mixed)
    cols = [total] + [seq_perm(total, i, 0, 0) for i in (1, 2, 3)]
    e = small_call(plane_body, "plane", (*cols, pre, dpre), [plain] * 4, [box], (mixed[0],))
    mixed = work(2, e[0], mixed)
    back = [e[0]] + [seq_perm(e[i], 0, i, 0) for i in (1, 2, 3)]
    half = jax.ShapeDtypeStruct((4, STATE, CHUNK), BF)
    give, stay = small_call(
        spread_body, "spread", (*back, keep, recv), [half] * 2, [pltpu.VMEM((4, STATE, CHUNK), F32)], (mixed[0],)
    )
    take = seq_perm(give, 0, 0, 1)
    gain = norm_gain.reshape(1, INNER)
    near, ss = near_gate_call(*mixed, cm, stay, gain, give)
    p = part_call(near, out_weight, ss)
    other, inv = far_gate_call(*mixed, cm, take, gain, ss, p)
    far_r, far_l = far_call(p, other, inv, out_weight)
    from_left, from_right = head_perm(far_r, 1), head_perm(far_l, -1)
    proj = lambda shift, side, after: proj_call(shift, side, near, other, inv, out_weight, after)
    right_l = proj(1, 1, far_r)
    near_l = head_perm(right_l, 1)
    left_r = proj(3, 0, right_l)
    near_r = head_perm(left_r, -1)
    right_r = proj(1, 0, left_r)
    left_l = proj(3, 1, right_r)
    shape = ((QOUT // 2, TOK), BF)
    sum_r = head_perm(call(relay_body, "relay", (right_r, from_left), [shape])[0], 1)
    sum_l = head_perm(call(relay_body, "relay", (left_l, from_right), [shape])[0], -1)
    own = proj(0, 2, left_l)
    return last_call(own, near_r, near_l, sum_r, sum_l)


def solution(mesh):
    placed = (
        P("seq", "head"),
        P("seq", "head", None),
        P("seq", "head"),
        P("head", "seq"),
        P("head"),
        P(None, "head"),
        P(None, "head", None),
        P("head"),
        P("head"),
        P("head", None),
    )
    return jax.shard_map(
        on_device, mesh=mesh, in_specs=placed, out_specs=P("head", "seq"), check_vma=False
    )
```

```python
import functools

import jax
import jax.numpy as jnp
from jax import lax
from jax.experimental import pallas as pl
from jax.experimental.pallas import tpu as pltpu
from jax.sharding import PartitionSpec as P

SPAN = 128
HEADS = 32
HD = 64
STATE = 128
TOK = 512
NB = 4
INNER = 2048
CHUNK = 256
NCH = INNER // CHUNK
EARLY = 5
HPC = CHUNK // HD
DOUT = 4096
QOUT = 1024
WROWS = 144
LOG2E = 1.4426950408889634
BF = jnp.bfloat16
F32 = jnp.float32
VMEM_LIMIT = 10 << 20


def silu(u):
    half = 0.5 * u
    return half + half * jnp.tanh(half)


def dot(a, b):
    return jnp.dot(a, b, preferred_element_type=F32)


def iota(shape, axis):
    return lax.broadcasted_iota(jnp.int32, shape, axis)


def onehot(first_head, width, lanes, low=0, high=128):
    k = iota((128, width), 0)
    h = first_head + (iota((128, width), 1) // lanes)
    hit = ((k & 31) == h) & (k >= low) & (k < high)
    return jnp.where(hit, 1.0, 0.0).astype(BF)


def split2(v):
    hi = v.astype(BF).astype(F32)
    return hi, (v - hi).astype(BF).astype(F32)


def column(row, n):
    eye = iota((n, n), 0) == iota((n, n), 1)
    return jnp.sum(jnp.where(eye, jnp.broadcast_to(row, (n, n)), 0.0), axis=1, keepdims=True)


def call(body, name, args, outs, spaces=(), scratch=(), cost=(10**6, 1 << 20, 0), aliases=None, limit=VMEM_LIMIT):
    specs = [pl.BlockSpec(memory_space=spaces[k] if k < len(spaces) else pltpu.VMEM) for k in range(len(args))]
    return pl.pallas_call(
        body,
        in_specs=specs,
        out_specs=[pl.BlockSpec(memory_space=pltpu.VMEM)] * len(outs),
        out_shape=[jax.ShapeDtypeStruct(s, d) for s, d in outs],
        scratch_shapes=list(scratch),
        input_output_aliases=aliases or {},
        compiler_params=pltpu.CompilerParams(vmem_limit_bytes=limit),
        cost_estimate=pl.CostEstimate(flops=cost[0], bytes_accessed=cost[1], transcendentals=cost[2]),
        name=name,
    )(*args)


def conv(window, taps, rows):
    u = taps[3] * window[8:]
    for k in range(3):
        u = u + taps[k] * pltpu.roll(window, 3 - k, 0)[8:]
    return silu(u)


def taps_of(ref, lanes):
    return [ref[k : k + 1, lanes] for k in range(4)]


def split3(v):
    hi = v.astype(BF).astype(F32)
    rest = v - hi
    mid = rest.astype(BF).astype(F32)
    return hi, mid, rest - mid


def spot():
    place = lax.axis_index("seq")
    return place & 1, (place >> 1) & 3, place >> 3, lax.axis_index("head")


def edge_body(x_ref, bc_ref, o, sem):
    a = pltpu.make_async_copy(x_ref.at[pl.ds(TOK - 8, 8), :], o.at[:, pl.ds(0, INNER)], sem.at[0])
    b = pltpu.make_async_copy(bc_ref.at[pl.ds(TOK - 8, 8), :], o.at[:, pl.ds(INNER, 256)], sem.at[1])
    a.start()
    b.start()
    a.wait()
    b.wait()


def halo_rows(h_ref, lanes):
    return jnp.where(lax.axis_index("seq") == 0, 0.0, h_ref[:, lanes].astype(F32))


def half_lanes(half, k, width=CHUNK):
    return pl.ds(pl.multiple_of(half * (INNER // 2) + k, 128), width)


def states(items, fetch, xv, cwx, tw, dtab, bts, wbuf, xw, xc_o, pst_o, end_o, dec_o, x0_o):
    nothing = jnp.zeros((8, 128), F32)
    count = len(items)
    head = lambda n: items[n][0] * (HEADS // 2) + items[n][1] * HPC
    spread = lambda n: dot(tw[...], onehot(head(n), CHUNK, HD, 0, 64))
    wbuf[0] = spread(0)
    for n in range(count + 1):
        if n < count:
            half, q = items[n]
            lanes = half_lanes(half, q * CHUNK)
            if n + 1 < count:
                wbuf[(n + 1) % 2] = spread(n + 1)
            dec_o[:, lanes] = dot(dtab[...], onehot(head(n), CHUNK, HD, 64, 128))
            if fetch:
                fetch[n].wait()
            x0_o[:, lanes] = xv[0:16, lanes]
        state = None
        for c in range(NB):
            if n < count:
                for r in (0, 64):
                    for l in (0, 128):
                        row = c * SPAN + r
                        part = half_lanes(half, q * CHUNK + l, 128)
                        if row == 0:
                            window = jnp.concatenate([nothing, xv[0:64, part].astype(F32)], axis=0)
                        else:
                            window = xv[pl.ds(row - 8, 72), part].astype(F32)
                        v = conv(window, taps_of(cwx, part), 64).astype(BF)
                        xc_o[pl.ds(row, 64), part] = v
                        w = wbuf[n % 2, pl.ds(row, 64), l : l + 128]
                        xw[n % 2, pl.ds(row, 64), l : l + 128] = (v.astype(F32) * w).astype(BF)
            if n > 0:
                before = half_lanes(items[n - 1][0], items[n - 1][1] * CHUNK)
                t = dot(bts[c], xw[(n - 1) % 2, pl.ds(c * SPAN, SPAN), :])
                state = t if c == 0 else dec_o[c : c + 1, before] * state + t
                if c < NB - 1:
                    pst_o[c, :, before] = state
                else:
                    end_o[n - 1] = state


def first_body(x_hbm, bv, cwx, cwb, dtv, alv,
               xc_o, pst_o, dec_o, x0_o, end_o, b_o, L_o, step_o, tw0_o, b0_o, tw, bts, dtab_o, xv,
               wbuf, xw, sem):
    core = spot()[0]
    order = [(1 - core, q) for q in range(4)] + [(core, q) for q in range(4)]
    copies = []
    for n, (half, q) in enumerate(order):
        lanes = half_lanes(half, q * CHUNK)
        copies.append(pltpu.make_async_copy(x_hbm.at[:, lanes], xv.at[:, lanes], sem.at[n]))
        copies[n].start()
    tri = jnp.where(iota((SPAN, SPAN), 0) <= iota((SPAN, SPAN), 1), 1.0, 0.0).astype(BF)
    v = dtv[...].astype(F32)
    t = jnp.exp(-jnp.abs(v))
    u = 1.0 + t
    d = u - 1.0
    flat = d == 0.0
    step = jnp.maximum(v, 0.0) + jnp.where(flat, t, jnp.log(u) * t / jnp.where(flat, 1.0, d))
    step_o[...] = step
    a = column(alv[...], HEADS)
    rate = jnp.concatenate(split3((-LOG2E * jnp.exp(a)) * step), axis=0).astype(BF)
    Ls, ends = [], []
    for c in range(NB):
        s = dot(rate[:, c * SPAN : (c + 1) * SPAN], tri)
        s = s[0:HEADS] + s[HEADS : 2 * HEADS] + s[2 * HEADS : 3 * HEADS]
        Ls.append(s)
        ends.append(jnp.broadcast_to(s[:, SPAN - 1 : SPAN], (HEADS, SPAN)))
    L = jnp.concatenate(Ls, axis=1)
    end = jnp.concatenate(ends, axis=1)
    L_o[...] = L
    w_hi, w_lo = split2(jnp.exp2(end - L) * step)
    d_hi, d_lo = split2(jnp.exp2(end))
    twt = jnp.transpose(jnp.concatenate([w_hi, w_lo, d_hi, d_lo], axis=0))
    tw[...] = twt.astype(BF)
    tw0_o[...] = twt[0:16].astype(BF)
    tw[pl.ds(0, 16), :] = jnp.zeros((16, 128), BF)
    rows = [twt[c * SPAN : c * SPAN + 1] for c in range(NB)]
    dtab = jnp.concatenate(rows + [jnp.zeros((12, SPAN), F32)], axis=0).astype(BF)
    dtab_o[...] = dtab
    b0_o[...] = bv[0:16, :STATE]
    btaps = [cwb[k][:, :STATE] for k in range(4)]
    nothing = jnp.zeros((8, STATE), F32)
    for c in range(NB):
        if c == 0:
            window = jnp.concatenate([nothing, bv[0:SPAN, :STATE].astype(F32)], axis=0)
        else:
            window = bv[pl.ds(c * SPAN - 8, SPAN + 8), :STATE].astype(F32)
        v = conv(window, btaps, SPAN)
        b_o[pl.ds(c * SPAN, SPAN), :] = v.astype(BF)
        bts[c] = jnp.transpose(v).astype(BF)
    states(order[:EARLY], copies, xv, cwx, tw, dtab_o, bts, wbuf, xw, xc_o, pst_o, end_o, dec_o, x0_o)
    for c in copies[EARLY:]:
        c.wait()


def rest_body(xv, cwx, tw, bts, dtab, xc_i, pst_i, dec_i, x0_i, after,
              xc_o, pst_o, dec_o, x0_o, end_o, wbuf, xw):
    core = spot()[0]
    items = [(core, q) for q in range(EARLY - 4, 4)]
    states(items, None, xv, cwx, tw, dtab, bts, wbuf, xw, xc_o, pst_o, end_o, dec_o, x0_o)


SHARED = [
    ((TOK, INNER), BF),
    ((NB - 1, STATE, INNER), F32),
    ((16, INNER), F32),
    ((16, INNER), BF),
]
ROOM = [
    pltpu.VMEM((2, TOK, CHUNK), F32),
    pltpu.VMEM((2, TOK, CHUNK), BF),
]


def first_call(x, bc, cwx, cwb, dt, al):
    return call(
        first_body,
        "first",
        (x, bc, cwx, cwb, dt, al),
        SHARED
        + [
            ((EARLY, STATE, CHUNK), F32),
            ((TOK, STATE), BF),
            ((HEADS, TOK), F32),
            ((HEADS, TOK), F32),
            ((16, 128), BF),
            ((16, STATE), BF),
            ((TOK, 128), BF),
            ((NB, STATE, SPAN), BF),
            ((16, 128), BF),
            ((TOK, INNER), BF),
        ],
        spaces=[pltpu.HBM],
        scratch=ROOM + [pltpu.SemaphoreType.DMA((NCH,))],
        cost=(10**5, 1 << 14, 0),
    )


def rest_call(x, cwx, tw, bts, dtab, xc, pst, dec, x0, after):
    return call(
        rest_body,
        "rest",
        (x, cwx, tw, bts, dtab, xc, pst, dec, x0, after),
        SHARED + [((NCH - EARLY, STATE, CHUNK), F32)],
        spaces=[pltpu.VMEM] * 9 + [pl.ANY],
        scratch=ROOM,
        aliases={5: 0, 6: 1, 7: 2, 8: 3},
        cost=(10**5, 1 << 14, 0),
    )


def wire_rows(decay):
    hi, lo = split2(decay)
    return jnp.concatenate([hi, lo, jnp.zeros((14, decay.shape[1]), F32)], axis=0)


def correct(half, bt, h_ref, x0_ref, cwx_ref, tw0_ref, ends, dec_ref, xc_o, ds_o, emit):
    for q in range(4):
        lanes = half_lanes(half, q * CHUNK)
        window = jnp.concatenate([halo_rows(h_ref, lanes), x0_ref[:, lanes].astype(F32)], axis=0)
        u = conv(window, taps_of(cwx_ref, lanes), 16).astype(BF)
        xc_o[0:16, lanes] = u
        w = dot(tw0_ref[...], onehot(half * (HEADS // 2) + q * HPC, CHUNK, HD, 0, 64))
        xw = jnp.concatenate([u.astype(F32) * w, jnp.zeros((SPAN - 16, CHUNK), F32)], axis=0).astype(BF)
        fix = dot(bt, xw)
        ds_o[:, lanes] = fix
        dec = dec_ref[0:8, lanes]
        after = dec[1:2] * dec[2:3] * dec[3:4]
        ref, n = ends[q]
        emit(q, ref[n] + after * fix, dec[0:1] * after)


def second_body(h_ref, x0_ref, b0_ref, cwx_ref, cwb_ref, tw0_ref, end_ref, dec_ref, xc_in, b_in,
                xc_o, b_o, ds_o, send_o, bt_o):
    v = jnp.concatenate([halo_rows(h_ref, pl.ds(INNER, STATE)), b0_ref[...].astype(F32)], axis=0)
    v = conv(v, [cwb_ref[k][:, :STATE] for k in range(4)], 16)
    b_o[0:16, :] = v.astype(BF)
    bt = jnp.transpose(jnp.concatenate([v, jnp.zeros((SPAN - 16, STATE), F32)], axis=0)).astype(BF)
    bt_o[...] = bt

    def emit(q, state, decay):
        send_o[q, 0:STATE, :] = state.astype(BF)
        send_o[q, STATE:WROWS, :] = wire_rows(decay).astype(BF)

    correct(1 - spot()[0], bt, h_ref, x0_ref, cwx_ref, tw0_ref, [(end_ref, q) for q in range(4)], dec_ref, xc_o, ds_o, emit)


def third_body(h_ref, x0_ref, bt_ref, cwx_ref, tw0_ref, end_ref, late_ref, dec_ref, xc_in, ds_in, xc_o, ds_o, keep_o):
    def emit(q, state, decay):
        keep_o[q, 0:STATE, :] = state
        keep_o[q, STATE:WROWS, :] = jnp.concatenate([decay, jnp.zeros((15, CHUNK), F32)], axis=0)

    ends = [(end_ref, 4 + q) if 4 + q < EARLY else (late_ref, 4 + q - EARLY) for q in range(4)]
    correct(spot()[0], bt_ref[...], h_ref, x0_ref, cwx_ref, tw0_ref, ends, dec_ref, xc_o, ds_o, emit)


def second_call(halo, x0, b0, cwx, cwb, tw0, end, dec, xc, b):
    return call(
        second_body,
        "second",
        (halo, x0, b0, cwx, cwb, tw0, end, dec, xc, b),
        [
            ((TOK, INNER), BF),
            ((TOK, STATE), BF),
            ((STATE, INNER), F32),
            ((4, WROWS, CHUNK), BF),
            ((STATE, 128), BF),
        ],
        aliases={8: 0, 9: 1},
        cost=(10**5, 1 << 14, 0),
    )


def third_call(halo, x0, bt, cwx, tw0, end, late, dec, xc, ds):
    return call(
        third_body,
        "third",
        (halo, x0, bt, cwx, tw0, end, late, dec, xc, ds),
        [((TOK, INNER), BF), ((STATE, INNER), F32), ((4, WROWS, CHUNK), F32)],
        aliases={8: 0, 9: 1},
        cost=(10**5, 1 << 14, 0),
    )


def table_body(L_ref, step_ref, ds_ref, h_ref, bc_ref, cwb_ref, b_ref, after_ref,
               c_o, sc_o, m2_o, tl_o, te_o, td_o, buf):
    L = L_ref[...]
    M = jnp.log(step_ref[...]) * LOG2E - L
    for j in range(NCH):
        m2_o[j, 0:HPC, :] = M[j * HPC : (j + 1) * HPC, :]
    zero = jnp.zeros((HEADS, TOK), F32)
    tl_o[...] = jnp.transpose(jnp.concatenate([*split3(L), zero], axis=0)).astype(BF)
    parts, before = [], jnp.zeros((HEADS, SPAN), F32)
    for c in range(NB):
        s = L[:, c * SPAN : (c + 1) * SPAN]
        parts.append(before + s)
        before = before + jnp.broadcast_to(s[:, SPAN - 1 : SPAN], (HEADS, SPAN))
    e = [*split2(jnp.exp2(L)), *split2(jnp.exp2(jnp.concatenate(parts, axis=1)))]
    te_o[...] = jnp.transpose(jnp.concatenate(e, axis=0)).astype(BF)
    d = [jnp.broadcast_to(p, (HEADS, SPAN)) for p in split2(column(ds_ref[...], HEADS))]
    d = jnp.concatenate([*d, jnp.zeros((2 * HEADS, SPAN), F32)], axis=0)
    td_o[...] = jnp.transpose(d)[0:16].astype(BF)
    buf[pl.ds(0, 8), :] = halo_rows(h_ref, pl.ds(INNER + STATE, STATE))
    buf[pl.ds(8, TOK), :] = bc_ref[:, STATE:].astype(F32)
    taps = [cwb_ref[k][:, STATE:] for k in range(4)]
    causal = iota((SPAN, SPAN), 0) >= iota((SPAN, SPAN), 1)
    for c in range(NB):
        rows = pl.ds(c * SPAN, SPAN)
        v = conv(buf[pl.ds(c * SPAN, SPAN + 8), :], taps, SPAN).astype(BF)
        c_o[rows, :] = v
        s = lax.dot_general(v, b_ref[rows, :], (((1,), (1,)), ((), ())), preferred_element_type=F32)
        sc_o[c] = jnp.where(causal, s, 0.0)


def table_call(L, step, ds, halo, bc, cwb, b, after):
    return call(
        table_body,
        "table",
        (L, step, ds, halo, bc, cwb, b, after),
        [
            ((TOK, STATE), BF),
            ((NB, SPAN, SPAN), F32),
            ((NCH, 8, TOK), F32),
            ((TOK, 128), BF),
            ((TOK, 128), BF),
            ((16, 128), BF),
        ],
        spaces=[pltpu.VMEM] * 7 + [pl.ANY],
        scratch=[pltpu.VMEM((TOK + 8, STATE), F32)],
        cost=(10**8, 2 << 20, 10**5),
    )


def decay_of(v):
    return v[STATE : STATE + 1] + v[STATE + 1 : STATE + 2]


def small_call(body, name, args, outs, scratch=(), after=()):
    n = len(args)
    m = len(after)

    def run(*refs):
        body(*refs[:n], *refs[n + m :])

    return call(
        run,
        name,
        (*args, *after),
        [(o.shape, o.dtype) for o in outs],
        spaces=[pltpu.VMEM] * n + [pl.ANY] * m,
        scratch=scratch,
    )


def pair_body(keep_ref, recv_ref, *outs):
    core, z = spot()[:2]
    for i in range(4):
        q = z ^ i
        own = keep_ref[q]
        other = recv_ref[q].astype(F32)
        early = jnp.where(core == 0, own, other)
        late = jnp.where(core == 0, other, own)
        d_early, d_late = decay_of(early), decay_of(late)
        outs[i][0:STATE, :] = (d_late * early[0:STATE] + late[0:STATE]).astype(BF)
        outs[i][STATE:WROWS, :] = wire_rows(d_early * d_late).astype(BF)


def row_body(r0, r1, r2, r3, total_o, pre_o, dpre_o, box):
    z = spot()[1]
    for i, r in enumerate((r0, r1, r2, r3)):
        box[z ^ i] = r[...].astype(F32)
    state = jnp.zeros((STATE, CHUNK), F32)
    decay = jnp.ones((1, CHUNK), F32)
    for k in range(4):
        pre_o[k] = state
        dpre_o[k] = jnp.broadcast_to(decay, (8, CHUNK))
        v = box[k]
        d = decay_of(v)
        state = d * state + v[0:STATE]
        decay = decay * d
    total_o[0:STATE, :] = state.astype(BF)
    total_o[STATE:WROWS, :] = wire_rows(decay).astype(BF)


def plane_body(r0, r1, r2, r3, pre_ref, dpre_ref, o0, o1, o2, o3, box):
    z, y = spot()[1:3]
    for i, r in enumerate((r0, r1, r2, r3)):
        box[y ^ i] = r[...].astype(F32)
    state = jnp.zeros((STATE, CHUNK), F32)
    for k in range(3):
        v = box[k]
        state = jnp.where(k < y, decay_of(v) * state + v[0:STATE], state)
    for i, o in enumerate((o0, o1, o2, o3)):
        q = z ^ i
        d = dpre_ref[q]
        o[...] = (pre_ref[q] + d[0:1] * state).astype(BF)


def spread_body(r0, r1, r2, r3, keep_ref, recv_ref, send_o, stay_o, box):
    core, z = spot()[:2]
    for i, r in enumerate((r0, r1, r2, r3)):
        box[z ^ i] = r[...].astype(F32)
    for q in range(4):
        early = jnp.where(core == 0, keep_ref[q], recv_ref[q].astype(F32))
        a = box[q]
        b = decay_of(early) * a + early[0:STATE]
        send_o[q] = jnp.where(core == 0, b, a).astype(BF)
        stay_o[q] = jnp.where(core == 0, a, b).astype(BF)


def mix_body(first_chunk, chunks, xc_ref, c_ref, sc_ref, z_ref, m2_ref, tl_ref, te_ref, td_ref, dec_ref, pst_ref,
             ds_ref, *rest):
    yg_o, g2_o, ex, ee = rest[-4:]
    left = iota((SPAN, SPAN), 1) < HD

    def expand(k):
        j = first_chunk + k
        ex[k % 2] = dot(tl_ref[...], onehot(j * HPC, HPC * SPAN, SPAN))
        ee[k % 2, :, 0:CHUNK] = dot(te_ref[...], onehot(j * HPC, CHUNK, HD, 0, 64))
        ee[k % 2, :, CHUNK:] = dot(te_ref[...], onehot(j * HPC, CHUNK, HD, 64, 128))

    expand(0)
    for k in range(chunks):
        j = first_chunk + k
        lanes = pl.ds(j * CHUNK, CHUNK)
        if k + 1 < chunks:
            expand(k + 1)
        skip = dot(td_ref[...], onehot(j * HPC, CHUNK, HD))[0:1]
        fix = ds_ref[:, lanes]
        for c in range(NB):
            rows = pl.ds(c * SPAN, SPAN)
            s = sc_ref[c]
            x = xc_ref[rows, lanes]
            parts = []
            for h in range(HPC):
                m2 = m2_ref[j, h : h + 1, c * SPAN : (c + 1) * SPAN]
                e = ex[k % 2, rows, h * SPAN : (h + 1) * SPAN] + m2
                parts.append((s * jnp.exp2(jnp.minimum(e, 8.0))).astype(BF))
            ys = []
            for p in range(HPC // 2):
                xp = x[:, p * SPAN : (p + 1) * SPAN].astype(F32)
                rhs = jnp.concatenate([jnp.where(left, xp, 0.0), jnp.where(left, 0.0, xp)], axis=0).astype(BF)
                ys.append(dot(jnp.concatenate([parts[2 * p], parts[2 * p + 1]], axis=1), rhs))
            y = jnp.concatenate(ys, axis=1) + skip * x.astype(F32)
            if c > 0:
                if c > 1:
                    fix = dec_ref[c - 1 : c, lanes] * fix
                ent = (pst_ref[c - 1, :, lanes] + fix).astype(BF)
                y = y + ee[k % 2, rows, 0:CHUNK] * dot(c_ref[rows, :], ent)
            gate = silu(z_ref[rows, lanes].astype(F32))
            yg_o[rows, lanes] = (y * gate).astype(BF)
            g2_o[rows, lanes] = (ee[k % 2, rows, CHUNK:] * gate).astype(BF)


def mix_call(first_chunk, chunks, args, after, before):
    n = len(args)
    return call(
        functools.partial(mix_body, first_chunk, chunks),
        "mix",
        (*args, after, *before),
        [((TOK, INNER), BF)] * 2,
        spaces=[pltpu.VMEM] * n + [pl.ANY],
        scratch=[pltpu.VMEM((2, TOK, HPC * SPAN), F32), pltpu.VMEM((2, TOK, 2 * CHUNK), F32)],
        aliases={n + 1: 0, n + 2: 1} if before else None,
        cost=(chunks * 25 * 10**7, chunks << 20, chunks * 6 * 10**5),
    )


def gated(yg_ref, g2_ref, c_ref, e_ref, gain_ref, half, blocks, n_o, ce, sums):
    at = lambda q: pl.ds(pl.multiple_of(half * (INNER // 2) + q * CHUNK, CHUNK), CHUNK)

    def carry(q):
        ce[q % 2] = dot(c_ref[...], e_ref[q])

    carry(0)
    for q in range(4):
        lanes = at(q)
        if q < 3:
            carry(q + 1)
        gain = gain_ref[:, lanes]
        for c in range(blocks):
            rows = pl.ds(c * SPAN, SPAN)
            g = yg_ref[rows, lanes].astype(F32) + ce[q % 2, rows, :] * g2_ref[rows, lanes].astype(F32)
            sq = g * g
            sq = sq[:, :128] + sq[:, 128:]
            sums[c] = sq if sums[c] is None else sums[c] + sq
            n_o[rows, q * CHUNK : (q + 1) * CHUNK] = (g * gain).astype(BF)


def near_gate_body(yg_ref, g2_ref, c_ref, e_ref, gain_ref, after_ref, n_o, ss_o, ce):
    sums = [None] * NB
    gated(yg_ref, g2_ref, c_ref, e_ref, gain_ref, spot()[0], NB, n_o, ce, sums)
    for c in range(NB):
        ss_o[pl.ds(c * SPAN, SPAN), :] = sums[c]


def far_gate_body(yg_ref, g2_ref, c_ref, e_ref, gain_ref, ss_ref, after_ref, n_o, inv_o, ce):
    sums = [ss_ref[pl.ds(c * SPAN, SPAN), :] for c in range(NB)]
    gated(yg_ref, g2_ref, c_ref, e_ref, gain_ref, 1 - spot()[0], NB, n_o, ce, sums)
    for c in range(NB):
        m = jnp.sum(sums[c], axis=1, keepdims=True) * (1.0 / INNER)
        inv_o[pl.ds(c * SPAN, SPAN), :] = jnp.broadcast_to(lax.rsqrt(m + 1e-05), (SPAN, 128))


def near_gate_call(yg, g2, cm, e, gain, after):
    return call(
        near_gate_body,
        "gate",
        (yg, g2, cm, e, gain, after),
        [((TOK, INNER // 2), BF), ((TOK, 128), F32)],
        spaces=[pltpu.VMEM] * 5 + [pl.ANY],
        scratch=[pltpu.VMEM((2, TOK, CHUNK), F32)],
        cost=(25 * 10**7, 4 << 20, 0),
    )


def far_gate_call(yg, g2, cm, e, gain, ss, after):
    return call(
        far_gate_body,
        "gate",
        (yg, g2, cm, e, gain, ss, after),
        [((TOK, INNER // 2), BF), ((TOK, 128), F32)],
        spaces=[pltpu.VMEM] * 6 + [pl.ANY],
        scratch=[pltpu.VMEM((2, TOK, CHUNK), F32)],
        cost=(25 * 10**7, 4 << 20, 0),
    )


def weight_block(w_ref, half, shift, k):
    lane = lax.rem(spot()[3] + shift, 4) * QOUT + k * CHUNK
    rows = pl.ds(pl.multiple_of(half * (INNER // 2), INNER // 2), INNER // 2)
    return w_ref[rows, pl.ds(pl.multiple_of(lane, CHUNK), CHUNK)]


def part_body(n_ref, w_ref, after_ref, p_o):
    core = spot()[0]
    for k in range(QOUT // CHUNK):
        p_o[:, k * CHUNK : (k + 1) * CHUNK] = dot(n_ref[...], weight_block(w_ref, core, 2, k))


def far_body(p_ref, n_ref, inv_ref, w_ref, r_o, l_o):
    core = spot()[0]
    for k in range(QOUT // CHUNK):
        y = p_ref[:, k * CHUNK : (k + 1) * CHUNK] + dot(n_ref[...], weight_block(w_ref, 1 - core, 2, k))
        o = (r_o, l_o)[k // 2]
        o[pl.ds((k % 2) * CHUNK, CHUNK), :] = jnp.transpose(y * inv_ref[:, 0:1]).astype(BF)


def proj_body(shift, first, count, near_ref, n_ref, inv_ref, w_ref, after_ref, o):
    core = spot()[0]
    for k in range(count):
        y = dot(near_ref[...], weight_block(w_ref, core, shift, first + k))
        y = y + dot(n_ref[...], weight_block(w_ref, 1 - core, shift, first + k))
        o[pl.ds(k * CHUNK, CHUNK), :] = jnp.transpose(y * inv_ref[:, 0:1]).astype(BF)


def part_call(near, w, after):
    return call(
        part_body,
        "part",
        (near, w, after),
        [((TOK, QOUT), F32)],
        spaces=[pltpu.VMEM] * 2 + [pl.ANY],
        cost=(TOK * INNER * QOUT, 5 << 20, 0),
    )[0]


def far_call(p, n, inv, w):
    return call(
        far_body,
        "far",
        (p, n, inv, w),
        [((QOUT // 2, TOK), BF)] * 2,
        cost=(TOK * INNER * QOUT, 5 << 20, 0),
    )


def proj_call(shift, side, near, n, inv, w, after):
    count = 2 if side < 2 else 4
    return call(
        functools.partial(proj_body, shift, 2 * side if side < 2 else 0, count),
        "proj",
        (near, n, inv, w, after),
        [((count * CHUNK, TOK), BF)],
        spaces=[pltpu.VMEM] * 4 + [pl.ANY],
        cost=(2 * TOK * INNER * count * CHUNK, 5 << 20, 0),
    )[0]


def relay_body(mine, a, o):
    o[...] = (mine[...].astype(F32) + a[...].astype(F32)).astype(BF)


def last_body(own, near_r, near_l, sum_r, sum_l, o_hbm, o, sem):
    copies = []
    for k in range(4):
        rows = pl.ds(k * CHUNK, CHUNK)
        side = pl.ds((k % 2) * CHUNK, CHUNK)
        near, total = ((near_r, sum_r), (near_l, sum_l))[k // 2]
        s = own[rows, :].astype(F32) + near[side, :].astype(F32) + total[side, :].astype(F32)
        o[rows, :] = s.astype(BF)
        copies.append(pltpu.make_async_copy(o.at[rows, :], o_hbm.at[rows, :], sem.at[k]))
        copies[k].start()
    for c in copies:
        c.wait()


def last_call(*args):
    return pl.pallas_call(
        last_body,
        in_specs=[pl.BlockSpec(memory_space=pltpu.VMEM)] * len(args),
        out_specs=pl.BlockSpec(memory_space=pltpu.HBM),
        out_shape=jax.ShapeDtypeStruct((QOUT, TOK), BF),
        scratch_shapes=[pltpu.VMEM((QOUT, TOK), BF), pltpu.SemaphoreType.DMA((4,))],
        compiler_params=pltpu.CompilerParams(vmem_limit_bytes=VMEM_LIMIT),
        name="last",
    )(*args)


def seq_perm(v, y, z, core):
    return lax.ppermute(v, "seq", [(src, src ^ (y * 8 + z * 2 + core)) for src in range(32)])


def head_perm(v, shift):
    return lax.ppermute(v, "head", [(s, (s + shift) % 4) for s in range(4)])


def on_device(x_in, bc_in, z_in, dt_raw, a_log, conv_x, conv_bc, d_skip, norm_gain, out_weight):
    bc = bc_in.reshape(TOK, 256)
    hbm = lambda v: pltpu.with_memory_space_constraint(v, pltpu.HBM)
    edge = call(
        edge_body,
        "edge",
        (hbm(x_in), hbm(bc)),
        [((8, INNER + 256), BF)],
        spaces=[pltpu.HBM] * 2,
        scratch=[pltpu.SemaphoreType.DMA((2,))],
    )[0]
    halo = lax.ppermute(edge, "seq", [(s, (s + 1) % 32) for s in range(32)])
    xc, pst, dec, x0, end, b, L, step, tw0, b0, tw, bts, dtab, xv = first_call(
        hbm(x_in), bc, conv_x, conv_bc, dt_raw, a_log.reshape(1, HEADS)
    )
    xc, b, ds, send, bt = second_call(halo, x0, b0, conv_x, conv_bc, tw0, end, dec, xc, b)
    recv = seq_perm(send, 0, 0, 1)
    xc, pst, dec, x0, late = rest_call(xv, conv_x, tw, bts, dtab, xc, pst, dec, x0, send)
    xc, ds, keep = third_call(halo, x0, bt, conv_x, tw0, end, late, dec, xc, ds)
    piece = jax.ShapeDtypeStruct((WROWS, CHUNK), BF)
    plain = jax.ShapeDtypeStruct((STATE, CHUNK), BF)
    box = pltpu.VMEM((4, WROWS, CHUNK), F32)
    splits = (3, 3, 2)
    q = small_call(pair_body, "pair", (keep, recv), [piece] * 4)
    cm, sc, m2, tl, te, td = table_call(L, step, d_skip.reshape(1, HEADS), halo, bc, conv_bc, b, q[0])
    known = (xc, cm, sc, z_in, m2, tl, te, td, dec, pst, ds)
    work = lambda k, after, before: mix_call(sum(splits[:k]), splits[k], known, after, before)
    mixed = work(0, q[0], ())
    rows = [q[0]] + [seq_perm(q[i], 0, i, 0) for i in (1, 2, 3)]
    total, pre, dpre = small_call(
        row_body,
        "row",
        rows,
        [piece, jax.ShapeDtypeStruct((4, STATE, CHUNK), F32), jax.ShapeDtypeStruct((4, 8, CHUNK), F32)],
        [box],
        (mixed[0],),
    )
    mixed = work(1, total, mixed)
    cols = [total] + [seq_perm(total, i, 0, 0) for i in (1, 2, 3)]
    e = small_call(plane_body, "plane", (*cols, pre, dpre), [plain] * 4, [box], (mixed[0],))
    mixed = work(2, e[0], mixed)
    back = [e[0]] + [seq_perm(e[i], 0, i, 0) for i in (1, 2, 3)]
    half = jax.ShapeDtypeStruct((4, STATE, CHUNK), BF)
    give, stay = small_call(
        spread_body, "spread", (*back, keep, recv), [half] * 2, [pltpu.VMEM((4, STATE, CHUNK), F32)], (mixed[0],)
    )
    take = seq_perm(give, 0, 0, 1)
    gain = norm_gain.reshape(1, INNER)
    near, ss = near_gate_call(*mixed, cm, stay, gain, give)
    p = part_call(near, out_weight, ss)
    other, inv = far_gate_call(*mixed, cm, take, gain, ss, p)
    far_r, far_l = far_call(p, other, inv, out_weight)
    from_left, from_right = head_perm(far_r, 1), head_perm(far_l, -1)
    proj = lambda shift, side, after: proj_call(shift, side, near, other, inv, out_weight, after)
    right_l = proj(1, 1, far_r)
    near_l = head_perm(right_l, 1)
    left_r = proj(3, 0, right_l)
    near_r = head_perm(left_r, -1)
    right_r = proj(1, 0, left_r)
    left_l = proj(3, 1, right_r)
    shape = ((QOUT // 2, TOK), BF)
    sum_r = head_perm(call(relay_body, "relay", (right_r, from_left), [shape])[0], 1)
    sum_l = head_perm(call(relay_body, "relay", (left_l, from_right), [shape])[0], -1)
    own = proj(0, 2, left_l)
    return last_call(own, near_r, near_l, sum_r, sum_l)


def solution(mesh):
    placed = (
        P("seq", "head"),
        P("seq", "head", None),
        P("seq", "head"),
        P("head", "seq"),
        P("head"),
        P(None, "head"),
        P(None, "head", None),
        P("head"),
        P("head"),
        P("head", None),
    )
    return jax.shard_map(
        on_device, mesh=mesh, in_specs=placed, out_specs=P("head", "seq"), check_vma=False
    )
```

```python
import functools

import jax
import jax.numpy as jnp
from jax import lax
from jax.experimental import pallas as pl
from jax.experimental.pallas import tpu as pltpu
from jax.sharding import PartitionSpec as P

SPAN = 128
HEADS = 32
HD = 64
STATE = 128
TOK = 512
NB = 4
INNER = 2048
CHUNK = 256
NCH = INNER // CHUNK
EARLY = 6
HPC = CHUNK // HD
DOUT = 4096
QOUT = 1024
WROWS = 144
LOG2E = 1.4426950408889634
BF = jnp.bfloat16
F32 = jnp.float32
VMEM_LIMIT = 10 << 20


def silu(u):
    half = 0.5 * u
    return half + half * jnp.tanh(half)


def dot(a, b):
    return jnp.dot(a, b, preferred_element_type=F32)


def iota(shape, axis):
    return lax.broadcasted_iota(jnp.int32, shape, axis)


def onehot(first_head, width, lanes, low=0, high=128):
    k = iota((128, width), 0)
    h = first_head + (iota((128, width), 1) // lanes)
    hit = ((k & 31) == h) & (k >= low) & (k < high)
    return jnp.where(hit, 1.0, 0.0).astype(BF)


def split2(v):
    hi = v.astype(BF).astype(F32)
    return hi, (v - hi).astype(BF).astype(F32)


def column(row, n):
    eye = iota((n, n), 0) == iota((n, n), 1)
    return jnp.sum(jnp.where(eye, jnp.broadcast_to(row, (n, n)), 0.0), axis=1, keepdims=True)


def call(body, name, args, outs, spaces=(), scratch=(), cost=(10**6, 1 << 20, 0), aliases=None, limit=VMEM_LIMIT):
    specs = [pl.BlockSpec(memory_space=spaces[k] if k < len(spaces) else pltpu.VMEM) for k in range(len(args))]
    return pl.pallas_call(
        body,
        in_specs=specs,
        out_specs=[pl.BlockSpec(memory_space=pltpu.VMEM)] * len(outs),
        out_shape=[jax.ShapeDtypeStruct(s, d) for s, d in outs],
        scratch_shapes=list(scratch),
        input_output_aliases=aliases or {},
        compiler_params=pltpu.CompilerParams(vmem_limit_bytes=limit),
        cost_estimate=pl.CostEstimate(flops=cost[0], bytes_accessed=cost[1], transcendentals=cost[2]),
        name=name,
    )(*args)


def conv(window, taps, rows):
    u = taps[3] * window[8:]
    for k in range(3):
        u = u + taps[k] * pltpu.roll(window, 3 - k, 0)[8:]
    return silu(u)


def taps_of(ref, lanes):
    return [ref[k : k + 1, lanes] for k in range(4)]


def split3(v):
    hi = v.astype(BF).astype(F32)
    rest = v - hi
    mid = rest.astype(BF).astype(F32)
    return hi, mid, rest - mid


def spot():
    place = lax.axis_index("seq")
    return place & 1, (place >> 1) & 3, place >> 3, lax.axis_index("head")


def edge_body(x_ref, bc_ref, o, sem):
    a = pltpu.make_async_copy(x_ref.at[pl.ds(TOK - 8, 8), :], o.at[:, pl.ds(0, INNER)], sem.at[0])
    b = pltpu.make_async_copy(bc_ref.at[pl.ds(TOK - 8, 8), :], o.at[:, pl.ds(INNER, 256)], sem.at[1])
    a.start()
    b.start()
    a.wait()
    b.wait()


def halo_rows(h_ref, lanes):
    return jnp.where(lax.axis_index("seq") == 0, 0.0, h_ref[:, lanes].astype(F32))


def half_lanes(half, k, width=CHUNK):
    return pl.ds(pl.multiple_of(half * (INNER // 2) + k, 128), width)


def states(items, fetch, xv, cwx, tw, dtab, bts, wbuf, xw, xc_o, pst_o, end_o, dec_o, x0_o):
    nothing = jnp.zeros((8, 128), F32)
    count = len(items)
    head = lambda n: items[n][0] * (HEADS // 2) + items[n][1] * HPC
    spread = lambda n: dot(tw[...], onehot(head(n), CHUNK, HD, 0, 64))
    wbuf[0] = spread(0)
    for n in range(count + 1):
        if n < count:
            half, q = items[n]
            lanes = half_lanes(half, q * CHUNK)
            if n + 1 < count:
                wbuf[(n + 1) % 2] = spread(n + 1)
            dec_o[:, lanes] = dot(dtab[...], onehot(head(n), CHUNK, HD, 64, 128))
            if fetch:
                fetch[n].wait()
            x0_o[:, lanes] = xv[0:16, lanes]
        state = None
        for c in range(NB):
            if n < count:
                for r in (0, 64):
                    for l in (0, 128):
                        row = c * SPAN + r
                        part = half_lanes(half, q * CHUNK + l, 128)
                        if row == 0:
                            window = jnp.concatenate([nothing, xv[0:64, part].astype(F32)], axis=0)
                        else:
                            window = xv[pl.ds(row - 8, 72), part].astype(F32)
                        v = conv(window, taps_of(cwx, part), 64).astype(BF)
                        xc_o[pl.ds(row, 64), part] = v
                        w = wbuf[n % 2, pl.ds(row, 64), l : l + 128]
                        xw[n % 2, pl.ds(row, 64), l : l + 128] = (v.astype(F32) * w).astype(BF)
            if n > 0:
                before = half_lanes(items[n - 1][0], items[n - 1][1] * CHUNK)
                t = dot(bts[c], xw[(n - 1) % 2, pl.ds(c * SPAN, SPAN), :])
                state = t if c == 0 else dec_o[c : c + 1, before] * state + t
                if c < NB - 1:
                    pst_o[c, :, before] = state
                else:
                    end_o[n - 1] = state


def first_body(x_hbm, bv, cwx, cwb, dtv, alv,
               xc_o, pst_o, dec_o, x0_o, end_o, b_o, L_o, step_o, tw0_o, b0_o, tw, bts, dtab_o, xv,
               wbuf, xw, sem):
    core = spot()[0]
    order = [(1 - core, q) for q in range(4)] + [(core, q) for q in range(4)]
    copies = []
    for n, (half, q) in enumerate(order):
        lanes = half_lanes(half, q * CHUNK)
        copies.append(pltpu.make_async_copy(x_hbm.at[:, lanes], xv.at[:, lanes], sem.at[n]))
        copies[n].start()
    tri = jnp.where(iota((SPAN, SPAN), 0) <= iota((SPAN, SPAN), 1), 1.0, 0.0).astype(BF)
    v = dtv[...].astype(F32)
    t = jnp.exp(-jnp.abs(v))
    u = 1.0 + t
    d = u - 1.0
    flat = d == 0.0
    step = jnp.maximum(v, 0.0) + jnp.where(flat, t, jnp.log(u) * t / jnp.where(flat, 1.0, d))
    step_o[...] = step
    a = column(alv[...], HEADS)
    rate = jnp.concatenate(split3((-LOG2E * jnp.exp(a)) * step), axis=0).astype(BF)
    Ls, ends = [], []
    for c in range(NB):
        s = dot(rate[:, c * SPAN : (c + 1) * SPAN], tri)
        s = s[0:HEADS] + s[HEADS : 2 * HEADS] + s[2 * HEADS : 3 * HEADS]
        Ls.append(s)
        ends.append(jnp.broadcast_to(s[:, SPAN - 1 : SPAN], (HEADS, SPAN)))
    L = jnp.concatenate(Ls, axis=1)
    end = jnp.concatenate(ends, axis=1)
    L_o[...] = L
    w_hi, w_lo = split2(jnp.exp2(end - L) * step)
    d_hi, d_lo = split2(jnp.exp2(end))
    twt = jnp.transpose(jnp.concatenate([w_hi, w_lo, d_hi, d_lo], axis=0))
    tw[...] = twt.astype(BF)
    tw0_o[...] = twt[0:16].astype(BF)
    tw[pl.ds(0, 16), :] = jnp.zeros((16, 128), BF)
    rows = [twt[c * SPAN : c * SPAN + 1] for c in range(NB)]
    dtab = jnp.concatenate(rows + [jnp.zeros((12, SPAN), F32)], axis=0).astype(BF)
    dtab_o[...] = dtab
    b0_o[...] = bv[0:16, :STATE]
    btaps = [cwb[k][:, :STATE] for k in range(4)]
    nothing = jnp.zeros((8, STATE), F32)
    for c in range(NB):
        if c == 0:
            window = jnp.concatenate([nothing, bv[0:SPAN, :STATE].astype(F32)], axis=0)
        else:
            window = bv[pl.ds(c * SPAN - 8, SPAN + 8), :STATE].astype(F32)
        v = conv(window, btaps, SPAN)
        b_o[pl.ds(c * SPAN, SPAN), :] = v.astype(BF)
        bts[c] = jnp.transpose(v).astype(BF)
    states(order[:EARLY], copies, xv, cwx, tw, dtab_o, bts, wbuf, xw, xc_o, pst_o, end_o, dec_o, x0_o)
    for c in copies[EARLY:]:
        c.wait()


def rest_body(xv, cwx, tw, bts, dtab, xc_i, pst_i, dec_i, x0_i, after,
              xc_o, pst_o, dec_o, x0_o, end_o, wbuf, xw):
    core = spot()[0]
    items = [(core, q) for q in range(EARLY - 4, 4)]
    states(items, None, xv, cwx, tw, dtab, bts, wbuf, xw, xc_o, pst_o, end_o, dec_o, x0_o)


SHARED = [
    ((TOK, INNER), BF),
    ((NB - 1, STATE, INNER), F32),
    ((16, INNER), F32),
    ((16, INNER), BF),
]
ROOM = [
    pltpu.VMEM((2, TOK, CHUNK), F32),
    pltpu.VMEM((2, TOK, CHUNK), BF),
]


def first_call(x, bc, cwx, cwb, dt, al):
    return call(
        first_body,
        "first",
        (x, bc, cwx, cwb, dt, al),
        SHARED
        + [
            ((EARLY, STATE, CHUNK), F32),
            ((TOK, STATE), BF),
            ((HEADS, TOK), F32),
            ((HEADS, TOK), F32),
            ((16, 128), BF),
            ((16, STATE), BF),
            ((TOK, 128), BF),
            ((NB, STATE, SPAN), BF),
            ((16, 128), BF),
            ((TOK, INNER), BF),
        ],
        spaces=[pltpu.HBM],
        scratch=ROOM + [pltpu.SemaphoreType.DMA((NCH,))],
        cost=(10**5, 1 << 14, 0),
    )


def rest_call(x, cwx, tw, bts, dtab, xc, pst, dec, x0, after):
    return call(
        rest_body,
        "rest",
        (x, cwx, tw, bts, dtab, xc, pst, dec, x0, after),
        SHARED + [((NCH - EARLY, STATE, CHUNK), F32)],
        spaces=[pltpu.VMEM] * 9 + [pl.ANY],
        scratch=ROOM,
        aliases={5: 0, 6: 1, 7: 2, 8: 3},
        cost=(10**5, 1 << 14, 0),
    )


def wire_rows(decay):
    hi, lo = split2(decay)
    return jnp.concatenate([hi, lo, jnp.zeros((14, decay.shape[1]), F32)], axis=0)


def correct(half, bt, h_ref, x0_ref, cwx_ref, tw0_ref, ends, dec_ref, xc_o, ds_o, emit):
    for q in range(4):
        lanes = half_lanes(half, q * CHUNK)
        window = jnp.concatenate([halo_rows(h_ref, lanes), x0_ref[:, lanes].astype(F32)], axis=0)
        u = conv(window, taps_of(cwx_ref, lanes), 16).astype(BF)
        xc_o[0:16, lanes] = u
        w = dot(tw0_ref[...], onehot(half * (HEADS // 2) + q * HPC, CHUNK, HD, 0, 64))
        xw = jnp.concatenate([u.astype(F32) * w, jnp.zeros((SPAN - 16, CHUNK), F32)], axis=0).astype(BF)
        fix = dot(bt, xw)
        ds_o[:, lanes] = fix
        dec = dec_ref[0:8, lanes]
        after = dec[1:2] * dec[2:3] * dec[3:4]
        ref, n = ends[q]
        emit(q, ref[n] + after * fix, dec[0:1] * after)


def second_body(h_ref, x0_ref, b0_ref, cwx_ref, cwb_ref, tw0_ref, end_ref, dec_ref, xc_in, b_in,
                xc_o, b_o, ds_o, send_o, bt_o):
    v = jnp.concatenate([halo_rows(h_ref, pl.ds(INNER, STATE)), b0_ref[...].astype(F32)], axis=0)
    v = conv(v, [cwb_ref[k][:, :STATE] for k in range(4)], 16)
    b_o[0:16, :] = v.astype(BF)
    bt = jnp.transpose(jnp.concatenate([v, jnp.zeros((SPAN - 16, STATE), F32)], axis=0)).astype(BF)
    bt_o[...] = bt

    def emit(q, state, decay):
        send_o[q, 0:STATE, :] = state.astype(BF)
        send_o[q, STATE:WROWS, :] = wire_rows(decay).astype(BF)

    correct(1 - spot()[0], bt, h_ref, x0_ref, cwx_ref, tw0_ref, [(end_ref, q) for q in range(4)], dec_ref, xc_o, ds_o, emit)


def third_body(h_ref, x0_ref, bt_ref, cwx_ref, tw0_ref, end_ref, late_ref, dec_ref, xc_in, ds_in, xc_o, ds_o, keep_o):
    def emit(q, state, decay):
        keep_o[q, 0:STATE, :] = state
        keep_o[q, STATE:WROWS, :] = jnp.concatenate([decay, jnp.zeros((15, CHUNK), F32)], axis=0)

    ends = [(end_ref, 4 + q) if 4 + q < EARLY else (late_ref, 4 + q - EARLY) for q in range(4)]
    correct(spot()[0], bt_ref[...], h_ref, x0_ref, cwx_ref, tw0_ref, ends, dec_ref, xc_o, ds_o, emit)


def second_call(halo, x0, b0, cwx, cwb, tw0, end, dec, xc, b):
    return call(
        second_body,
        "second",
        (halo, x0, b0, cwx, cwb, tw0, end, dec, xc, b),
        [
            ((TOK, INNER), BF),
            ((TOK, STATE), BF),
            ((STATE, INNER), F32),
            ((4, WROWS, CHUNK), BF),
            ((STATE, 128), BF),
        ],
        aliases={8: 0, 9: 1},
        cost=(10**5, 1 << 14, 0),
    )


def third_call(halo, x0, bt, cwx, tw0, end, late, dec, xc, ds):
    return call(
        third_body,
        "third",
        (halo, x0, bt, cwx, tw0, end, late, dec, xc, ds),
        [((TOK, INNER), BF), ((STATE, INNER), F32), ((4, WROWS, CHUNK), F32)],
        aliases={8: 0, 9: 1},
        cost=(10**5, 1 << 14, 0),
    )


def table_body(L_ref, step_ref, ds_ref, h_ref, bc_ref, cwb_ref, b_ref, after_ref,
               c_o, sc_o, m2_o, tl_o, te_o, td_o, buf):
    L = L_ref[...]
    M = jnp.log(step_ref[...]) * LOG2E - L
    for j in range(NCH):
        m2_o[j, 0:HPC, :] = M[j * HPC : (j + 1) * HPC, :]
    zero = jnp.zeros((HEADS, TOK), F32)
    tl_o[...] = jnp.transpose(jnp.concatenate([*split3(L), zero], axis=0)).astype(BF)
    parts, before = [], jnp.zeros((HEADS, SPAN), F32)
    for c in range(NB):
        s = L[:, c * SPAN : (c + 1) * SPAN]
        parts.append(before + s)
        before = before + jnp.broadcast_to(s[:, SPAN - 1 : SPAN], (HEADS, SPAN))
    e = [*split2(jnp.exp2(L)), *split2(jnp.exp2(jnp.concatenate(parts, axis=1)))]
    te_o[...] = jnp.transpose(jnp.concatenate(e, axis=0)).astype(BF)
    d = [jnp.broadcast_to(p, (HEADS, SPAN)) for p in split2(column(ds_ref[...], HEADS))]
    d = jnp.concatenate([*d, jnp.zeros((2 * HEADS, SPAN), F32)], axis=0)
    td_o[...] = jnp.transpose(d)[0:16].astype(BF)
    buf[pl.ds(0, 8), :] = halo_rows(h_ref, pl.ds(INNER + STATE, STATE))
    buf[pl.ds(8, TOK), :] = bc_ref[:, STATE:].astype(F32)
    taps = [cwb_ref[k][:, STATE:] for k in range(4)]
    causal = iota((SPAN, SPAN), 0) >= iota((SPAN, SPAN), 1)
    for c in range(NB):
        rows = pl.ds(c * SPAN, SPAN)
        v = conv(buf[pl.ds(c * SPAN, SPAN + 8), :], taps, SPAN).astype(BF)
        c_o[rows, :] = v
        s = lax.dot_general(v, b_ref[rows, :], (((1,), (1,)), ((), ())), preferred_element_type=F32)
        sc_o[c] = jnp.where(causal, s, 0.0)


def table_call(L, step, ds, halo, bc, cwb, b, after):
    return call(
        table_body,
        "table",
        (L, step, ds, halo, bc, cwb, b, after),
        [
            ((TOK, STATE), BF),
            ((NB, SPAN, SPAN), F32),
            ((NCH, 8, TOK), F32),
            ((TOK, 128), BF),
            ((TOK, 128), BF),
            ((16, 128), BF),
        ],
        spaces=[pltpu.VMEM] * 7 + [pl.ANY],
        scratch=[pltpu.VMEM((TOK + 8, STATE), F32)],
        cost=(10**8, 2 << 20, 10**5),
    )


def decay_of(v):
    return v[STATE : STATE + 1] + v[STATE + 1 : STATE + 2]


def small_call(body, name, args, outs, scratch=(), after=()):
    n = len(args)
    m = len(after)

    def run(*refs):
        body(*refs[:n], *refs[n + m :])

    return call(
        run,
        name,
        (*args, *after),
        [(o.shape, o.dtype) for o in outs],
        spaces=[pltpu.VMEM] * n + [pl.ANY] * m,
        scratch=scratch,
    )


def pair_body(keep_ref, recv_ref, *outs):
    core, z = spot()[:2]
    for i in range(4):
        q = z ^ i
        own = keep_ref[q]
        other = recv_ref[q].astype(F32)
        early = jnp.where(core == 0, own, other)
        late = jnp.where(core == 0, other, own)
        d_early, d_late = decay_of(early), decay_of(late)
        outs[i][0:STATE, :] = (d_late * early[0:STATE] + late[0:STATE]).astype(BF)
        outs[i][STATE:WROWS, :] = wire_rows(d_early * d_late).astype(BF)


def row_body(r0, r1, r2, r3, total_o, pre_o, dpre_o, box):
    z = spot()[1]
    for i, r in enumerate((r0, r1, r2, r3)):
        box[z ^ i] = r[...].astype(F32)
    state = jnp.zeros((STATE, CHUNK), F32)
    decay = jnp.ones((1, CHUNK), F32)
    for k in range(4):
        pre_o[k] = state
        dpre_o[k] = jnp.broadcast_to(decay, (8, CHUNK))
        v = box[k]
        d = decay_of(v)
        state = d * state + v[0:STATE]
        decay = decay * d
    total_o[0:STATE, :] = state.astype(BF)
    total_o[STATE:WROWS, :] = wire_rows(decay).astype(BF)


def plane_body(r0, r1, r2, r3, pre_ref, dpre_ref, o0, o1, o2, o3, box):
    z, y = spot()[1:3]
    for i, r in enumerate((r0, r1, r2, r3)):
        box[y ^ i] = r[...].astype(F32)
    state = jnp.zeros((STATE, CHUNK), F32)
    for k in range(3):
        v = box[k]
        state = jnp.where(k < y, decay_of(v) * state + v[0:STATE], state)
    for i, o in enumerate((o0, o1, o2, o3)):
        q = z ^ i
        d = dpre_ref[q]
        o[...] = (pre_ref[q] + d[0:1] * state).astype(BF)


def spread_body(r0, r1, r2, r3, keep_ref, recv_ref, send_o, stay_o, box):
    core, z = spot()[:2]
    for i, r in enumerate((r0, r1, r2, r3)):
        box[z ^ i] = r[...].astype(F32)
    for q in range(4):
        early = jnp.where(core == 0, keep_ref[q], recv_ref[q].astype(F32))
        a = box[q]
        b = decay_of(early) * a + early[0:STATE]
        send_o[q] = jnp.where(core == 0, b, a).astype(BF)
        stay_o[q] = jnp.where(core == 0, a, b).astype(BF)


def mix_body(first_chunk, chunks, xc_ref, c_ref, sc_ref, z_ref, m2_ref, tl_ref, te_ref, td_ref, dec_ref, pst_ref,
             ds_ref, *rest):
    yg_o, g2_o, ex, ee = rest[-4:]
    left = iota((SPAN, SPAN), 1) < HD

    def expand(k):
        j = first_chunk + k
        ex[k % 2] = dot(tl_ref[...], onehot(j * HPC, HPC * SPAN, SPAN))
        ee[k % 2, :, 0:CHUNK] = dot(te_ref[...], onehot(j * HPC, CHUNK, HD, 0, 64))
        ee[k % 2, :, CHUNK:] = dot(te_ref[...], onehot(j * HPC, CHUNK, HD, 64, 128))

    expand(0)
    for k in range(chunks):
        j = first_chunk + k
        lanes = pl.ds(j * CHUNK, CHUNK)
        if k + 1 < chunks:
            expand(k + 1)
        skip = dot(td_ref[...], onehot(j * HPC, CHUNK, HD))[0:1]
        fix = ds_ref[:, lanes]
        for c in range(NB):
            rows = pl.ds(c * SPAN, SPAN)
            s = sc_ref[c]
            x = xc_ref[rows, lanes]
            parts = []
            for h in range(HPC):
                m2 = m2_ref[j, h : h + 1, c * SPAN : (c + 1) * SPAN]
                e = ex[k % 2, rows, h * SPAN : (h + 1) * SPAN] + m2
                parts.append((s * jnp.exp2(jnp.minimum(e, 8.0))).astype(BF))
            ys = []
            for p in range(HPC // 2):
                xp = x[:, p * SPAN : (p + 1) * SPAN].astype(F32)
                rhs = jnp.concatenate([jnp.where(left, xp, 0.0), jnp.where(left, 0.0, xp)], axis=0).astype(BF)
                ys.append(dot(jnp.concatenate([parts[2 * p], parts[2 * p + 1]], axis=1), rhs))
            y = jnp.concatenate(ys, axis=1) + skip * x.astype(F32)
            if c > 0:
                if c > 1:
                    fix = dec_ref[c - 1 : c, lanes] * fix
                ent = (pst_ref[c - 1, :, lanes] + fix).astype(BF)
                y = y + ee[k % 2, rows, 0:CHUNK] * dot(c_ref[rows, :], ent)
            gate = silu(z_ref[rows, lanes].astype(F32))
            yg_o[rows, lanes] = (y * gate).astype(BF)
            g2_o[rows, lanes] = (ee[k % 2, rows, CHUNK:] * gate).astype(BF)


def mix_call(first_chunk, chunks, args, after, before):
    n = len(args)
    return call(
        functools.partial(mix_body, first_chunk, chunks),
        "mix",
        (*args, after, *before),
        [((TOK, INNER), BF)] * 2,
        spaces=[pltpu.VMEM] * n + [pl.ANY],
        scratch=[pltpu.VMEM((2, TOK, HPC * SPAN), F32), pltpu.VMEM((2, TOK, 2 * CHUNK), F32)],
        aliases={n + 1: 0, n + 2: 1} if before else None,
        cost=(chunks * 25 * 10**7, chunks << 20, chunks * 6 * 10**5),
    )


def gated(yg_ref, g2_ref, c_ref, e_ref, gain_ref, half, blocks, n_o, ce, sums):
    at = lambda q: pl.ds(pl.multiple_of(half * (INNER // 2) + q * CHUNK, CHUNK), CHUNK)

    def carry(q):
        ce[q % 2] = dot(c_ref[...], e_ref[q])

    carry(0)
    for q in range(4):
        lanes = at(q)
        if q < 3:
            carry(q + 1)
        gain = gain_ref[:, lanes]
        for c in range(blocks):
            rows = pl.ds(c * SPAN, SPAN)
            g = yg_ref[rows, lanes].astype(F32) + ce[q % 2, rows, :] * g2_ref[rows, lanes].astype(F32)
            sq = g * g
            sq = sq[:, :128] + sq[:, 128:]
            sums[c] = sq if sums[c] is None else sums[c] + sq
            n_o[rows, q * CHUNK : (q + 1) * CHUNK] = (g * gain).astype(BF)


def near_gate_body(yg_ref, g2_ref, c_ref, e_ref, gain_ref, after_ref, n_o, ss_o, ce):
    sums = [None] * NB
    gated(yg_ref, g2_ref, c_ref, e_ref, gain_ref, spot()[0], NB, n_o, ce, sums)
    for c in range(NB):
        ss_o[pl.ds(c * SPAN, SPAN), :] = sums[c]


def far_gate_body(yg_ref, g2_ref, c_ref, e_ref, gain_ref, ss_ref, after_ref, n_o, inv_o, ce):
    sums = [ss_ref[pl.ds(c * SPAN, SPAN), :] for c in range(NB)]
    gated(yg_ref, g2_ref, c_ref, e_ref, gain_ref, 1 - spot()[0], NB, n_o, ce, sums)
    for c in range(NB):
        m = jnp.sum(sums[c], axis=1, keepdims=True) * (1.0 / INNER)
        inv_o[pl.ds(c * SPAN, SPAN), :] = jnp.broadcast_to(lax.rsqrt(m + 1e-05), (SPAN, 128))


def near_gate_call(yg, g2, cm, e, gain, after):
    return call(
        near_gate_body,
        "gate",
        (yg, g2, cm, e, gain, after),
        [((TOK, INNER // 2), BF), ((TOK, 128), F32)],
        spaces=[pltpu.VMEM] * 5 + [pl.ANY],
        scratch=[pltpu.VMEM((2, TOK, CHUNK), F32)],
        cost=(25 * 10**7, 4 << 20, 0),
    )


def far_gate_call(yg, g2, cm, e, gain, ss, after):
    return call(
        far_gate_body,
        "gate",
        (yg, g2, cm, e, gain, ss, after),
        [((TOK, INNER // 2), BF), ((TOK, 128), F32)],
        spaces=[pltpu.VMEM] * 6 + [pl.ANY],
        scratch=[pltpu.VMEM((2, TOK, CHUNK), F32)],
        cost=(25 * 10**7, 4 << 20, 0),
    )


def weight_block(w_ref, half, shift, k):
    lane = lax.rem(spot()[3] + shift, 4) * QOUT + k * CHUNK
    rows = pl.ds(pl.multiple_of(half * (INNER // 2), INNER // 2), INNER // 2)
    return w_ref[rows, pl.ds(pl.multiple_of(lane, CHUNK), CHUNK)]


def part_body(n_ref, w_ref, after_ref, p_o):
    core = spot()[0]
    for k in range(QOUT // CHUNK):
        p_o[:, k * CHUNK : (k + 1) * CHUNK] = dot(n_ref[...], weight_block(w_ref, core, 2, k))


def far_body(p_ref, n_ref, inv_ref, w_ref, r_o, l_o):
    core = spot()[0]
    for k in range(QOUT // CHUNK):
        y = p_ref[:, k * CHUNK : (k + 1) * CHUNK] + dot(n_ref[...], weight_block(w_ref, 1 - core, 2, k))
        o = (r_o, l_o)[k // 2]
        o[pl.ds((k % 2) * CHUNK, CHUNK), :] = jnp.transpose(y * inv_ref[:, 0:1]).astype(BF)


def proj_body(shift, first, count, near_ref, n_ref, inv_ref, w_ref, after_ref, o):
    core = spot()[0]
    for k in range(count):
        y = dot(near_ref[...], weight_block(w_ref, core, shift, first + k))
        y = y + dot(n_ref[...], weight_block(w_ref, 1 - core, shift, first + k))
        o[pl.ds(k * CHUNK, CHUNK), :] = jnp.transpose(y * inv_ref[:, 0:1]).astype(BF)


def part_call(near, w, after):
    return call(
        part_body,
        "part",
        (near, w, after),
        [((TOK, QOUT), F32)],
        spaces=[pltpu.VMEM] * 2 + [pl.ANY],
        cost=(TOK * INNER * QOUT, 5 << 20, 0),
    )[0]


def far_call(p, n, inv, w):
    return call(
        far_body,
        "far",
        (p, n, inv, w),
        [((QOUT // 2, TOK), BF)] * 2,
        cost=(TOK * INNER * QOUT, 5 << 20, 0),
    )


def proj_call(shift, side, near, n, inv, w, after):
    count = 2 if side < 2 else 4
    return call(
        functools.partial(proj_body, shift, 2 * side if side < 2 else 0, count),
        "proj",
        (near, n, inv, w, after),
        [((count * CHUNK, TOK), BF)],
        spaces=[pltpu.VMEM] * 4 + [pl.ANY],
        cost=(2 * TOK * INNER * count * CHUNK, 5 << 20, 0),
    )[0]


def relay_body(mine, a, o):
    o[...] = (mine[...].astype(F32) + a[...].astype(F32)).astype(BF)


def last_body(side, own, near, total, *rest):
    o_hbm, o, sem = rest[-3:]
    base = side * (QOUT // 2)
    copies = []
    for k in range(4):
        rows = pl.ds(k * 128, 128)
        there = pl.ds(base + k * 128, 128)
        s = own[there, :].astype(F32) + near[rows, :].astype(F32) + total[rows, :].astype(F32)
        o[rows, :] = s.astype(BF)
        copies.append(pltpu.make_async_copy(o.at[rows, :], o_hbm.at[there, :], sem.at[k]))
        copies[k].start()
    for c in copies:
        c.wait()


def last_call(side, own, near, total, before=()):
    return pl.pallas_call(
        functools.partial(last_body, side),
        in_specs=[pl.BlockSpec(memory_space=pltpu.VMEM)] * 3 + [pl.BlockSpec(memory_space=pltpu.HBM)] * len(before),
        out_specs=pl.BlockSpec(memory_space=pltpu.HBM),
        out_shape=jax.ShapeDtypeStruct((QOUT, TOK), BF),
        scratch_shapes=[pltpu.VMEM((QOUT // 2, TOK), BF), pltpu.SemaphoreType.DMA((4,))],
        input_output_aliases={3: 0} if before else {},
        compiler_params=pltpu.CompilerParams(vmem_limit_bytes=VMEM_LIMIT),
        name="last",
    )(own, near, total, *before)


def seq_perm(v, y, z, core):
    return lax.ppermute(v, "seq", [(src, src ^ (y * 8 + z * 2 + core)) for src in range(32)])


def head_perm(v, shift):
    return lax.ppermute(v, "head", [(s, (s + shift) % 4) for s in range(4)])


def on_device(x_in, bc_in, z_in, dt_raw, a_log, conv_x, conv_bc, d_skip, norm_gain, out_weight):
    bc = bc_in.reshape(TOK, 256)
    hbm = lambda v: pltpu.with_memory_space_constraint(v, pltpu.HBM)
    edge = call(
        edge_body,
        "edge",
        (hbm(x_in), hbm(bc)),
        [((8, INNER + 256), BF)],
        spaces=[pltpu.HBM] * 2,
        scratch=[pltpu.SemaphoreType.DMA((2,))],
    )[0]
    halo = lax.ppermute(edge, "seq", [(s, (s + 1) % 32) for s in range(32)])
    xc, pst, dec, x0, end, b, L, step, tw0, b0, tw, bts, dtab, xv = first_call(
        hbm(x_in), bc, conv_x, conv_bc, dt_raw, a_log.reshape(1, HEADS)
    )
    xc, b, ds, send, bt = second_call(halo, x0, b0, conv_x, conv_bc, tw0, end, dec, xc, b)
    recv = seq_perm(send, 0, 0, 1)
    xc, pst, dec, x0, late = rest_call(xv, conv_x, tw, bts, dtab, xc, pst, dec, x0, send)
    xc, ds, keep = third_call(halo, x0, bt, conv_x, tw0, end, late, dec, xc, ds)
    piece = jax.ShapeDtypeStruct((WROWS, CHUNK), BF)
    plain = jax.ShapeDtypeStruct((STATE, CHUNK), BF)
    box = pltpu.VMEM((4, WROWS, CHUNK), F32)
    splits = (3, 3, 2)
    q = small_call(pair_body, "pair", (keep, recv), [piece] * 4)
    cm, sc, m2, tl, te, td = table_call(L, step, d_skip.reshape(1, HEADS), halo, bc, conv_bc, b, q[0])
    known = (xc, cm, sc, z_in, m2, tl, te, td, dec, pst, ds)
    work = lambda k, after, before: mix_call(sum(splits[:k]), splits[k], known, after, before)
    mixed = work(0, q[0], ())
    rows = [q[0]] + [seq_perm(q[i], 0, i, 0) for i in (1, 2, 3)]
    total, pre, dpre = small_call(
        row_body,
        "row",
        rows,
        [piece, jax.ShapeDtypeStruct((4, STATE, CHUNK), F32), jax.ShapeDtypeStruct((4, 8, CHUNK), F32)],
        [box],
        (mixed[0],),
    )
    mixed = work(1, total, mixed)
    cols = [total] + [seq_perm(total, i, 0, 0) for i in (1, 2, 3)]
    e = small_call(plane_body, "plane", (*cols, pre, dpre), [plain] * 4, [box], (mixed[0],))
    mixed = work(2, e[0], mixed)
    back = [e[0]] + [seq_perm(e[i], 0, i, 0) for i in (1, 2, 3)]
    half = jax.ShapeDtypeStruct((4, STATE, CHUNK), BF)
    give, stay = small_call(
        spread_body, "spread", (*back, keep, recv), [half] * 2, [pltpu.VMEM((4, STATE, CHUNK), F32)], (mixed[0],)
    )
    take = seq_perm(give, 0, 0, 1)
    gain = norm_gain.reshape(1, INNER)
    near, ss = near_gate_call(*mixed, cm, stay, gain, give)
    p = part_call(near, out_weight, ss)
    other, inv = far_gate_call(*mixed, cm, take, gain, ss, p)
    far_r, far_l = far_call(p, other, inv, out_weight)
    from_left, from_right = head_perm(far_r, 1), head_perm(far_l, -1)
    proj = lambda shift, side, after: proj_call(shift, side, near, other, inv, out_weight, after)
    right_l = proj(1, 1, far_r)
    near_l = head_perm(right_l, 1)
    left_r = proj(3, 0, right_l)
    near_r = head_perm(left_r, -1)
    right_r = proj(1, 0, left_r)
    left_l = proj(3, 1, right_r)
    shape = ((QOUT // 2, TOK), BF)
    sum_r = head_perm(call(relay_body, "relay", (right_r, from_left), [shape])[0], 1)
    sum_l = head_perm(call(relay_body, "relay", (left_l, from_right), [shape])[0], -1)
    own = proj(0, 2, left_l)
    out = last_call(1, own, near_l, sum_l)
    return last_call(0, own, near_r, sum_r, (out,))


def solution(mesh):
    placed = (
        P("seq", "head"),
        P("seq", "head", None),
        P("seq", "head"),
        P("head", "seq"),
        P("head"),
        P(None, "head"),
        P(None, "head", None),
        P("head"),
        P("head"),
        P("head", None),
    )
    return jax.shard_map(
        on_device, mesh=mesh, in_specs=placed, out_specs=P("head", "seq"), check_vma=False
    )
```

```python
import functools

import jax
import jax.numpy as jnp
from jax import lax
from jax.experimental import pallas as pl
from jax.experimental.pallas import tpu as pltpu
from jax.sharding import PartitionSpec as P

SPAN = 128
HEADS = 32
HD = 64
STATE = 128
TOK = 512
NB = 4
INNER = 2048
CHUNK = 256
NCH = INNER // CHUNK
EARLY = 5
HPC = CHUNK // HD
DOUT = 4096
QOUT = 1024
WROWS = 144
LOG2E = 1.4426950408889634
BF = jnp.bfloat16
F32 = jnp.float32
VMEM_LIMIT = 10 << 20


def silu(u):
    half = 0.5 * u
    return half + half * jnp.tanh(half)


def dot(a, b):
    return jnp.dot(a, b, preferred_element_type=F32)


def iota(shape, axis):
    return lax.broadcasted_iota(jnp.int32, shape, axis)


def onehot(first_head, width, lanes, low=0, high=128):
    k = iota((128, width), 0)
    h = first_head + (iota((128, width), 1) // lanes)
    hit = ((k & 31) == h) & (k >= low) & (k < high)
    return jnp.where(hit, 1.0, 0.0).astype(BF)


def split2(v):
    hi = v.astype(BF).astype(F32)
    return hi, (v - hi).astype(BF).astype(F32)


def column(row, n):
    eye = iota((n, n), 0) == iota((n, n), 1)
    return jnp.sum(jnp.where(eye, jnp.broadcast_to(row, (n, n)), 0.0), axis=1, keepdims=True)


def call(body, name, args, outs, spaces=(), scratch=(), cost=(10**6, 1 << 20, 0), aliases=None, limit=VMEM_LIMIT):
    specs = [pl.BlockSpec(memory_space=spaces[k] if k < len(spaces) else pltpu.VMEM) for k in range(len(args))]
    return pl.pallas_call(
        body,
        in_specs=specs,
        out_specs=[pl.BlockSpec(memory_space=pltpu.VMEM)] * len(outs),
        out_shape=[jax.ShapeDtypeStruct(s, d) for s, d in outs],
        scratch_shapes=list(scratch),
        input_output_aliases=aliases or {},
        compiler_params=pltpu.CompilerParams(vmem_limit_bytes=limit),
        cost_estimate=pl.CostEstimate(flops=cost[0], bytes_accessed=cost[1], transcendentals=cost[2]),
        name=name,
    )(*args)


def conv(window, taps, rows):
    before = pltpu.roll(window, 1, 0)
    near = taps[3] * window + taps[2] * before
    far = taps[1] * window + taps[0] * before
    return silu(near[8:] + pltpu.roll(far, 2, 0)[8:])


def taps_of(ref, lanes):
    return [ref[k : k + 1, lanes] for k in range(4)]


def split3(v):
    hi = v.astype(BF).astype(F32)
    rest = v - hi
    mid = rest.astype(BF).astype(F32)
    return hi, mid, rest - mid


def spot():
    place = lax.axis_index("seq")
    return place & 1, (place >> 1) & 3, place >> 3, lax.axis_index("head")


def edge_body(x_ref, bc_ref, o, sem):
    a = pltpu.make_async_copy(x_ref.at[pl.ds(TOK - 8, 8), :], o.at[:, pl.ds(0, INNER)], sem.at[0])
    b = pltpu.make_async_copy(bc_ref.at[pl.ds(TOK - 8, 8), :], o.at[:, pl.ds(INNER, 256)], sem.at[1])
    a.start()
    b.start()
    a.wait()
    b.wait()


def halo_rows(h_ref, lanes):
    return jnp.where(lax.axis_index("seq") == 0, 0.0, h_ref[:, lanes].astype(F32))


def half_lanes(half, k, width=CHUNK):
    return pl.ds(pl.multiple_of(half * (INNER // 2) + k, 128), width)


def states(items, fetch, xv, cwx, tw, dtab, bts, wbuf, xw, xc_o, pst_o, end_o, dec_o, x0_o):
    nothing = jnp.zeros((8, 128), F32)
    count = len(items)
    head = lambda n: items[n][0] * (HEADS // 2) + items[n][1] * HPC
    spread = lambda n: dot(tw[...], onehot(head(n), CHUNK, HD, 0, 64))
    wbuf[0] = spread(0)
    for n in range(count + 1):
        if n < count:
            half, q = items[n]
            lanes = half_lanes(half, q * CHUNK)
            if n + 1 < count:
                wbuf[(n + 1) % 2] = spread(n + 1)
            dec_o[:, lanes] = dot(dtab[...], onehot(head(n), CHUNK, HD, 64, 128))
            if fetch:
                fetch[n].wait()
            x0_o[:, lanes] = xv[0:16, lanes]
        state = None
        for c in range(NB):
            if n < count:
                for r in (0, 64):
                    for l in (0, 128):
                        row = c * SPAN + r
                        part = half_lanes(half, q * CHUNK + l, 128)
                        if row == 0:
                            window = jnp.concatenate([nothing, xv[0:64, part].astype(F32)], axis=0)
                        else:
                            window = xv[pl.ds(row - 8, 72), part].astype(F32)
                        v = conv(window, taps_of(cwx, part), 64).astype(BF)
                        xc_o[pl.ds(row, 64), part] = v
                        w = wbuf[n % 2, pl.ds(row, 64), l : l + 128]
                        xw[n % 2, pl.ds(row, 64), l : l + 128] = (v.astype(F32) * w).astype(BF)
            if n > 0:
                before = half_lanes(items[n - 1][0], items[n - 1][1] * CHUNK)
                t = dot(bts[c], xw[(n - 1) % 2, pl.ds(c * SPAN, SPAN), :])
                state = t if c == 0 else dec_o[c : c + 1, before] * state + t
                if c < NB - 1:
                    pst_o[c, :, before] = state
                else:
                    end_o[n - 1] = state


def first_body(x_hbm, bv, cwx, cwb, dtv, alv,
               xc_o, pst_o, dec_o, x0_o, end_o, b_o, L_o, step_o, tw0_o, b0_o, tw, bts, dtab_o, xv,
               wbuf, xw, sem):
    core = spot()[0]
    order = [(1 - core, q) for q in range(4)] + [(core, q) for q in range(4)]
    copies = []
    for n, (half, q) in enumerate(order):
        lanes = half_lanes(half, q * CHUNK)
        copies.append(pltpu.make_async_copy(x_hbm.at[:, lanes], xv.at[:, lanes], sem.at[n]))
        copies[n].start()
    tri = jnp.where(iota((SPAN, SPAN), 0) <= iota((SPAN, SPAN), 1), 1.0, 0.0).astype(BF)
    v = dtv[...].astype(F32)
    t = jnp.exp(-jnp.abs(v))
    u = 1.0 + t
    d = u - 1.0
    flat = d == 0.0
    step = jnp.maximum(v, 0.0) + jnp.where(flat, t, jnp.log(u) * t / jnp.where(flat, 1.0, d))
    step_o[...] = step
    a = column(alv[...], HEADS)
    rate = jnp.concatenate(split3((-LOG2E * jnp.exp(a)) * step), axis=0).astype(BF)
    Ls, ends = [], []
    for c in range(NB):
        s = dot(rate[:, c * SPAN : (c + 1) * SPAN], tri)
        s = s[0:HEADS] + s[HEADS : 2 * HEADS] + s[2 * HEADS : 3 * HEADS]
        Ls.append(s)
        ends.append(jnp.broadcast_to(s[:, SPAN - 1 : SPAN], (HEADS, SPAN)))
    L = jnp.concatenate(Ls, axis=1)
    end = jnp.concatenate(ends, axis=1)
    L_o[...] = L
    w_hi, w_lo = split2(jnp.exp2(end - L) * step)
    d_hi, d_lo = split2(jnp.exp2(end))
    twt = jnp.transpose(jnp.concatenate([w_hi, w_lo, d_hi, d_lo], axis=0))
    tw[...] = twt.astype(BF)
    tw0_o[...] = twt[0:16].astype(BF)
    tw[pl.ds(0, 16), :] = jnp.zeros((16, 128), BF)
    rows = [twt[c * SPAN : c * SPAN + 1] for c in range(NB)]
    dtab = jnp.concatenate(rows + [jnp.zeros((12, SPAN), F32)], axis=0).astype(BF)
    dtab_o[...] = dtab
    b0_o[...] = bv[0:16, :STATE]
    btaps = [cwb[k][:, :STATE] for k in range(4)]
    nothing = jnp.zeros((8, STATE), F32)
    for c in range(NB):
        if c == 0:
            window = jnp.concatenate([nothing, bv[0:SPAN, :STATE].astype(F32)], axis=0)
        else:
            window = bv[pl.ds(c * SPAN - 8, SPAN + 8), :STATE].astype(F32)
        v = conv(window, btaps, SPAN)
        b_o[pl.ds(c * SPAN, SPAN), :] = v.astype(BF)
        bts[c] = jnp.transpose(v).astype(BF)
    states(order[:EARLY], copies, xv, cwx, tw, dtab_o, bts, wbuf, xw, xc_o, pst_o, end_o, dec_o, x0_o)
    for c in copies[EARLY:]:
        c.wait()


def rest_body(xv, cwx, tw, bts, dtab, xc_i, pst_i, dec_i, x0_i, after,
              xc_o, pst_o, dec_o, x0_o, end_o, wbuf, xw):
    core = spot()[0]
    items = [(core, q) for q in range(EARLY - 4, 4)]
    states(items, None, xv, cwx, tw, dtab, bts, wbuf, xw, xc_o, pst_o, end_o, dec_o, x0_o)


SHARED = [
    ((TOK, INNER), BF),
    ((NB - 1, STATE, INNER), F32),
    ((16, INNER), F32),
    ((16, INNER), BF),
]
ROOM = [
    pltpu.VMEM((2, TOK, CHUNK), F32),
    pltpu.VMEM((2, TOK, CHUNK), BF),
]


def first_call(x, bc, cwx, cwb, dt, al):
    return call(
        first_body,
        "first",
        (x, bc, cwx, cwb, dt, al),
        SHARED
        + [
            ((EARLY, STATE, CHUNK), F32),
            ((TOK, STATE), BF),
            ((HEADS, TOK), F32),
            ((HEADS, TOK), F32),
            ((16, 128), BF),
            ((16, STATE), BF),
            ((TOK, 128), BF),
            ((NB, STATE, SPAN), BF),
            ((16, 128), BF),
            ((TOK, INNER), BF),
        ],
        spaces=[pltpu.HBM],
        scratch=ROOM + [pltpu.SemaphoreType.DMA((NCH,))],
        cost=(10**5, 1 << 14, 0),
    )


def rest_call(x, cwx, tw, bts, dtab, xc, pst, dec, x0, after):
    return call(
        rest_body,
        "rest",
        (x, cwx, tw, bts, dtab, xc, pst, dec, x0, after),
        SHARED + [((NCH - EARLY, STATE, CHUNK), F32)],
        spaces=[pltpu.VMEM] * 9 + [pl.ANY],
        scratch=ROOM,
        aliases={5: 0, 6: 1, 7: 2, 8: 3},
        cost=(10**5, 1 << 14, 0),
    )


def wire_rows(decay):
    hi, lo = split2(decay)
    return jnp.concatenate([hi, lo, jnp.zeros((14, decay.shape[1]), F32)], axis=0)


def correct(half, bt, h_ref, x0_ref, cwx_ref, tw0_ref, ends, dec_ref, xc_o, ds_o, emit):
    for q in range(4):
        lanes = half_lanes(half, q * CHUNK)
        window = jnp.concatenate([halo_rows(h_ref, lanes), x0_ref[:, lanes].astype(F32)], axis=0)
        u = conv(window, taps_of(cwx_ref, lanes), 16).astype(BF)
        xc_o[0:16, lanes] = u
        w = dot(tw0_ref[...], onehot(half * (HEADS // 2) + q * HPC, CHUNK, HD, 0, 64))
        xw = jnp.concatenate([u.astype(F32) * w, jnp.zeros((SPAN - 16, CHUNK), F32)], axis=0).astype(BF)
        fix = dot(bt, xw)
        ds_o[:, lanes] = fix
        dec = dec_ref[0:8, lanes]
        after = dec[1:2] * dec[2:3] * dec[3:4]
        ref, n = ends[q]
        emit(q, ref[n] + after * fix, dec[0:1] * after)


def second_body(h_ref, x0_ref, b0_ref, cwx_ref, cwb_ref, tw0_ref, end_ref, dec_ref, xc_in, b_in,
                xc_o, b_o, ds_o, send_o, bt_o):
    v = jnp.concatenate([halo_rows(h_ref, pl.ds(INNER, STATE)), b0_ref[...].astype(F32)], axis=0)
    v = conv(v, [cwb_ref[k][:, :STATE] for k in range(4)], 16)
    b_o[0:16, :] = v.astype(BF)
    bt = jnp.transpose(jnp.concatenate([v, jnp.zeros((SPAN - 16, STATE), F32)], axis=0)).astype(BF)
    bt_o[...] = bt

    def emit(q, state, decay):
        send_o[q, 0:STATE, :] = state.astype(BF)
        send_o[q, STATE:WROWS, :] = wire_rows(decay).astype(BF)

    correct(1 - spot()[0], bt, h_ref, x0_ref, cwx_ref, tw0_ref, [(end_ref, q) for q in range(4)], dec_ref, xc_o, ds_o, emit)


def third_body(h_ref, x0_ref, bt_ref, cwx_ref, tw0_ref, end_ref, late_ref, dec_ref, xc_in, ds_in, xc_o, ds_o, keep_o):
    def emit(q, state, decay):
        keep_o[q, 0:STATE, :] = state
        keep_o[q, STATE:WROWS, :] = jnp.concatenate([decay, jnp.zeros((15, CHUNK), F32)], axis=0)

    ends = [(end_ref, 4 + q) if 4 + q < EARLY else (late_ref, 4 + q - EARLY) for q in range(4)]
    correct(spot()[0], bt_ref[...], h_ref, x0_ref, cwx_ref, tw0_ref, ends, dec_ref, xc_o, ds_o, emit)


def second_call(halo, x0, b0, cwx, cwb, tw0, end, dec, xc, b):
    return call(
        second_body,
        "second",
        (halo, x0, b0, cwx, cwb, tw0, end, dec, xc, b),
        [
            ((TOK, INNER), BF),
            ((TOK, STATE), BF),
            ((STATE, INNER), F32),
            ((4, WROWS, CHUNK), BF),
            ((STATE, 128), BF),
        ],
        aliases={8: 0, 9: 1},
        cost=(10**5, 1 << 14, 0),
    )


def third_call(halo, x0, bt, cwx, tw0, end, late, dec, xc, ds):
    return call(
        third_body,
        "third",
        (halo, x0, bt, cwx, tw0, end, late, dec, xc, ds),
        [((TOK, INNER), BF), ((STATE, INNER), F32), ((4, WROWS, CHUNK), F32)],
        aliases={8: 0, 9: 1},
        cost=(10**5, 1 << 14, 0),
    )


def table_body(L_ref, step_ref, ds_ref, h_ref, bc_ref, cwb_ref, b_ref, after_ref,
               c_o, sc_o, m2_o, tl_o, te_o, td_o, buf):
    L = L_ref[...]
    M = jnp.log(step_ref[...]) * LOG2E - L
    for j in range(NCH):
        m2_o[j, 0:HPC, :] = M[j * HPC : (j + 1) * HPC, :]
    zero = jnp.zeros((HEADS, TOK), F32)
    tl_o[...] = jnp.transpose(jnp.concatenate([*split3(L), zero], axis=0)).astype(BF)
    parts, before = [], jnp.zeros((HEADS, SPAN), F32)
    for c in range(NB):
        s = L[:, c * SPAN : (c + 1) * SPAN]
        parts.append(before + s)
        before = before + jnp.broadcast_to(s[:, SPAN - 1 : SPAN], (HEADS, SPAN))
    e = [*split2(jnp.exp2(L)), *split2(jnp.exp2(jnp.concatenate(parts, axis=1)))]
    te_o[...] = jnp.transpose(jnp.concatenate(e, axis=0)).astype(BF)
    d = [jnp.broadcast_to(p, (HEADS, SPAN)) for p in split2(column(ds_ref[...], HEADS))]
    d = jnp.concatenate([*d, jnp.zeros((2 * HEADS, SPAN), F32)], axis=0)
    td_o[...] = jnp.transpose(d)[0:16].astype(BF)
    buf[pl.ds(0, 8), :] = halo_rows(h_ref, pl.ds(INNER + STATE, STATE))
    buf[pl.ds(8, TOK), :] = bc_ref[:, STATE:].astype(F32)
    taps = [cwb_ref[k][:, STATE:] for k in range(4)]
    causal = iota((SPAN, SPAN), 0) >= iota((SPAN, SPAN), 1)
    for c in range(NB):
        rows = pl.ds(c * SPAN, SPAN)
        v = conv(buf[pl.ds(c * SPAN, SPAN + 8), :], taps, SPAN).astype(BF)
        c_o[rows, :] = v
        s = lax.dot_general(v, b_ref[rows, :], (((1,), (1,)), ((), ())), preferred_element_type=F32)
        sc_o[c] = jnp.where(causal, s, 0.0)


def table_call(L, step, ds, halo, bc, cwb, b, after):
    return call(
        table_body,
        "table",
        (L, step, ds, halo, bc, cwb, b, after),
        [
            ((TOK, STATE), BF),
            ((NB, SPAN, SPAN), F32),
            ((NCH, 8, TOK), F32),
            ((TOK, 128), BF),
            ((TOK, 128), BF),
            ((16, 128), BF),
        ],
        spaces=[pltpu.VMEM] * 7 + [pl.ANY],
        scratch=[pltpu.VMEM((TOK + 8, STATE), F32)],
        cost=(10**8, 2 << 20, 10**5),
    )


def decay_of(v):
    return v[STATE : STATE + 1] + v[STATE + 1 : STATE + 2]


def small_call(body, name, args, outs, scratch=(), after=()):
    n = len(args)
    m = len(after)

    def run(*refs):
        body(*refs[:n], *refs[n + m :])

    return call(
        run,
        name,
        (*args, *after),
        [(o.shape, o.dtype) for o in outs],
        spaces=[pltpu.VMEM] * n + [pl.ANY] * m,
        scratch=scratch,
    )


def pair_body(keep_ref, recv_ref, *outs):
    core, z = spot()[:2]
    for i in range(4):
        q = (z + i) & 3
        own = keep_ref[q]
        other = recv_ref[q].astype(F32)
        early = jnp.where(core == 0, own, other)
        late = jnp.where(core == 0, other, own)
        d_early, d_late = decay_of(early), decay_of(late)
        outs[i][0:STATE, :] = (d_late * early[0:STATE] + late[0:STATE]).astype(BF)
        outs[i][STATE:WROWS, :] = wire_rows(d_early * d_late).astype(BF)


def row_body(r0, r1, r2, r3, total_o, pre_o, dpre_o, box):
    z = spot()[1]
    for i, r in enumerate((r0, r1, r2, r3)):
        box[(z - i) & 3] = r[...].astype(F32)
    state = jnp.zeros((STATE, CHUNK), F32)
    decay = jnp.ones((1, CHUNK), F32)
    for k in range(4):
        pre_o[k] = state
        dpre_o[k] = jnp.broadcast_to(decay, (8, CHUNK))
        v = box[k]
        d = decay_of(v)
        state = d * state + v[0:STATE]
        decay = decay * d
    total_o[0:STATE, :] = state.astype(BF)
    total_o[STATE:WROWS, :] = wire_rows(decay).astype(BF)


def plane_body(r0, r1, r2, r3, pre_ref, dpre_ref, o0, o1, o2, o3, box):
    z, y = spot()[1:3]
    for i, r in enumerate((r0, r1, r2, r3)):
        box[y ^ i] = r[...].astype(F32)
    state = jnp.zeros((STATE, CHUNK), F32)
    for k in range(3):
        v = box[k]
        state = jnp.where(k < y, decay_of(v) * state + v[0:STATE], state)
    for i, o in enumerate((o0, o1, o2, o3)):
        q = (z + i) & 3
        d = dpre_ref[q]
        o[...] = (pre_ref[q] + d[0:1] * state).astype(BF)


def spread_body(r0, r1, r2, r3, keep_ref, recv_ref, send_o, stay_o, box):
    core, z = spot()[:2]
    for i, r in enumerate((r0, r1, r2, r3)):
        box[(z - i) & 3] = r[...].astype(F32)
    for q in range(4):
        early = jnp.where(core == 0, keep_ref[q], recv_ref[q].astype(F32))
        a = box[q]
        b = decay_of(early) * a + early[0:STATE]
        send_o[q] = jnp.where(core == 0, b, a).astype(BF)
        stay_o[q] = jnp.where(core == 0, a, b).astype(BF)


def mix_body(first_chunk, chunks, xc_ref, c_ref, sc_ref, z_ref, m2_ref, tl_ref, te_ref, td_ref, dec_ref, pst_ref,
             ds_ref, *rest):
    yg_o, g2_o, ex, ee = rest[-4:]
    left = iota((SPAN, SPAN), 1) < HD

    def expand(k):
        j = first_chunk + k
        ex[k % 2] = dot(tl_ref[...], onehot(j * HPC, HPC * SPAN, SPAN))
        ee[k % 2, :, 0:CHUNK] = dot(te_ref[...], onehot(j * HPC, CHUNK, HD, 0, 64))
        ee[k % 2, :, CHUNK:] = dot(te_ref[...], onehot(j * HPC, CHUNK, HD, 64, 128))

    expand(0)
    for k in range(chunks):
        j = first_chunk + k
        lanes = pl.ds(j * CHUNK, CHUNK)
        if k + 1 < chunks:
            expand(k + 1)
        skip = dot(td_ref[...], onehot(j * HPC, CHUNK, HD))[0:1]
        fix = ds_ref[:, lanes]
        for c in range(NB):
            rows = pl.ds(c * SPAN, SPAN)
            s = sc_ref[c]
            x = xc_ref[rows, lanes]
            parts = []
            for h in range(HPC):
                m2 = m2_ref[j, h : h + 1, c * SPAN : (c + 1) * SPAN]
                e = ex[k % 2, rows, h * SPAN : (h + 1) * SPAN] + m2
                parts.append((s * jnp.exp2(jnp.minimum(e, 8.0))).astype(BF))
            ys = []
            for p in range(HPC // 2):
                xp = x[:, p * SPAN : (p + 1) * SPAN].astype(F32)
                rhs = jnp.concatenate([jnp.where(left, xp, 0.0), jnp.where(left, 0.0, xp)], axis=0).astype(BF)
                ys.append(dot(jnp.concatenate([parts[2 * p], parts[2 * p + 1]], axis=1), rhs))
            y = jnp.concatenate(ys, axis=1) + skip * x.astype(F32)
            if c > 0:
                if c > 1:
                    fix = dec_ref[c - 1 : c, lanes] * fix
                ent = (pst_ref[c - 1, :, lanes] + fix).astype(BF)
                y = y + ee[k % 2, rows, 0:CHUNK] * dot(c_ref[rows, :], ent)
            gate = silu(z_ref[rows, lanes].astype(F32))
            yg_o[rows, lanes] = (y * gate).astype(BF)
            g2_o[rows, lanes] = (ee[k % 2, rows, CHUNK:] * gate).astype(BF)


def mix_call(first_chunk, chunks, args, after, before):
    n = len(args)
    return call(
        functools.partial(mix_body, first_chunk, chunks),
        "mix",
        (*args, after, *before),
        [((TOK, INNER), BF)] * 2,
        spaces=[pltpu.VMEM] * n + [pl.ANY],
        scratch=[pltpu.VMEM((2, TOK, HPC * SPAN), F32), pltpu.VMEM((2, TOK, 2 * CHUNK), F32)],
        aliases={n + 1: 0, n + 2: 1} if before else None,
        cost=(chunks * 25 * 10**7, chunks << 20, chunks * 6 * 10**5),
    )


def gated(yg_ref, g2_ref, c_ref, e_ref, gain_ref, half, blocks, n_o, ce, sums):
    at = lambda q: pl.ds(pl.multiple_of(half * (INNER // 2) + q * CHUNK, CHUNK), CHUNK)

    def carry(q):
        ce[q % 2] = dot(c_ref[...], e_ref[q])

    carry(0)
    for q in range(4):
        lanes = at(q)
        if q < 3:
            carry(q + 1)
        gain = gain_ref[:, lanes]
        for c in range(blocks):
            rows = pl.ds(c * SPAN, SPAN)
            g = yg_ref[rows, lanes].astype(F32) + ce[q % 2, rows, :] * g2_ref[rows, lanes].astype(F32)
            sq = g * g
            sq = sq[:, :128] + sq[:, 128:]
            sums[c] = sq if sums[c] is None else sums[c] + sq
            n_o[rows, q * CHUNK : (q + 1) * CHUNK] = (g * gain).astype(BF)


def near_gate_body(yg_ref, g2_ref, c_ref, e_ref, gain_ref, after_ref, n_o, ss_o, ce):
    sums = [None] * NB
    gated(yg_ref, g2_ref, c_ref, e_ref, gain_ref, spot()[0], NB, n_o, ce, sums)
    for c in range(NB):
        ss_o[pl.ds(c * SPAN, SPAN), :] = sums[c]


def far_gate_body(yg_ref, g2_ref, c_ref, e_ref, gain_ref, ss_ref, after_ref, n_o, inv_o, ce):
    sums = [ss_ref[pl.ds(c * SPAN, SPAN), :] for c in range(NB)]
    gated(yg_ref, g2_ref, c_ref, e_ref, gain_ref, 1 - spot()[0], NB, n_o, ce, sums)
    for c in range(NB):
        m = jnp.sum(sums[c], axis=1, keepdims=True) * (1.0 / INNER)
        inv_o[pl.ds(c * SPAN, SPAN), :] = jnp.broadcast_to(lax.rsqrt(m + 1e-05), (SPAN, 128))


def near_gate_call(yg, g2, cm, e, gain, after):
    return call(
        near_gate_body,
        "gate",
        (yg, g2, cm, e, gain, after),
        [((TOK, INNER // 2), BF), ((TOK, 128), F32)],
        spaces=[pltpu.VMEM] * 5 + [pl.ANY],
        scratch=[pltpu.VMEM((2, TOK, CHUNK), F32)],
        cost=(25 * 10**7, 4 << 20, 0),
    )


def far_gate_call(yg, g2, cm, e, gain, ss, after):
    return call(
        far_gate_body,
        "gate",
        (yg, g2, cm, e, gain, ss, after),
        [((TOK, INNER // 2), BF), ((TOK, 128), F32)],
        spaces=[pltpu.VMEM] * 6 + [pl.ANY],
        scratch=[pltpu.VMEM((2, TOK, CHUNK), F32)],
        cost=(25 * 10**7, 4 << 20, 0),
    )


def weight_block(w_ref, half, shift, k):
    lane = lax.rem(spot()[3] + shift, 4) * QOUT + k * CHUNK
    rows = pl.ds(pl.multiple_of(half * (INNER // 2), INNER // 2), INNER // 2)
    return w_ref[rows, pl.ds(pl.multiple_of(lane, CHUNK), CHUNK)]


def part_body(n_ref, w_ref, after_ref, p_o):
    core = spot()[0]
    for k in range(QOUT // CHUNK):
        p_o[:, k * CHUNK : (k + 1) * CHUNK] = dot(n_ref[...], weight_block(w_ref, core, 2, k))


def far_body(p_ref, n_ref, inv_ref, w_ref, r_o, l_o):
    core = spot()[0]
    for k in range(QOUT // CHUNK):
        y = p_ref[:, k * CHUNK : (k + 1) * CHUNK] + dot(n_ref[...], weight_block(w_ref, 1 - core, 2, k))
        o = (r_o, l_o)[k // 2]
        o[pl.ds((k % 2) * CHUNK, CHUNK), :] = jnp.transpose(y * inv_ref[:, 0:1]).astype(BF)


def proj_body(shift, first, count, near_ref, n_ref, inv_ref, w_ref, after_ref, o):
    core = spot()[0]
    for k in range(count):
        y = dot(near_ref[...], weight_block(w_ref, core, shift, first + k))
        y = y + dot(n_ref[...], weight_block(w_ref, 1 - core, shift, first + k))
        o[pl.ds(k * CHUNK, CHUNK), :] = jnp.transpose(y * inv_ref[:, 0:1]).astype(BF)


def part_call(near, w, after):
    return call(
        part_body,
        "part",
        (near, w, after),
        [((TOK, QOUT), F32)],
        spaces=[pltpu.VMEM] * 2 + [pl.ANY],
        cost=(TOK * INNER * QOUT, 5 << 20, 0),
    )[0]


def far_call(p, n, inv, w):
    return call(
        far_body,
        "far",
        (p, n, inv, w),
        [((QOUT // 2, TOK), BF)] * 2,
        cost=(TOK * INNER * QOUT, 5 << 20, 0),
    )


def proj_call(shift, side, near, n, inv, w, after):
    count = 2 if side < 2 else 4
    return call(
        functools.partial(proj_body, shift, 2 * side if side < 2 else 0, count),
        "proj",
        (near, n, inv, w, after),
        [((count * CHUNK, TOK), BF)],
        spaces=[pltpu.VMEM] * 4 + [pl.ANY],
        cost=(2 * TOK * INNER * count * CHUNK, 5 << 20, 0),
    )[0]


def relay_body(mine, a, o):
    o[...] = (mine[...].astype(F32) + a[...].astype(F32)).astype(BF)


def last_body(own, near_r, near_l, sum_r, sum_l, o_hbm, o, sem):
    copies = []
    for k in range(4):
        rows = pl.ds(k * CHUNK, CHUNK)
        side = pl.ds((k % 2) * CHUNK, CHUNK)
        near, total = ((near_r, sum_r), (near_l, sum_l))[k // 2]
        s = own[rows, :].astype(F32) + near[side, :].astype(F32) + total[side, :].astype(F32)
        o[rows, :] = s.astype(BF)
        copies.append(pltpu.make_async_copy(o.at[rows, :], o_hbm.at[rows, :], sem.at[k]))
        copies[k].start()
    for c in copies:
        c.wait()


def last_call(*args):
    return pl.pallas_call(
        last_body,
        in_specs=[pl.BlockSpec(memory_space=pltpu.VMEM)] * len(args),
        out_specs=pl.BlockSpec(memory_space=pltpu.HBM),
        out_shape=jax.ShapeDtypeStruct((QOUT, TOK), BF),
        scratch_shapes=[pltpu.VMEM((QOUT, TOK), BF), pltpu.SemaphoreType.DMA((4,))],
        compiler_params=pltpu.CompilerParams(vmem_limit_bytes=VMEM_LIMIT),
        name="last",
    )(*args)


def seq_perm(v, y, z, core):
    pairs = []
    for src in range(32):
        row = (src >> 3) ^ y
        column = (((src >> 1) & 3) + z) & 3
        pairs.append((src, row * 8 + column * 2 + ((src & 1) ^ core)))
    return lax.ppermute(v, "seq", pairs)


def head_perm(v, shift):
    return lax.ppermute(v, "head", [(s, (s + shift) % 4) for s in range(4)])


def on_device(x_in, bc_in, z_in, dt_raw, a_log, conv_x, conv_bc, d_skip, norm_gain, out_weight):
    bc = bc_in.reshape(TOK, 256)
    hbm = lambda v: pltpu.with_memory_space_constraint(v, pltpu.HBM)
    edge = call(
        edge_body,
        "edge",
        (hbm(x_in), hbm(bc)),
        [((8, INNER + 256), BF)],
        spaces=[pltpu.HBM] * 2,
        scratch=[pltpu.SemaphoreType.DMA((2,))],
    )[0]
    halo = lax.ppermute(edge, "seq", [(s, (s + 1) % 32) for s in range(32)])
    xc, pst, dec, x0, end, b, L, step, tw0, b0, tw, bts, dtab, xv = first_call(
        hbm(x_in), bc, conv_x, conv_bc, dt_raw, a_log.reshape(1, HEADS)
    )
    xc, b, ds, send, bt = second_call(halo, x0, b0, conv_x, conv_bc, tw0, end, dec, xc, b)
    recv = seq_perm(send, 0, 0, 1)
    xc, pst, dec, x0, late = rest_call(xv, conv_x, tw, bts, dtab, xc, pst, dec, x0, send)
    xc, ds, keep = third_call(halo, x0, bt, conv_x, tw0, end, late, dec, xc, ds)
    piece = jax.ShapeDtypeStruct((WROWS, CHUNK), BF)
    plain = jax.ShapeDtypeStruct((STATE, CHUNK), BF)
    box = pltpu.VMEM((4, WROWS, CHUNK), F32)
    splits = (3, 3, 2)
    q = small_call(pair_body, "pair", (keep, recv), [piece] * 4)
    cm, sc, m2, tl, te, td = table_call(L, step, d_skip.reshape(1, HEADS), halo, bc, conv_bc, b, q[0])
    known = (xc, cm, sc, z_in, m2, tl, te, td, dec, pst, ds)
    work = lambda k, after, before: mix_call(sum(splits[:k]), splits[k], known, after, before)
    mixed = work(0, q[0], ())
    rows = [q[0]] + [seq_perm(q[i], 0, i, 0) for i in (1, 2, 3)]
    total, pre, dpre = small_call(
        row_body,
        "row",
        rows,
        [piece, jax.ShapeDtypeStruct((4, STATE, CHUNK), F32), jax.ShapeDtypeStruct((4, 8, CHUNK), F32)],
        [box],
        (mixed[0],),
    )
    mixed = work(1, total, mixed)
    cols = [total] + [seq_perm(total, i, 0, 0) for i in (1, 2, 3)]
    e = small_call(plane_body, "plane", (*cols, pre, dpre), [plain] * 4, [box], (mixed[0],))
    mixed = work(2, e[0], mixed)
    back = [e[0]] + [seq_perm(e[i], 0, i, 0) for i in (1, 2, 3)]
    half = jax.ShapeDtypeStruct((4, STATE, CHUNK), BF)
    give, stay = small_call(
        spread_body, "spread", (*back, keep, recv), [half] * 2, [pltpu.VMEM((4, STATE, CHUNK), F32)], (mixed[0],)
    )
    take = seq_perm(give, 0, 0, 1)
    gain = norm_gain.reshape(1, INNER)
    near, ss = near_gate_call(*mixed, cm, stay, gain, give)
    p = part_call(near, out_weight, ss)
    other, inv = far_gate_call(*mixed, cm, take, gain, ss, p)
    far_r, far_l = far_call(p, other, inv, out_weight)
    from_left, from_right = head_perm(far_r, 1), head_perm(far_l, -1)
    proj = lambda shift, side, after: proj_call(shift, side, near, other, inv, out_weight, after)
    right_l = proj(1, 1, far_r)
    near_l = head_perm(right_l, 1)
    left_r = proj(3, 0, right_l)
    near_r = head_perm(left_r, -1)
    right_r = proj(1, 0, left_r)
    left_l = proj(3, 1, right_r)
    shape = ((QOUT // 2, TOK), BF)
    sum_r = head_perm(call(relay_body, "relay", (right_r, from_left), [shape])[0], 1)
    sum_l = head_perm(call(relay_body, "relay", (left_l, from_right), [shape])[0], -1)
    own = proj(0, 2, left_l)
    return last_call(own, near_r, near_l, sum_r, sum_l)


def solution(mesh):
    placed = (
        P("seq", "head"),
        P("seq", "head", None),
        P("seq", "head"),
        P("head", "seq"),
        P("head"),
        P(None, "head"),
        P(None, "head", None),
        P("head"),
        P("head"),
        P("head", None),
    )
    return jax.shard_map(
        on_device, mesh=mesh, in_specs=placed, out_specs=P("head", "seq"), check_vma=False
    )
```

```python
import functools

import jax
import jax.numpy as jnp
from jax import lax
from jax.experimental import pallas as pl
from jax.experimental.pallas import tpu as pltpu
from jax.sharding import PartitionSpec as P

SPAN = 128
HEADS = 32
HD = 64
STATE = 128
TOK = 512
NB = 4
INNER = 2048
CHUNK = 256
NCH = INNER // CHUNK
EARLY = 5
HPC = CHUNK // HD
DOUT = 4096
QOUT = 1024
WROWS = 144
LOG2E = 1.4426950408889634
BF = jnp.bfloat16
F32 = jnp.float32
VMEM_LIMIT = 10 << 20


def silu(u):
    half = 0.5 * u
    return half + half * jnp.tanh(half)


def dot(a, b):
    return jnp.dot(a, b, preferred_element_type=F32)


def iota(shape, axis):
    return lax.broadcasted_iota(jnp.int32, shape, axis)


def onehot(first_head, width, lanes, low=0, high=128):
    k = iota((128, width), 0)
    h = first_head + (iota((128, width), 1) // lanes)
    hit = ((k & 31) == h) & (k >= low) & (k < high)
    return jnp.where(hit, 1.0, 0.0).astype(BF)


def split2(v):
    hi = v.astype(BF).astype(F32)
    return hi, (v - hi).astype(BF).astype(F32)


def column(row, n):
    eye = iota((n, n), 0) == iota((n, n), 1)
    return jnp.sum(jnp.where(eye, jnp.broadcast_to(row, (n, n)), 0.0), axis=1, keepdims=True)


def call(body, name, args, outs, spaces=(), scratch=(), cost=(10**6, 1 << 20, 0), aliases=None, limit=VMEM_LIMIT):
    specs = [pl.BlockSpec(memory_space=spaces[k] if k < len(spaces) else pltpu.VMEM) for k in range(len(args))]
    return pl.pallas_call(
        body,
        in_specs=specs,
        out_specs=[pl.BlockSpec(memory_space=pltpu.VMEM)] * len(outs),
        out_shape=[jax.ShapeDtypeStruct(s, d) for s, d in outs],
        scratch_shapes=list(scratch),
        input_output_aliases=aliases or {},
        compiler_params=pltpu.CompilerParams(vmem_limit_bytes=limit),
        cost_estimate=pl.CostEstimate(flops=cost[0], bytes_accessed=cost[1], transcendentals=cost[2]),
        name=name,
    )(*args)


def conv(window, taps, rows):
    before = pltpu.roll(window, 1, 0)
    near = taps[3] * window + taps[2] * before
    far = taps[1] * window + taps[0] * before
    half = near[8:] + pltpu.roll(far, 2, 0)[8:]
    return half + half * jnp.tanh(half)


def taps_of(ref, lanes):
    return [0.5 * ref[k : k + 1, lanes] for k in range(4)]


def split3(v):
    hi = v.astype(BF).astype(F32)
    rest = v - hi
    mid = rest.astype(BF).astype(F32)
    return hi, mid, rest - mid


def spot():
    place = lax.axis_index("seq")
    return place & 1, (place >> 1) & 3, place >> 3, lax.axis_index("head")


def edge_body(x_ref, bc_ref, o, sem):
    a = pltpu.make_async_copy(x_ref.at[pl.ds(TOK - 8, 8), :], o.at[:, pl.ds(0, INNER)], sem.at[0])
    b = pltpu.make_async_copy(bc_ref.at[pl.ds(TOK - 8, 8), :], o.at[:, pl.ds(INNER, 256)], sem.at[1])
    a.start()
    b.start()
    a.wait()
    b.wait()


def halo_rows(h_ref, lanes):
    return jnp.where(lax.axis_index("seq") == 0, 0.0, h_ref[:, lanes].astype(F32))


def half_lanes(half, k, width=CHUNK):
    return pl.ds(pl.multiple_of(half * (INNER // 2) + k, 128), width)


def states(items, xv, cwx, tw, dtab, bts, wbuf, xw, xc_o, pst_o, end_o, dec_o, x0_o):
    nothing = jnp.zeros((8, 128), F32)
    count = len(items)
    head = lambda n: items[n][0] * (HEADS // 2) + items[n][1] * HPC
    spread = lambda n: dot(tw[...], onehot(head(n), CHUNK, HD, 0, 64))
    wbuf[0] = spread(0)
    for n in range(count + 1):
        if n < count:
            half, q = items[n]
            lanes = half_lanes(half, q * CHUNK)
            if n + 1 < count:
                wbuf[(n + 1) % 2] = spread(n + 1)
            dec_o[:, lanes] = dot(dtab[...], onehot(head(n), CHUNK, HD, 64, 128))
            x0_o[:, lanes] = xv[0:16, lanes]
        state = None
        for c in range(NB):
            if n < count:
                for r in (0, 64):
                    for l in (0, 128):
                        row = c * SPAN + r
                        part = half_lanes(half, q * CHUNK + l, 128)
                        if row == 0:
                            window = jnp.concatenate([nothing, xv[0:64, part].astype(F32)], axis=0)
                        else:
                            window = xv[pl.ds(row - 8, 72), part].astype(F32)
                        v = conv(window, taps_of(cwx, part), 64).astype(BF)
                        xc_o[pl.ds(row, 64), part] = v
                        w = wbuf[n % 2, pl.ds(row, 64), l : l + 128]
                        xw[n % 2, pl.ds(row, 64), l : l + 128] = (v.astype(F32) * w).astype(BF)
            if n > 0:
                before = half_lanes(items[n - 1][0], items[n - 1][1] * CHUNK)
                t = dot(bts[c], xw[(n - 1) % 2, pl.ds(c * SPAN, SPAN), :])
                state = t if c == 0 else dec_o[c : c + 1, before] * state + t
                if c < NB - 1:
                    pst_o[c, :, before] = state
                else:
                    end_o[n - 1] = state


def first_body(x_hbm, bv, cwx, cwb, dtv, alv,
               xc_o, pst_o, dec_o, x0_o, end_o, b_o, L_o, step_o, tw0_o, b0_o, tw, bts, dtab_o, xv,
               wbuf, xw, sem):
    core = spot()[0]
    order = [(1 - core, q) for q in range(4)] + [(core, q) for q in range(4)]
    copies = []
    for n, (half, q) in enumerate(order):
        lanes = half_lanes(half, q * CHUNK)
        copies.append(pltpu.make_async_copy(x_hbm.at[:, lanes], xv.at[:, lanes], sem.at[n]))
        copies[n].start()
    tri = jnp.where(iota((SPAN, SPAN), 0) <= iota((SPAN, SPAN), 1), 1.0, 0.0).astype(BF)
    v = dtv[...].astype(F32)
    t = jnp.exp(-jnp.abs(v))
    u = 1.0 + t
    d = u - 1.0
    flat = d == 0.0
    step = jnp.maximum(v, 0.0) + jnp.where(flat, t, jnp.log(u) * t / jnp.where(flat, 1.0, d))
    step_o[...] = step
    a = column(alv[...], HEADS)
    rate = jnp.concatenate(split3((-LOG2E * jnp.exp(a)) * step), axis=0).astype(BF)
    Ls, ends = [], []
    for c in range(NB):
        s = dot(rate[:, c * SPAN : (c + 1) * SPAN], tri)
        s = s[0:HEADS] + s[HEADS : 2 * HEADS] + s[2 * HEADS : 3 * HEADS]
        Ls.append(s)
        ends.append(jnp.broadcast_to(s[:, SPAN - 1 : SPAN], (HEADS, SPAN)))
    for c in copies[:EARLY]:
        c.wait()
    L = jnp.concatenate(Ls, axis=1)
    end = jnp.concatenate(ends, axis=1)
    L_o[...] = L
    w_hi, w_lo = split2(jnp.exp2(end - L) * step)
    d_hi, d_lo = split2(jnp.exp2(end))
    twt = jnp.transpose(jnp.concatenate([w_hi, w_lo, d_hi, d_lo], axis=0))
    tw[...] = twt.astype(BF)
    tw0_o[...] = twt[0:16].astype(BF)
    tw[pl.ds(0, 16), :] = jnp.zeros((16, 128), BF)
    rows = [twt[c * SPAN : c * SPAN + 1] for c in range(NB)]
    dtab = jnp.concatenate(rows + [jnp.zeros((12, SPAN), F32)], axis=0).astype(BF)
    dtab_o[...] = dtab
    b0_o[...] = bv[0:16, :STATE]
    btaps = [0.5 * cwb[k][:, :STATE] for k in range(4)]
    nothing = jnp.zeros((8, STATE), F32)
    for c in range(NB):
        if c == 0:
            window = jnp.concatenate([nothing, bv[0:SPAN, :STATE].astype(F32)], axis=0)
        else:
            window = bv[pl.ds(c * SPAN - 8, SPAN + 8), :STATE].astype(F32)
        v = conv(window, btaps, SPAN)
        b_o[pl.ds(c * SPAN, SPAN), :] = v.astype(BF)
        bts[c] = jnp.transpose(v).astype(BF)
    states(order[:EARLY], xv, cwx, tw, dtab_o, bts, wbuf, xw, xc_o, pst_o, end_o, dec_o, x0_o)
    for c in copies[EARLY:]:
        c.wait()


def rest_body(xv, cwx, tw, bts, dtab, xc_i, pst_i, dec_i, x0_i, after,
              xc_o, pst_o, dec_o, x0_o, end_o, wbuf, xw):
    core = spot()[0]
    items = [(core, q) for q in range(EARLY - 4, 4)]
    states(items, xv, cwx, tw, dtab, bts, wbuf, xw, xc_o, pst_o, end_o, dec_o, x0_o)


SHARED = [
    ((TOK, INNER), BF),
    ((NB - 1, STATE, INNER), F32),
    ((16, INNER), F32),
    ((16, INNER), BF),
]
ROOM = [
    pltpu.VMEM((2, TOK, CHUNK), F32),
    pltpu.VMEM((2, TOK, CHUNK), BF),
]


def first_call(x, bc, cwx, cwb, dt, al):
    return call(
        first_body,
        "first",
        (x, bc, cwx, cwb, dt, al),
        SHARED
        + [
            ((EARLY, STATE, CHUNK), F32),
            ((TOK, STATE), BF),
            ((HEADS, TOK), F32),
            ((HEADS, TOK), F32),
            ((16, 128), BF),
            ((16, STATE), BF),
            ((TOK, 128), BF),
            ((NB, STATE, SPAN), BF),
            ((16, 128), BF),
            ((TOK, INNER), BF),
        ],
        spaces=[pltpu.HBM],
        scratch=ROOM + [pltpu.SemaphoreType.DMA((NCH,))],
        cost=(10**5, 1 << 14, 0),
    )


def rest_call(x, cwx, tw, bts, dtab, xc, pst, dec, x0, after):
    return call(
        rest_body,
        "rest",
        (x, cwx, tw, bts, dtab, xc, pst, dec, x0, after),
        SHARED + [((NCH - EARLY, STATE, CHUNK), F32)],
        spaces=[pltpu.VMEM] * 9 + [pl.ANY],
        scratch=ROOM,
        aliases={5: 0, 6: 1, 7: 2, 8: 3},
        cost=(10**5, 1 << 14, 0),
    )


def wire_rows(decay):
    hi, lo = split2(decay)
    return jnp.concatenate([hi, lo, jnp.zeros((14, decay.shape[1]), F32)], axis=0)


def correct(half, bt, h_ref, x0_ref, cwx_ref, tw0_ref, ends, dec_ref, xc_o, ds_o, emit):
    for q in range(4):
        lanes = half_lanes(half, q * CHUNK)
        window = jnp.concatenate([halo_rows(h_ref, lanes), x0_ref[:, lanes].astype(F32)], axis=0)
        u = conv(window, taps_of(cwx_ref, lanes), 16).astype(BF)
        xc_o[0:16, lanes] = u
        w = dot(tw0_ref[...], onehot(half * (HEADS // 2) + q * HPC, CHUNK, HD, 0, 64))
        xw = jnp.concatenate([u.astype(F32) * w, jnp.zeros((SPAN - 16, CHUNK), F32)], axis=0).astype(BF)
        fix = dot(bt, xw)
        ds_o[:, lanes] = fix
        dec = dec_ref[0:8, lanes]
        after = dec[1:2] * dec[2:3] * dec[3:4]
        ref, n = ends[q]
        emit(q, ref[n] + after * fix, dec[0:1] * after)


def second_body(h_ref, x0_ref, b0_ref, cwx_ref, cwb_ref, tw0_ref, end_ref, dec_ref, xc_in, b_in,
                xc_o, b_o, ds_o, send_o, bt_o):
    v = jnp.concatenate([halo_rows(h_ref, pl.ds(INNER, STATE)), b0_ref[...].astype(F32)], axis=0)
    v = conv(v, [0.5 * cwb_ref[k][:, :STATE] for k in range(4)], 16)
    b_o[0:16, :] = v.astype(BF)
    bt = jnp.transpose(jnp.concatenate([v, jnp.zeros((SPAN - 16, STATE), F32)], axis=0)).astype(BF)
    bt_o[...] = bt

    def emit(q, state, decay):
        send_o[q, 0:STATE, :] = state.astype(BF)
        send_o[q, STATE:WROWS, :] = wire_rows(decay).astype(BF)

    correct(1 - spot()[0], bt, h_ref, x0_ref, cwx_ref, tw0_ref, [(end_ref, q) for q in range(4)], dec_ref, xc_o, ds_o, emit)


def third_body(h_ref, x0_ref, bt_ref, cwx_ref, tw0_ref, end_ref, late_ref, dec_ref, xc_in, ds_in, xc_o, ds_o, keep_o):
    def emit(q, state, decay):
        keep_o[q, 0:STATE, :] = state
        keep_o[q, STATE:WROWS, :] = jnp.concatenate([decay, jnp.zeros((15, CHUNK), F32)], axis=0)

    ends = [(end_ref, 4 + q) if 4 + q < EARLY else (late_ref, 4 + q - EARLY) for q in range(4)]
    correct(spot()[0], bt_ref[...], h_ref, x0_ref, cwx_ref, tw0_ref, ends, dec_ref, xc_o, ds_o, emit)


def second_call(halo, x0, b0, cwx, cwb, tw0, end, dec, xc, b):
    return call(
        second_body,
        "second",
        (halo, x0, b0, cwx, cwb, tw0, end, dec, xc, b),
        [
            ((TOK, INNER), BF),
            ((TOK, STATE), BF),
            ((STATE, INNER), F32),
            ((4, WROWS, CHUNK), BF),
            ((STATE, 128), BF),
        ],
        aliases={8: 0, 9: 1},
        cost=(10**5, 1 << 14, 0),
    )


def third_call(halo, x0, bt, cwx, tw0, end, late, dec, xc, ds):
    return call(
        third_body,
        "third",
        (halo, x0, bt, cwx, tw0, end, late, dec, xc, ds),
        [((TOK, INNER), BF), ((STATE, INNER), F32), ((4, WROWS, CHUNK), F32)],
        aliases={8: 0, 9: 1},
        cost=(10**5, 1 << 14, 0),
    )


def table_body(L_ref, step_ref, ds_ref, h_ref, bc_ref, cwb_ref, b_ref, after_ref,
               c_o, sc_o, m2_o, tl_o, te_o, td_o, buf):
    L = L_ref[...]
    M = jnp.log(step_ref[...]) * LOG2E - L
    for j in range(NCH):
        m2_o[j, 0:HPC, :] = M[j * HPC : (j + 1) * HPC, :]
    zero = jnp.zeros((HEADS, TOK), F32)
    tl_o[...] = jnp.transpose(jnp.concatenate([*split3(L), zero], axis=0)).astype(BF)
    parts, before = [], jnp.zeros((HEADS, SPAN), F32)
    for c in range(NB):
        s = L[:, c * SPAN : (c + 1) * SPAN]
        parts.append(before + s)
        before = before + jnp.broadcast_to(s[:, SPAN - 1 : SPAN], (HEADS, SPAN))
    e = [*split2(jnp.exp2(L)), *split2(jnp.exp2(jnp.concatenate(parts, axis=1)))]
    te_o[...] = jnp.transpose(jnp.concatenate(e, axis=0)).astype(BF)
    d = [jnp.broadcast_to(p, (HEADS, SPAN)) for p in split2(column(ds_ref[...], HEADS))]
    d = jnp.concatenate([*d, jnp.zeros((2 * HEADS, SPAN), F32)], axis=0)
    td_o[...] = jnp.transpose(d)[0:16].astype(BF)
    buf[pl.ds(0, 8), :] = halo_rows(h_ref, pl.ds(INNER + STATE, STATE))
    buf[pl.ds(8, TOK), :] = bc_ref[:, STATE:].astype(F32)
    taps = [0.5 * cwb_ref[k][:, STATE:] for k in range(4)]
    causal = iota((SPAN, SPAN), 0) >= iota((SPAN, SPAN), 1)
    for c in range(NB):
        rows = pl.ds(c * SPAN, SPAN)
        v = conv(buf[pl.ds(c * SPAN, SPAN + 8), :], taps, SPAN).astype(BF)
        c_o[rows, :] = v
        s = lax.dot_general(v, b_ref[rows, :], (((1,), (1,)), ((), ())), preferred_element_type=F32)
        sc_o[c] = jnp.where(causal, s, 0.0)


def table_call(L, step, ds, halo, bc, cwb, b, after):
    return call(
        table_body,
        "table",
        (L, step, ds, halo, bc, cwb, b, after),
        [
            ((TOK, STATE), BF),
            ((NB, SPAN, SPAN), F32),
            ((NCH, 8, TOK), F32),
            ((TOK, 128), BF),
            ((TOK, 128), BF),
            ((16, 128), BF),
        ],
        spaces=[pltpu.VMEM] * 7 + [pl.ANY],
        scratch=[pltpu.VMEM((TOK + 8, STATE), F32)],
        cost=(10**8, 2 << 20, 10**5),
    )


def decay_of(v):
    return v[STATE : STATE + 1] + v[STATE + 1 : STATE + 2]


def small_call(body, name, args, outs, scratch=(), after=()):
    n = len(args)
    m = len(after)

    def run(*refs):
        body(*refs[:n], *refs[n + m :])

    return call(
        run,
        name,
        (*args, *after),
        [(o.shape, o.dtype) for o in outs],
        spaces=[pltpu.VMEM] * n + [pl.ANY] * m,
        scratch=scratch,
    )


def pair_body(keep_ref, recv_ref, *outs):
    core, z = spot()[:2]
    for i in range(4):
        q = (z + i) & 3
        own = keep_ref[q]
        other = recv_ref[q].astype(F32)
        early = jnp.where(core == 0, own, other)
        late = jnp.where(core == 0, other, own)
        d_early, d_late = decay_of(early), decay_of(late)
        outs[i][0:STATE, :] = (d_late * early[0:STATE] + late[0:STATE]).astype(BF)
        outs[i][STATE:WROWS, :] = wire_rows(d_early * d_late).astype(BF)


def row_body(r0, r1, r2, r3, total_o, pre_o, dpre_o, box):
    z = spot()[1]
    for i, r in enumerate((r0, r1, r2, r3)):
        box[(z - i) & 3] = r[...].astype(F32)
    state = jnp.zeros((STATE, CHUNK), F32)
    decay = jnp.ones((1, CHUNK), F32)
    for k in range(4):
        pre_o[k] = state
        dpre_o[k] = jnp.broadcast_to(decay, (8, CHUNK))
        v = box[k]
        d = decay_of(v)
        state = d * state + v[0:STATE]
        decay = decay * d
    total_o[0:STATE, :] = state.astype(BF)
    total_o[STATE:WROWS, :] = wire_rows(decay).astype(BF)


def plane_body(r0, r1, r2, r3, pre_ref, dpre_ref, o0, o1, o2, o3, box):
    z, y = spot()[1:3]
    for i, r in enumerate((r0, r1, r2, r3)):
        box[y ^ i] = r[...].astype(F32)
    state = jnp.zeros((STATE, CHUNK), F32)
    for k in range(3):
        v = box[k]
        state = jnp.where(k < y, decay_of(v) * state + v[0:STATE], state)
    for i, o in enumerate((o0, o1, o2, o3)):
        q = (z + i) & 3
        d = dpre_ref[q]
        o[...] = (pre_ref[q] + d[0:1] * state).astype(BF)


def spread_body(r0, r1, r2, r3, keep_ref, recv_ref, send_o, stay_o, box):
    core, z = spot()[:2]
    for i, r in enumerate((r0, r1, r2, r3)):
        box[(z - i) & 3] = r[...].astype(F32)
    for q in range(4):
        early = jnp.where(core == 0, keep_ref[q], recv_ref[q].astype(F32))
        a = box[q]
        b = decay_of(early) * a + early[0:STATE]
        send_o[q] = jnp.where(core == 0, b, a).astype(BF)
        stay_o[q] = jnp.where(core == 0, a, b).astype(BF)


def mix_body(first_chunk, chunks, xc_ref, c_ref, sc_ref, z_ref, m2_ref, tl_ref, te_ref, td_ref, dec_ref, pst_ref,
             ds_ref, *rest):
    yg_o, g2_o, ex, ee = rest[-4:]
    left = iota((SPAN, SPAN), 1) < HD

    def expand(k):
        j = first_chunk + k
        ex[k % 2] = dot(tl_ref[...], onehot(j * HPC, HPC * SPAN, SPAN))
        ee[k % 2, :, 0:CHUNK] = dot(te_ref[...], onehot(j * HPC, CHUNK, HD, 0, 64))
        ee[k % 2, :, CHUNK:] = dot(te_ref[...], onehot(j * HPC, CHUNK, HD, 64, 128))

    expand(0)
    for k in range(chunks):
        j = first_chunk + k
        lanes = pl.ds(j * CHUNK, CHUNK)
        if k + 1 < chunks:
            expand(k + 1)
        skip = dot(td_ref[...], onehot(j * HPC, CHUNK, HD))[0:1]
        fix = ds_ref[:, lanes]
        for c in range(NB):
            rows = pl.ds(c * SPAN, SPAN)
            s = sc_ref[c]
            x = xc_ref[rows, lanes]
            parts = []
            for h in range(HPC):
                m2 = m2_ref[j, h : h + 1, c * SPAN : (c + 1) * SPAN]
                e = ex[k % 2, rows, h * SPAN : (h + 1) * SPAN] + m2
                parts.append((s * jnp.exp2(jnp.minimum(e, 8.0))).astype(BF))
            ys = []
            for p in range(HPC // 2):
                xp = x[:, p * SPAN : (p + 1) * SPAN].astype(F32)
                rhs = jnp.concatenate([jnp.where(left, xp, 0.0), jnp.where(left, 0.0, xp)], axis=0).astype(BF)
                ys.append(dot(jnp.concatenate([parts[2 * p], parts[2 * p + 1]], axis=1), rhs))
            y = jnp.concatenate(ys, axis=1) + skip * x.astype(F32)
            if c > 0:
                if c > 1:
                    fix = dec_ref[c - 1 : c, lanes] * fix
                ent = (pst_ref[c - 1, :, lanes] + fix).astype(BF)
                y = y + ee[k % 2, rows, 0:CHUNK] * dot(c_ref[rows, :], ent)
            gate = silu(z_ref[rows, lanes].astype(F32))
            yg_o[rows, lanes] = (y * gate).astype(BF)
            g2_o[rows, lanes] = (ee[k % 2, rows, CHUNK:] * gate).astype(BF)


def mix_call(first_chunk, chunks, args, after, before):
    n = len(args)
    return call(
        functools.partial(mix_body, first_chunk, chunks),
        "mix",
        (*args, after, *before),
        [((TOK, INNER), BF)] * 2,
        spaces=[pltpu.VMEM] * n + [pl.ANY],
        scratch=[pltpu.VMEM((2, TOK, HPC * SPAN), F32), pltpu.VMEM((2, TOK, 2 * CHUNK), F32)],
        aliases={n + 1: 0, n + 2: 1} if before else None,
        cost=(chunks * 25 * 10**7, chunks << 20, chunks * 6 * 10**5),
    )


def gated(yg_ref, g2_ref, c_ref, e_ref, gain_ref, half, blocks, n_o, ce, sums):
    at = lambda q: pl.ds(pl.multiple_of(half * (INNER // 2) + q * CHUNK, CHUNK), CHUNK)

    def carry(q):
        ce[q % 2] = dot(c_ref[...], e_ref[q])

    carry(0)
    for q in range(4):
        lanes = at(q)
        if q < 3:
            carry(q + 1)
        gain = gain_ref[:, lanes]
        for c in range(blocks):
            rows = pl.ds(c * SPAN, SPAN)
            g = yg_ref[rows, lanes].astype(F32) + ce[q % 2, rows, :] * g2_ref[rows, lanes].astype(F32)
            sq = g * g
            sq = sq[:, :128] + sq[:, 128:]
            sums[c] = sq if sums[c] is None else sums[c] + sq
            n_o[rows, q * CHUNK : (q + 1) * CHUNK] = (g * gain).astype(BF)


def near_gate_body(yg_ref, g2_ref, c_ref, e_ref, gain_ref, after_ref, n_o, ss_o, ce):
    sums = [None] * NB
    gated(yg_ref, g2_ref, c_ref, e_ref, gain_ref, spot()[0], NB, n_o, ce, sums)
    for c in range(NB):
        ss_o[pl.ds(c * SPAN, SPAN), :] = sums[c]


def far_gate_body(yg_ref, g2_ref, c_ref, e_ref, gain_ref, ss_ref, after_ref, n_o, inv_o, ce):
    sums = [ss_ref[pl.ds(c * SPAN, SPAN), :] for c in range(NB)]
    gated(yg_ref, g2_ref, c_ref, e_ref, gain_ref, 1 - spot()[0], NB, n_o, ce, sums)
    for c in range(NB):
        m = jnp.sum(sums[c], axis=1, keepdims=True) * (1.0 / INNER)
        inv_o[pl.ds(c * SPAN, SPAN), :] = jnp.broadcast_to(lax.rsqrt(m + 1e-05), (SPAN, 128))


def near_gate_call(yg, g2, cm, e, gain, after):
    return call(
        near_gate_body,
        "gate",
        (yg, g2, cm, e, gain, after),
        [((TOK, INNER // 2), BF), ((TOK, 128), F32)],
        spaces=[pltpu.VMEM] * 5 + [pl.ANY],
        scratch=[pltpu.VMEM((2, TOK, CHUNK), F32)],
        cost=(25 * 10**7, 4 << 20, 0),
    )


def far_gate_call(yg, g2, cm, e, gain, ss, after):
    return call(
        far_gate_body,
        "gate",
        (yg, g2, cm, e, gain, ss, after),
        [((TOK, INNER // 2), BF), ((TOK, 128), F32)],
        spaces=[pltpu.VMEM] * 6 + [pl.ANY],
        scratch=[pltpu.VMEM((2, TOK, CHUNK), F32)],
        cost=(25 * 10**7, 4 << 20, 0),
    )


def weight_block(w_ref, half, shift, k):
    lane = lax.rem(spot()[3] + shift, 4) * QOUT + k * CHUNK
    rows = pl.ds(pl.multiple_of(half * (INNER // 2), INNER // 2), INNER // 2)
    return w_ref[rows, pl.ds(pl.multiple_of(lane, CHUNK), CHUNK)]


def part_body(n_ref, w_ref, after_ref, p_o):
    core = spot()[0]
    for k in range(QOUT // CHUNK):
        p_o[:, k * CHUNK : (k + 1) * CHUNK] = dot(n_ref[...], weight_block(w_ref, core, 2, k))


def far_body(p_ref, n_ref, inv_ref, w_ref, r_o, l_o):
    core = spot()[0]
    for k in range(QOUT // CHUNK):
        y = p_ref[:, k * CHUNK : (k + 1) * CHUNK] + dot(n_ref[...], weight_block(w_ref, 1 - core, 2, k))
        o = (r_o, l_o)[k // 2]
        o[pl.ds((k % 2) * CHUNK, CHUNK), :] = jnp.transpose(y * inv_ref[:, 0:1]).astype(BF)


def proj_body(shift, first, count, near_ref, n_ref, inv_ref, w_ref, after_ref, o):
    core = spot()[0]
    for k in range(count):
        y = dot(near_ref[...], weight_block(w_ref, core, shift, first + k))
        y = y + dot(n_ref[...], weight_block(w_ref, 1 - core, shift, first + k))
        o[pl.ds(k * CHUNK, CHUNK), :] = jnp.transpose(y * inv_ref[:, 0:1]).astype(BF)


def part_call(near, w, after):
    return call(
        part_body,
        "part",
        (near, w, after),
        [((TOK, QOUT), F32)],
        spaces=[pltpu.VMEM] * 2 + [pl.ANY],
        cost=(TOK * INNER * QOUT, 5 << 20, 0),
    )[0]


def far_call(p, n, inv, w):
    return call(
        far_body,
        "far",
        (p, n, inv, w),
        [((QOUT // 2, TOK), BF)] * 2,
        cost=(TOK * INNER * QOUT, 5 << 20, 0),
    )


def proj_call(shift, side, near, n, inv, w, after):
    count = 2 if side < 2 else 4
    return call(
        functools.partial(proj_body, shift, 2 * side if side < 2 else 0, count),
        "proj",
        (near, n, inv, w, after),
        [((count * CHUNK, TOK), BF)],
        spaces=[pltpu.VMEM] * 4 + [pl.ANY],
        cost=(2 * TOK * INNER * count * CHUNK, 5 << 20, 0),
    )[0]


def relay_body(mine, a, o):
    o[...] = (mine[...].astype(F32) + a[...].astype(F32)).astype(BF)


def last_body(own, near_r, near_l, sum_r, sum_l, o_hbm, o, sem):
    copies = []
    for k in range(4):
        rows = pl.ds(k * CHUNK, CHUNK)
        side = pl.ds((k % 2) * CHUNK, CHUNK)
        near, total = ((near_r, sum_r), (near_l, sum_l))[k // 2]
        s = own[rows, :].astype(F32) + near[side, :].astype(F32) + total[side, :].astype(F32)
        o[rows, :] = s.astype(BF)
        copies.append(pltpu.make_async_copy(o.at[rows, :], o_hbm.at[rows, :], sem.at[k]))
        copies[k].start()
    for c in copies:
        c.wait()


def last_call(*args):
    return pl.pallas_call(
        last_body,
        in_specs=[pl.BlockSpec(memory_space=pltpu.VMEM)] * len(args),
        out_specs=pl.BlockSpec(memory_space=pltpu.HBM),
        out_shape=jax.ShapeDtypeStruct((QOUT, TOK), BF),
        scratch_shapes=[pltpu.VMEM((QOUT, TOK), BF), pltpu.SemaphoreType.DMA((4,))],
        compiler_params=pltpu.CompilerParams(vmem_limit_bytes=VMEM_LIMIT),
        name="last",
    )(*args)


def seq_perm(v, y, z, core):
    pairs = []
    for src in range(32):
        row = (src >> 3) ^ y
        column = (((src >> 1) & 3) + z) & 3
        pairs.append((src, row * 8 + column * 2 + ((src & 1) ^ core)))
    return lax.ppermute(v, "seq", pairs)


def head_perm(v, shift):
    return lax.ppermute(v, "head", [(s, (s + shift) % 4) for s in range(4)])


def on_device(x_in, bc_in, z_in, dt_raw, a_log, conv_x, conv_bc, d_skip, norm_gain, out_weight):
    bc = bc_in.reshape(TOK, 256)
    hbm = lambda v: pltpu.with_memory_space_constraint(v, pltpu.HBM)
    edge = call(
        edge_body,
        "edge",
        (hbm(x_in), hbm(bc)),
        [((8, INNER + 256), BF)],
        spaces=[pltpu.HBM] * 2,
        scratch=[pltpu.SemaphoreType.DMA((2,))],
    )[0]
    halo = lax.ppermute(edge, "seq", [(s, (s + 1) % 32) for s in range(32)])
    xc, pst, dec, x0, end, b, L, step, tw0, b0, tw, bts, dtab, xv = first_call(
        hbm(x_in), bc, conv_x, conv_bc, dt_raw, a_log.reshape(1, HEADS)
    )
    xc, b, ds, send, bt = second_call(halo, x0, b0, conv_x, conv_bc, tw0, end, dec, xc, b)
    recv = seq_perm(send, 0, 0, 1)
    xc, pst, dec, x0, late = rest_call(xv, conv_x, tw, bts, dtab, xc, pst, dec, x0, send)
    xc, ds, keep = third_call(halo, x0, bt, conv_x, tw0, end, late, dec, xc, ds)
    piece = jax.ShapeDtypeStruct((WROWS, CHUNK), BF)
    plain = jax.ShapeDtypeStruct((STATE, CHUNK), BF)
    box = pltpu.VMEM((4, WROWS, CHUNK), F32)
    splits = (3, 3, 2)
    q = small_call(pair_body, "pair", (keep, recv), [piece] * 4)
    cm, sc, m2, tl, te, td = table_call(L, step, d_skip.reshape(1, HEADS), halo, bc, conv_bc, b, q[0])
    known = (xc, cm, sc, z_in, m2, tl, te, td, dec, pst, ds)
    work = lambda k, after, before: mix_call(sum(splits[:k]), splits[k], known, after, before)
    mixed = work(0, q[0], ())
    rows = [q[0]] + [seq_perm(q[i], 0, i, 0) for i in (1, 2, 3)]
    total, pre, dpre = small_call(
        row_body,
        "row",
        rows,
        [piece, jax.ShapeDtypeStruct((4, STATE, CHUNK), F32), jax.ShapeDtypeStruct((4, 8, CHUNK), F32)],
        [box],
        (mixed[0],),
    )
    mixed = work(1, total, mixed)
    cols = [total] + [seq_perm(total, i, 0, 0) for i in (1, 2, 3)]
    e = small_call(plane_body, "plane", (*cols, pre, dpre), [plain] * 4, [box], (mixed[0],))
    mixed = work(2, e[0], mixed)
    back = [e[0]] + [seq_perm(e[i], 0, i, 0) for i in (1, 2, 3)]
    half = jax.ShapeDtypeStruct((4, STATE, CHUNK), BF)
    give, stay = small_call(
        spread_body, "spread", (*back, keep, recv), [half] * 2, [pltpu.VMEM((4, STATE, CHUNK), F32)], (mixed[0],)
    )
    take = seq_perm(give, 0, 0, 1)
    gain = norm_gain.reshape(1, INNER)
    near, ss = near_gate_call(*mixed, cm, stay, gain, give)
    p = part_call(near, out_weight, ss)
    other, inv = far_gate_call(*mixed, cm, take, gain, ss, p)
    far_r, far_l = far_call(p, other, inv, out_weight)
    from_left, from_right = head_perm(far_r, 1), head_perm(far_l, -1)
    proj = lambda shift, side, after: proj_call(shift, side, near, other, inv, out_weight, after)
    right_l = proj(1, 1, far_r)
    near_l = head_perm(right_l, 1)
    left_r = proj(3, 0, right_l)
    near_r = head_perm(left_r, -1)
    right_r = proj(1, 0, left_r)
    left_l = proj(3, 1, right_r)
    shape = ((QOUT // 2, TOK), BF)
    sum_r = head_perm(call(relay_body, "relay", (right_r, from_left), [shape])[0], 1)
    sum_l = head_perm(call(relay_body, "relay", (left_l, from_right), [shape])[0], -1)
    own = proj(0, 2, left_l)
    return last_call(own, near_r, near_l, sum_r, sum_l)


def solution(mesh):
    placed = (
        P("seq", "head"),
        P("seq", "head", None),
        P("seq", "head"),
        P("head", "seq"),
        P("head"),
        P(None, "head"),
        P(None, "head", None),
        P("head"),
        P("head"),
        P("head", None),
    )
    return jax.shard_map(
        on_device, mesh=mesh, in_specs=placed, out_specs=P("head", "seq"), check_vma=False
    )
```

```python
import functools

import jax
import jax.numpy as jnp
from jax import lax
from jax.experimental import pallas as pl
from jax.experimental.pallas import tpu as pltpu
from jax.sharding import PartitionSpec as P

SPAN = 128
HEADS = 32
HD = 64
STATE = 128
TOK = 512
NB = 4
INNER = 2048
CHUNK = 256
NCH = INNER // CHUNK
EARLY = 6
HPC = CHUNK // HD
DOUT = 4096
QOUT = 1024
WROWS = 144
LOG2E = 1.4426950408889634
BF = jnp.bfloat16
F32 = jnp.float32
VMEM_LIMIT = 10 << 20


def silu(u):
    half = 0.5 * u
    return half + half * jnp.tanh(half)


def dot(a, b):
    return jnp.dot(a, b, preferred_element_type=F32)


def iota(shape, axis):
    return lax.broadcasted_iota(jnp.int32, shape, axis)


def onehot(first_head, width, lanes, low=0, high=128):
    k = iota((128, width), 0)
    h = first_head + (iota((128, width), 1) // lanes)
    hit = ((k & 31) == h) & (k >= low) & (k < high)
    return jnp.where(hit, 1.0, 0.0).astype(BF)


def split2(v):
    hi = v.astype(BF).astype(F32)
    return hi, (v - hi).astype(BF).astype(F32)


def column(row, n):
    eye = iota((n, n), 0) == iota((n, n), 1)
    return jnp.sum(jnp.where(eye, jnp.broadcast_to(row, (n, n)), 0.0), axis=1, keepdims=True)


def call(body, name, args, outs, spaces=(), scratch=(), cost=(10**6, 1 << 20, 0), aliases=None, limit=VMEM_LIMIT):
    specs = [pl.BlockSpec(memory_space=spaces[k] if k < len(spaces) else pltpu.VMEM) for k in range(len(args))]
    return pl.pallas_call(
        body,
        in_specs=specs,
        out_specs=[pl.BlockSpec(memory_space=pltpu.VMEM)] * len(outs),
        out_shape=[jax.ShapeDtypeStruct(s, d) for s, d in outs],
        scratch_shapes=list(scratch),
        input_output_aliases=aliases or {},
        compiler_params=pltpu.CompilerParams(vmem_limit_bytes=limit),
        cost_estimate=pl.CostEstimate(flops=cost[0], bytes_accessed=cost[1], transcendentals=cost[2]),
        name=name,
    )(*args)


def conv(window, taps, rows):
    before = pltpu.roll(window, 1, 0)
    near = taps[3] * window + taps[2] * before
    far = taps[1] * window + taps[0] * before
    half = near[8:] + pltpu.roll(far, 2, 0)[8:]
    return half + half * jnp.tanh(half)


def taps_of(ref, lanes):
    return [0.5 * ref[k : k + 1, lanes] for k in range(4)]


def split3(v):
    hi = v.astype(BF).astype(F32)
    rest = v - hi
    mid = rest.astype(BF).astype(F32)
    return hi, mid, rest - mid


def spot():
    place = lax.axis_index("seq")
    return place & 1, (place >> 1) & 3, place >> 3, lax.axis_index("head")


def edge_body(x_ref, bc_ref, o, sem):
    a = pltpu.make_async_copy(x_ref.at[pl.ds(TOK - 8, 8), :], o.at[:, pl.ds(0, INNER)], sem.at[0])
    b = pltpu.make_async_copy(bc_ref.at[pl.ds(TOK - 8, 8), :], o.at[:, pl.ds(INNER, 256)], sem.at[1])
    a.start()
    b.start()
    a.wait()
    b.wait()


def halo_rows(h_ref, lanes):
    return jnp.where(lax.axis_index("seq") == 0, 0.0, h_ref[:, lanes].astype(F32))


def half_lanes(half, k, width=CHUNK):
    return pl.ds(pl.multiple_of(half * (INNER // 2) + k, 128), width)


def states(items, xv, cwx, tw, dtab, bts, wbuf, xw, xc_o, pst_o, end_o, dec_o, x0_o):
    nothing = jnp.zeros((8, 128), F32)
    count = len(items)
    head = lambda n: items[n][0] * (HEADS // 2) + items[n][1] * HPC
    spread = lambda n: dot(tw[...], onehot(head(n), CHUNK, HD, 0, 64))
    wbuf[0] = spread(0)
    for n in range(count + 1):
        if n < count:
            half, q = items[n]
            lanes = half_lanes(half, q * CHUNK)
            if n + 1 < count:
                wbuf[(n + 1) % 2] = spread(n + 1)
            dec_o[:, lanes] = dot(dtab[...], onehot(head(n), CHUNK, HD, 64, 128))
            x0_o[:, lanes] = xv[0:16, lanes]
        state = None
        for c in range(NB):
            if n < count:
                for r in (0, 64):
                    for l in (0, 128):
                        row = c * SPAN + r
                        part = half_lanes(half, q * CHUNK + l, 128)
                        if row == 0:
                            window = jnp.concatenate([nothing, xv[0:64, part].astype(F32)], axis=0)
                        else:
                            window = xv[pl.ds(row - 8, 72), part].astype(F32)
                        v = conv(window, taps_of(cwx, part), 64).astype(BF)
                        xc_o[pl.ds(row, 64), part] = v
                        w = wbuf[n % 2, pl.ds(row, 64), l : l + 128]
                        xw[n % 2, pl.ds(row, 64), l : l + 128] = (v.astype(F32) * w).astype(BF)
            if n > 0:
                before = half_lanes(items[n - 1][0], items[n - 1][1] * CHUNK)
                t = dot(bts[c], xw[(n - 1) % 2, pl.ds(c * SPAN, SPAN), :])
                state = t if c == 0 else dec_o[c : c + 1, before] * state + t
                if c < NB - 1:
                    pst_o[c, :, before] = state
                else:
                    end_o[n - 1] = state


def first_body(x_hbm, bv, cwx, cwb, dtv, alv,
               xc_o, pst_o, dec_o, x0_o, end_o, b_o, L_o, step_o, tw0_o, b0_o, tw, bts, dtab_o, xv,
               wbuf, xw, sem):
    core = spot()[0]
    order = [(1 - core, q) for q in range(4)] + [(core, q) for q in range(4)]
    copies = []
    for n, (half, q) in enumerate(order):
        lanes = half_lanes(half, q * CHUNK)
        copies.append(pltpu.make_async_copy(x_hbm.at[:, lanes], xv.at[:, lanes], sem.at[n]))
        copies[n].start()
    tri = jnp.where(iota((SPAN, SPAN), 0) <= iota((SPAN, SPAN), 1), 1.0, 0.0).astype(BF)
    v = dtv[...].astype(F32)
    t = jnp.exp(-jnp.abs(v))
    u = 1.0 + t
    d = u - 1.0
    flat = d == 0.0
    step = jnp.maximum(v, 0.0) + jnp.where(flat, t, jnp.log(u) * t / jnp.where(flat, 1.0, d))
    step_o[...] = step
    a = column(alv[...], HEADS)
    rate = jnp.concatenate(split3((-LOG2E * jnp.exp(a)) * step), axis=0).astype(BF)
    Ls, ends = [], []
    for c in range(NB):
        s = dot(rate[:, c * SPAN : (c + 1) * SPAN], tri)
        s = s[0:HEADS] + s[HEADS : 2 * HEADS] + s[2 * HEADS : 3 * HEADS]
        Ls.append(s)
        ends.append(jnp.broadcast_to(s[:, SPAN - 1 : SPAN], (HEADS, SPAN)))
    for c in copies[:EARLY]:
        c.wait()
    L = jnp.concatenate(Ls, axis=1)
    end = jnp.concatenate(ends, axis=1)
    L_o[...] = L
    w_hi, w_lo = split2(jnp.exp2(end - L) * step)
    d_hi, d_lo = split2(jnp.exp2(end))
    twt = jnp.transpose(jnp.concatenate([w_hi, w_lo, d_hi, d_lo], axis=0))
    tw[...] = twt.astype(BF)
    tw0_o[...] = twt[0:16].astype(BF)
    tw[pl.ds(0, 16), :] = jnp.zeros((16, 128), BF)
    rows = [twt[c * SPAN : c * SPAN + 1] for c in range(NB)]
    dtab = jnp.concatenate(rows + [jnp.zeros((12, SPAN), F32)], axis=0).astype(BF)
    dtab_o[...] = dtab
    b0_o[...] = bv[0:16, :STATE]
    btaps = [0.5 * cwb[k][:, :STATE] for k in range(4)]
    nothing = jnp.zeros((8, STATE), F32)
    for c in range(NB):
        if c == 0:
            window = jnp.concatenate([nothing, bv[0:SPAN, :STATE].astype(F32)], axis=0)
        else:
            window = bv[pl.ds(c * SPAN - 8, SPAN + 8), :STATE].astype(F32)
        v = conv(window, btaps, SPAN)
        b_o[pl.ds(c * SPAN, SPAN), :] = v.astype(BF)
        bts[c] = jnp.transpose(v).astype(BF)
    states(order[:EARLY], xv, cwx, tw, dtab_o, bts, wbuf, xw, xc_o, pst_o, end_o, dec_o, x0_o)
    for c in copies[EARLY:]:
        c.wait()


def rest_body(xv, cwx, tw, bts, dtab, xc_i, pst_i, dec_i, x0_i, after,
              xc_o, pst_o, dec_o, x0_o, end_o, wbuf, xw):
    core = spot()[0]
    items = [(core, q) for q in range(EARLY - 4, 4)]
    states(items, xv, cwx, tw, dtab, bts, wbuf, xw, xc_o, pst_o, end_o, dec_o, x0_o)


SHARED = [
    ((TOK, INNER), BF),
    ((NB - 1, STATE, INNER), F32),
    ((16, INNER), F32),
    ((16, INNER), BF),
]
ROOM = [
    pltpu.VMEM((2, TOK, CHUNK), F32),
    pltpu.VMEM((2, TOK, CHUNK), BF),
]


def first_call(x, bc, cwx, cwb, dt, al):
    return call(
        first_body,
        "first",
        (x, bc, cwx, cwb, dt, al),
        SHARED
        + [
            ((EARLY, STATE, CHUNK), F32),
            ((TOK, STATE), BF),
            ((HEADS, TOK), F32),
            ((HEADS, TOK), F32),
            ((16, 128), BF),
            ((16, STATE), BF),
            ((TOK, 128), BF),
            ((NB, STATE, SPAN), BF),
            ((16, 128), BF),
            ((TOK, INNER), BF),
        ],
        spaces=[pltpu.HBM],
        scratch=ROOM + [pltpu.SemaphoreType.DMA((NCH,))],
        cost=(10**5, 1 << 14, 0),
    )


def rest_call(x, cwx, tw, bts, dtab, xc, pst, dec, x0, after):
    return call(
        rest_body,
        "rest",
        (x, cwx, tw, bts, dtab, xc, pst, dec, x0, after),
        SHARED + [((NCH - EARLY, STATE, CHUNK), F32)],
        spaces=[pltpu.VMEM] * 9 + [pl.ANY],
        scratch=ROOM,
        aliases={5: 0, 6: 1, 7: 2, 8: 3},
        cost=(10**5, 1 << 14, 0),
    )


def wire_rows(decay):
    hi, lo = split2(decay)
    return jnp.concatenate([hi, lo, jnp.zeros((14, decay.shape[1]), F32)], axis=0)


def correct(half, bt, h_ref, x0_ref, cwx_ref, tw0_ref, ends, dec_ref, xc_o, ds_o, emit):
    for q in range(4):
        lanes = half_lanes(half, q * CHUNK)
        window = jnp.concatenate([halo_rows(h_ref, lanes), x0_ref[:, lanes].astype(F32)], axis=0)
        u = conv(window, taps_of(cwx_ref, lanes), 16).astype(BF)
        xc_o[0:16, lanes] = u
        w = dot(tw0_ref[...], onehot(half * (HEADS // 2) + q * HPC, CHUNK, HD, 0, 64))
        xw = jnp.concatenate([u.astype(F32) * w, jnp.zeros((SPAN - 16, CHUNK), F32)], axis=0).astype(BF)
        fix = dot(bt, xw)
        ds_o[:, lanes] = fix
        dec = dec_ref[0:8, lanes]
        after = dec[1:2] * dec[2:3] * dec[3:4]
        ref, n = ends[q]
        emit(q, ref[n] + after * fix, dec[0:1] * after)


def second_body(h_ref, x0_ref, b0_ref, cwx_ref, cwb_ref, tw0_ref, end_ref, dec_ref, xc_in, b_in,
                xc_o, b_o, ds_o, send_o, bt_o):
    v = jnp.concatenate([halo_rows(h_ref, pl.ds(INNER, STATE)), b0_ref[...].astype(F32)], axis=0)
    v = conv(v, [0.5 * cwb_ref[k][:, :STATE] for k in range(4)], 16)
    b_o[0:16, :] = v.astype(BF)
    bt = jnp.transpose(jnp.concatenate([v, jnp.zeros((SPAN - 16, STATE), F32)], axis=0)).astype(BF)
    bt_o[...] = bt

    def emit(q, state, decay):
        send_o[q, 0:STATE, :] = state.astype(BF)
        send_o[q, STATE:WROWS, :] = wire_rows(decay).astype(BF)

    correct(1 - spot()[0], bt, h_ref, x0_ref, cwx_ref, tw0_ref, [(end_ref, q) for q in range(4)], dec_ref, xc_o, ds_o, emit)


def third_body(h_ref, x0_ref, bt_ref, cwx_ref, tw0_ref, end_ref, late_ref, dec_ref, xc_in, ds_in, xc_o, ds_o, keep_o):
    def emit(q, state, decay):
        keep_o[q, 0:STATE, :] = state
        keep_o[q, STATE:WROWS, :] = jnp.concatenate([decay, jnp.zeros((15, CHUNK), F32)], axis=0)

    ends = [(end_ref, 4 + q) if 4 + q < EARLY else (late_ref, 4 + q - EARLY) for q in range(4)]
    correct(spot()[0], bt_ref[...], h_ref, x0_ref, cwx_ref, tw0_ref, ends, dec_ref, xc_o, ds_o, emit)


def second_call(halo, x0, b0, cwx, cwb, tw0, end, dec, xc, b):
    return call(
        second_body,
        "second",
        (halo, x0, b0, cwx, cwb, tw0, end, dec, xc, b),
        [
            ((TOK, INNER), BF),
            ((TOK, STATE), BF),
            ((STATE, INNER), F32),
            ((4, WROWS, CHUNK), BF),
            ((STATE, 128), BF),
        ],
        aliases={8: 0, 9: 1},
        cost=(10**5, 1 << 14, 0),
    )


def third_call(halo, x0, bt, cwx, tw0, end, late, dec, xc, ds):
    return call(
        third_body,
        "third",
        (halo, x0, bt, cwx, tw0, end, late, dec, xc, ds),
        [((TOK, INNER), BF), ((STATE, INNER), F32), ((4, WROWS, CHUNK), F32)],
        aliases={8: 0, 9: 1},
        cost=(10**5, 1 << 14, 0),
    )


def table_body(L_ref, step_ref, ds_ref, h_ref, bc_ref, cwb_ref, b_ref, after_ref,
               c_o, sc_o, m2_o, tl_o, te_o, td_o, buf):
    L = L_ref[...]
    M = jnp.log(step_ref[...]) * LOG2E - L
    for j in range(NCH):
        m2_o[j, 0:HPC, :] = M[j * HPC : (j + 1) * HPC, :]
    zero = jnp.zeros((HEADS, TOK), F32)
    tl_o[...] = jnp.transpose(jnp.concatenate([*split3(L), zero], axis=0)).astype(BF)
    parts, before = [], jnp.zeros((HEADS, SPAN), F32)
    for c in range(NB):
        s = L[:, c * SPAN : (c + 1) * SPAN]
        parts.append(before + s)
        before = before + jnp.broadcast_to(s[:, SPAN - 1 : SPAN], (HEADS, SPAN))
    e = [*split2(jnp.exp2(L)), *split2(jnp.exp2(jnp.concatenate(parts, axis=1)))]
    te_o[...] = jnp.transpose(jnp.concatenate(e, axis=0)).astype(BF)
    d = [jnp.broadcast_to(p, (HEADS, SPAN)) for p in split2(column(ds_ref[...], HEADS))]
    d = jnp.concatenate([*d, jnp.zeros((2 * HEADS, SPAN), F32)], axis=0)
    td_o[...] = jnp.transpose(d)[0:16].astype(BF)
    buf[pl.ds(0, 8), :] = halo_rows(h_ref, pl.ds(INNER + STATE, STATE))
    buf[pl.ds(8, TOK), :] = bc_ref[:, STATE:].astype(F32)
    taps = [0.5 * cwb_ref[k][:, STATE:] for k in range(4)]
    causal = iota((SPAN, SPAN), 0) >= iota((SPAN, SPAN), 1)
    for c in range(NB):
        rows = pl.ds(c * SPAN, SPAN)
        v = conv(buf[pl.ds(c * SPAN, SPAN + 8), :], taps, SPAN).astype(BF)
        c_o[rows, :] = v
        s = lax.dot_general(v, b_ref[rows, :], (((1,), (1,)), ((), ())), preferred_element_type=F32)
        sc_o[c] = jnp.where(causal, s, 0.0)


def table_call(L, step, ds, halo, bc, cwb, b, after):
    return call(
        table_body,
        "table",
        (L, step, ds, halo, bc, cwb, b, after),
        [
            ((TOK, STATE), BF),
            ((NB, SPAN, SPAN), F32),
            ((NCH, 8, TOK), F32),
            ((TOK, 128), BF),
            ((TOK, 128), BF),
            ((16, 128), BF),
        ],
        spaces=[pltpu.VMEM] * 7 + [pl.ANY],
        scratch=[pltpu.VMEM((TOK + 8, STATE), F32)],
        cost=(10**8, 2 << 20, 10**5),
    )


def decay_of(v):
    return v[STATE : STATE + 1] + v[STATE + 1 : STATE + 2]


def small_call(body, name, args, outs, scratch=(), after=()):
    n = len(args)
    m = len(after)

    def run(*refs):
        body(*refs[:n], *refs[n + m :])

    return call(
        run,
        name,
        (*args, *after),
        [(o.shape, o.dtype) for o in outs],
        spaces=[pltpu.VMEM] * n + [pl.ANY] * m,
        scratch=scratch,
    )


def pair_body(keep_ref, recv_ref, *outs):
    core, z = spot()[:2]
    for i in range(4):
        q = (z + i) & 3
        own = keep_ref[q]
        other = recv_ref[q].astype(F32)
        early = jnp.where(core == 0, own, other)
        late = jnp.where(core == 0, other, own)
        d_early, d_late = decay_of(early), decay_of(late)
        outs[i][0:STATE, :] = (d_late * early[0:STATE] + late[0:STATE]).astype(BF)
        outs[i][STATE:WROWS, :] = wire_rows(d_early * d_late).astype(BF)


def row_body(r0, r1, r2, r3, total_o, pre_o, dpre_o, box):
    z = spot()[1]
    for i, r in enumerate((r0, r1, r2, r3)):
        box[(z - i) & 3] = r[...].astype(F32)
    state = jnp.zeros((STATE, CHUNK), F32)
    decay = jnp.ones((1, CHUNK), F32)
    for k in range(4):
        pre_o[k] = state
        dpre_o[k] = jnp.broadcast_to(decay, (8, CHUNK))
        v = box[k]
        d = decay_of(v)
        state = d * state + v[0:STATE]
        decay = decay * d
    total_o[0:STATE, :] = state.astype(BF)
    total_o[STATE:WROWS, :] = wire_rows(decay).astype(BF)


def plane_body(r0, r1, r2, r3, pre_ref, dpre_ref, o0, o1, o2, o3, box):
    z, y = spot()[1:3]
    for i, r in enumerate((r0, r1, r2, r3)):
        box[y ^ i] = r[...].astype(F32)
    state = jnp.zeros((STATE, CHUNK), F32)
    for k in range(3):
        v = box[k]
        state = jnp.where(k < y, decay_of(v) * state + v[0:STATE], state)
    for i, o in enumerate((o0, o1, o2, o3)):
        q = (z + i) & 3
        d = dpre_ref[q]
        o[...] = (pre_ref[q] + d[0:1] * state).astype(BF)


def spread_body(r0, r1, r2, r3, keep_ref, recv_ref, send_o, stay_o, box):
    core, z = spot()[:2]
    for i, r in enumerate((r0, r1, r2, r3)):
        box[(z - i) & 3] = r[...].astype(F32)
    for q in range(4):
        early = jnp.where(core == 0, keep_ref[q], recv_ref[q].astype(F32))
        a = box[q]
        b = decay_of(early) * a + early[0:STATE]
        send_o[q] = jnp.where(core == 0, b, a).astype(BF)
        stay_o[q] = jnp.where(core == 0, a, b).astype(BF)


def mix_body(first_chunk, chunks, xc_ref, c_ref, sc_ref, z_ref, m2_ref, tl_ref, te_ref, td_ref, dec_ref, pst_ref,
             ds_ref, *rest):
    yg_o, g2_o, ex, ee = rest[-4:]
    left = iota((SPAN, SPAN), 1) < HD

    def expand(k):
        j = first_chunk + k
        ex[k % 2] = dot(tl_ref[...], onehot(j * HPC, HPC * SPAN, SPAN))
        ee[k % 2, :, 0:CHUNK] = dot(te_ref[...], onehot(j * HPC, CHUNK, HD, 0, 64))
        ee[k % 2, :, CHUNK:] = dot(te_ref[...], onehot(j * HPC, CHUNK, HD, 64, 128))

    expand(0)
    for k in range(chunks):
        j = first_chunk + k
        lanes = pl.ds(j * CHUNK, CHUNK)
        if k + 1 < chunks:
            expand(k + 1)
        skip = dot(td_ref[...], onehot(j * HPC, CHUNK, HD))[0:1]
        fix = ds_ref[:, lanes]
        for c in range(NB):
            rows = pl.ds(c * SPAN, SPAN)
            s = sc_ref[c]
            x = xc_ref[rows, lanes]
            parts = []
            for h in range(HPC):
                m2 = m2_ref[j, h : h + 1, c * SPAN : (c + 1) * SPAN]
                e = ex[k % 2, rows, h * SPAN : (h + 1) * SPAN] + m2
                parts.append((s * jnp.exp2(jnp.minimum(e, 8.0))).astype(BF))
            ys = []
            for p in range(HPC // 2):
                xp = x[:, p * SPAN : (p + 1) * SPAN].astype(F32)
                rhs = jnp.concatenate([jnp.where(left, xp, 0.0), jnp.where(left, 0.0, xp)], axis=0).astype(BF)
                ys.append(dot(jnp.concatenate([parts[2 * p], parts[2 * p + 1]], axis=1), rhs))
            y = jnp.concatenate(ys, axis=1) + skip * x.astype(F32)
            if c > 0:
                if c > 1:
                    fix = dec_ref[c - 1 : c, lanes] * fix
                ent = (pst_ref[c - 1, :, lanes] + fix).astype(BF)
                y = y + ee[k % 2, rows, 0:CHUNK] * dot(c_ref[rows, :], ent)
            gate = silu(z_ref[rows, lanes].astype(F32))
            yg_o[rows, lanes] = (y * gate).astype(BF)
            g2_o[rows, lanes] = (ee[k % 2, rows, CHUNK:] * gate).astype(BF)


def mix_call(first_chunk, chunks, args, after, before):
    n = len(args)
    return call(
        functools.partial(mix_body, first_chunk, chunks),
        "mix",
        (*args, after, *before),
        [((TOK, INNER), BF)] * 2,
        spaces=[pltpu.VMEM] * n + [pl.ANY],
        scratch=[pltpu.VMEM((2, TOK, HPC * SPAN), F32), pltpu.VMEM((2, TOK, 2 * CHUNK), F32)],
        aliases={n + 1: 0, n + 2: 1} if before else None,
        cost=(chunks * 25 * 10**7, chunks << 20, chunks * 6 * 10**5),
    )


def gated(yg_ref, g2_ref, c_ref, e_ref, gain_ref, half, blocks, n_o, ce, sums):
    at = lambda q: pl.ds(pl.multiple_of(half * (INNER // 2) + q * CHUNK, CHUNK), CHUNK)

    def carry(q):
        ce[q % 2] = dot(c_ref[...], e_ref[q])

    carry(0)
    for q in range(4):
        lanes = at(q)
        if q < 3:
            carry(q + 1)
        gain = gain_ref[:, lanes]
        for c in range(blocks):
            rows = pl.ds(c * SPAN, SPAN)
            g = yg_ref[rows, lanes].astype(F32) + ce[q % 2, rows, :] * g2_ref[rows, lanes].astype(F32)
            sq = g * g
            sq = sq[:, :128] + sq[:, 128:]
            sums[c] = sq if sums[c] is None else sums[c] + sq
            n_o[rows, q * CHUNK : (q + 1) * CHUNK] = (g * gain).astype(BF)


def near_gate_body(yg_ref, g2_ref, c_ref, e_ref, gain_ref, after_ref, n_o, ss_o, ce):
    sums = [None] * NB
    gated(yg_ref, g2_ref, c_ref, e_ref, gain_ref, spot()[0], NB, n_o, ce, sums)
    for c in range(NB):
        ss_o[pl.ds(c * SPAN, SPAN), :] = sums[c]


def far_gate_body(yg_ref, g2_ref, c_ref, e_ref, gain_ref, ss_ref, after_ref, n_o, inv_o, ce):
    sums = [ss_ref[pl.ds(c * SPAN, SPAN), :] for c in range(NB)]
    gated(yg_ref, g2_ref, c_ref, e_ref, gain_ref, 1 - spot()[0], NB, n_o, ce, sums)
    for c in range(NB):
        m = jnp.sum(sums[c], axis=1, keepdims=True) * (1.0 / INNER)
        inv_o[pl.ds(c * SPAN, SPAN), :] = jnp.broadcast_to(lax.rsqrt(m + 1e-05), (SPAN, 128))


def near_gate_call(yg, g2, cm, e, gain, after):
    return call(
        near_gate_body,
        "gate",
        (yg, g2, cm, e, gain, after),
        [((TOK, INNER // 2), BF), ((TOK, 128), F32)],
        spaces=[pltpu.VMEM] * 5 + [pl.ANY],
        scratch=[pltpu.VMEM((2, TOK, CHUNK), F32)],
        cost=(25 * 10**7, 4 << 20, 0),
    )


def far_gate_call(yg, g2, cm, e, gain, ss, after):
    return call(
        far_gate_body,
        "gate",
        (yg, g2, cm, e, gain, ss, after),
        [((TOK, INNER // 2), BF), ((TOK, 128), F32)],
        spaces=[pltpu.VMEM] * 6 + [pl.ANY],
        scratch=[pltpu.VMEM((2, TOK, CHUNK), F32)],
        cost=(25 * 10**7, 4 << 20, 0),
    )


def weight_block(w_ref, half, shift, k):
    lane = lax.rem(spot()[3] + shift, 4) * QOUT + k * CHUNK
    rows = pl.ds(pl.multiple_of(half * (INNER // 2), INNER // 2), INNER // 2)
    return w_ref[rows, pl.ds(pl.multiple_of(lane, CHUNK), CHUNK)]


def part_body(n_ref, w_ref, after_ref, p_o):
    core = spot()[0]
    for k in range(QOUT // CHUNK):
        p_o[:, k * CHUNK : (k + 1) * CHUNK] = dot(n_ref[...], weight_block(w_ref, core, 2, k))


def far_body(p_ref, n_ref, inv_ref, w_ref, r_o, l_o):
    core = spot()[0]
    for k in range(QOUT // CHUNK):
        y = p_ref[:, k * CHUNK : (k + 1) * CHUNK] + dot(n_ref[...], weight_block(w_ref, 1 - core, 2, k))
        o = (r_o, l_o)[k // 2]
        o[pl.ds((k % 2) * CHUNK, CHUNK), :] = jnp.transpose(y * inv_ref[:, 0:1]).astype(BF)


def proj_body(shift, first, count, near_ref, n_ref, inv_ref, w_ref, after_ref, o):
    core = spot()[0]
    for k in range(count):
        y = dot(near_ref[...], weight_block(w_ref, core, shift, first + k))
        y = y + dot(n_ref[...], weight_block(w_ref, 1 - core, shift, first + k))
        o[pl.ds(k * CHUNK, CHUNK), :] = jnp.transpose(y * inv_ref[:, 0:1]).astype(BF)


def part_call(near, w, after):
    return call(
        part_body,
        "part",
        (near, w, after),
        [((TOK, QOUT), F32)],
        spaces=[pltpu.VMEM] * 2 + [pl.ANY],
        cost=(TOK * INNER * QOUT, 5 << 20, 0),
    )[0]


def far_call(p, n, inv, w):
    return call(
        far_body,
        "far",
        (p, n, inv, w),
        [((QOUT // 2, TOK), BF)] * 2,
        cost=(TOK * INNER * QOUT, 5 << 20, 0),
    )


def proj_call(shift, side, near, n, inv, w, after):
    count = 2 if side < 2 else 4
    return call(
        functools.partial(proj_body, shift, 2 * side if side < 2 else 0, count),
        "proj",
        (near, n, inv, w, after),
        [((count * CHUNK, TOK), BF)],
        spaces=[pltpu.VMEM] * 4 + [pl.ANY],
        cost=(2 * TOK * INNER * count * CHUNK, 5 << 20, 0),
    )[0]


def relay_body(mine, a, o):
    o[...] = (mine[...].astype(F32) + a[...].astype(F32)).astype(BF)


def last_body(own, near_r, near_l, sum_r, sum_l, o_hbm, o, sem):
    copies = []
    for k in range(4):
        rows = pl.ds(k * CHUNK, CHUNK)
        side = pl.ds((k % 2) * CHUNK, CHUNK)
        near, total = ((near_r, sum_r), (near_l, sum_l))[k // 2]
        s = own[rows, :].astype(F32) + near[side, :].astype(F32) + total[side, :].astype(F32)
        o[rows, :] = s.astype(BF)
        copies.append(pltpu.make_async_copy(o.at[rows, :], o_hbm.at[rows, :], sem.at[k]))
        copies[k].start()
    for c in copies:
        c.wait()


def last_call(*args):
    return pl.pallas_call(
        last_body,
        in_specs=[pl.BlockSpec(memory_space=pltpu.VMEM)] * len(args),
        out_specs=pl.BlockSpec(memory_space=pltpu.HBM),
        out_shape=jax.ShapeDtypeStruct((QOUT, TOK), BF),
        scratch_shapes=[pltpu.VMEM((QOUT, TOK), BF), pltpu.SemaphoreType.DMA((4,))],
        compiler_params=pltpu.CompilerParams(vmem_limit_bytes=VMEM_LIMIT),
        name="last",
    )(*args)


def seq_perm(v, y, z, core):
    pairs = []
    for src in range(32):
        row = (src >> 3) ^ y
        column = (((src >> 1) & 3) + z) & 3
        pairs.append((src, row * 8 + column * 2 + ((src & 1) ^ core)))
    return lax.ppermute(v, "seq", pairs)


def head_perm(v, shift):
    return lax.ppermute(v, "head", [(s, (s + shift) % 4) for s in range(4)])


def on_device(x_in, bc_in, z_in, dt_raw, a_log, conv_x, conv_bc, d_skip, norm_gain, out_weight):
    bc = bc_in.reshape(TOK, 256)
    hbm = lambda v: pltpu.with_memory_space_constraint(v, pltpu.HBM)
    edge = call(
        edge_body,
        "edge",
        (hbm(x_in), hbm(bc)),
        [((8, INNER + 256), BF)],
        spaces=[pltpu.HBM] * 2,
        scratch=[pltpu.SemaphoreType.DMA((2,))],
    )[0]
    halo = lax.ppermute(edge, "seq", [(s, (s + 1) % 32) for s in range(32)])
    xc, pst, dec, x0, end, b, L, step, tw0, b0, tw, bts, dtab, xv = first_call(
        hbm(x_in), bc, conv_x, conv_bc, dt_raw, a_log.reshape(1, HEADS)
    )
    xc, b, ds, send, bt = second_call(halo, x0, b0, conv_x, conv_bc, tw0, end, dec, xc, b)
    recv = seq_perm(send, 0, 0, 1)
    xc, pst, dec, x0, late = rest_call(xv, conv_x, tw, bts, dtab, xc, pst, dec, x0, send)
    xc, ds, keep = third_call(halo, x0, bt, conv_x, tw0, end, late, dec, xc, ds)
    piece = jax.ShapeDtypeStruct((WROWS, CHUNK), BF)
    plain = jax.ShapeDtypeStruct((STATE, CHUNK), BF)
    box = pltpu.VMEM((4, WROWS, CHUNK), F32)
    splits = (3, 3, 2)
    q = small_call(pair_body, "pair", (keep, recv), [piece] * 4)
    cm, sc, m2, tl, te, td = table_call(L, step, d_skip.reshape(1, HEADS), halo, bc, conv_bc, b, q[0])
    known = (xc, cm, sc, z_in, m2, tl, te, td, dec, pst, ds)
    work = lambda k, after, before: mix_call(sum(splits[:k]), splits[k], known, after, before)
    mixed = work(0, q[0], ())
    rows = [q[0]] + [seq_perm(q[i], 0, i, 0) for i in (1, 2, 3)]
    total, pre, dpre = small_call(
        row_body,
        "row",
        rows,
        [piece, jax.ShapeDtypeStruct((4, STATE, CHUNK), F32), jax.ShapeDtypeStruct((4, 8, CHUNK), F32)],
        [box],
        (mixed[0],),
    )
    mixed = work(1, total, mixed)
    cols = [total] + [seq_perm(total, i, 0, 0) for i in (1, 2, 3)]
    e = small_call(plane_body, "plane", (*cols, pre, dpre), [plain] * 4, [box], (mixed[0],))
    mixed = work(2, e[0], mixed)
    back = [e[0]] + [seq_perm(e[i], 0, i, 0) for i in (1, 2, 3)]
    half = jax.ShapeDtypeStruct((4, STATE, CHUNK), BF)
    give, stay = small_call(
        spread_body, "spread", (*back, keep, recv), [half] * 2, [pltpu.VMEM((4, STATE, CHUNK), F32)], (mixed[0],)
    )
    take = seq_perm(give, 0, 0, 1)
    gain = norm_gain.reshape(1, INNER)
    near, ss = near_gate_call(*mixed, cm, stay, gain, give)
    p = part_call(near, out_weight, ss)
    other, inv = far_gate_call(*mixed, cm, take, gain, ss, p)
    far_r, far_l = far_call(p, other, inv, out_weight)
    from_left, from_right = head_perm(far_r, 1), head_perm(far_l, -1)
    proj = lambda shift, side, after: proj_call(shift, side, near, other, inv, out_weight, after)
    right_l = proj(1, 1, far_r)
    near_l = head_perm(right_l, 1)
    left_r = proj(3, 0, right_l)
    near_r = head_perm(left_r, -1)
    right_r = proj(1, 0, left_r)
    left_l = proj(3, 1, right_r)
    shape = ((QOUT // 2, TOK), BF)
    sum_r = head_perm(call(relay_body, "relay", (right_r, from_left), [shape])[0], 1)
    sum_l = head_perm(call(relay_body, "relay", (left_l, from_right), [shape])[0], -1)
    own = proj(0, 2, left_l)
    return last_call(own, near_r, near_l, sum_r, sum_l)


def solution(mesh):
    placed = (
        P("seq", "head"),
        P("seq", "head", None),
        P("seq", "head"),
        P("head", "seq"),
        P("head"),
        P(None, "head"),
        P(None, "head", None),
        P("head"),
        P("head"),
        P("head", None),
    )
    return jax.shard_map(
        on_device, mesh=mesh, in_specs=placed, out_specs=P("head", "seq"), check_vma=False
    )
```
